32 devices in a mesh: gx: 2 (over core), gy: 4 (over y, x), gz: 4 (over z).
Axes of the slice: x: 2, y: 2, z: 4, core: 2. Of those that a mesh axis runs over, the one named last changes fastest.
Arguments:
- heights: float32 [8192, 1024], P(('gy', 'gz'), 'gx'), may hold values from -6 to 6
- scene_ids: int32 [8192, 1024], P(('gy', 'gz'), 'gx'), may hold values from 0 to 15, as said below
- scene_offset: float32 [16], replicated, may hold values from -4 to 4
- scene_weight: float32 [16], replicated, may hold values from 0.2 to 5
- band_gain: float32 [6], replicated, may hold values from 0.3 to 1.5
Outputs:
- blended: float32 [8192, 1024], P(('gy', 'gz'), 'gx')
The draws below stay inside these ranges and needn't reach their ends.
Inputs may be any that keep to these rules, and one draw needn't show every extreme that they name: `scene_ids`: scene index of each cell.
All inputs are finite; a program needn't handle non-finite values.
Results may differ from the reference program's by a relative error of at most 0.00002.
Values sent between devices are 32-bit elements; how exact they have to be, the bound alone decides.
A program may use at most 128 MiB of HBM per device.

```python
import math
import jax
import jax.numpy as jnp

SCENES = 16
LEVELS = 6
NR = 8192
NC = 1024


def draw_scene_ids(key, part):
    key_grid = jax.random.fold_in(key, 11)
    key_jitter = jax.random.fold_in(key, 23)
    grid = jax.random.randint(key_grid, (NR // 48 + 2, NC // 48 + 2), 0, SCENES).astype(jnp.int32)
    grid = grid.at[0, 0].set(SCENES - 1).at[0, 1].set(0)
    jitter = jax.random.randint(key_jitter, (NR,), 0, 16).astype(jnp.int32)
    row_cell = (jnp.arange(NR, dtype=jnp.int32) // 48)[:, None]
    col_cell = (jnp.arange(NC, dtype=jnp.int32)[None, :] + jitter[:, None]) // 48
    return grid[row_cell, col_cell].astype(jnp.int32)


def shard_levels(stream_key, extent, split, least, top_value):
    def one(dim, shards_of):
        steps = jax.random.uniform(jax.random.fold_in(jax.random.fold_in(stream_key, 6), dim), (shards_of,), jnp.float32, least / len(split), top_value / len(split))
        return jnp.repeat(jnp.exp(steps), extent[dim] // shards_of).reshape((-1,) + (1,) * (len(extent) - dim - 1))

    factor_of = one(*split[0])
    for cut in split[1:]:
        factor_of = factor_of * one(*cut)
    return factor_of


def gaussian(stream_key, dims, scale, bound, cuts=(), kind=jnp.bfloat16):
    values = scale * jax.random.normal(stream_key, dims, jnp.float32)
    if cuts:
        values = values * shard_levels(stream_key, dims, cuts, -0.22, 0.18)
    return jnp.clip(values, -bound, bound).astype(kind)


def setup_inputs(seed: int = 0) -> dict:
    key_of = jax.random.split(jax.random.key(seed), 6)
    return {
        "heights": gaussian(key_of[0], (NR, NC), 1.0, 6.0, ((0, 16), (1, 2)), jnp.float32),
        "scene_ids": draw_scene_ids(jax.random.fold_in(key_of[5], 71), 0),
        "scene_offset": jnp.clip(jax.random.uniform(key_of[2], (SCENES,), jnp.float32, -4.0, 4.0), -4.0, 4.0),
        "scene_weight": jnp.clip(jnp.exp(jax.random.uniform(key_of[3], (SCENES,), jnp.float32, math.log(0.2), math.log(5.0))), 0.2, 5.0),
        "band_gain": jnp.clip(jnp.exp(jax.random.uniform(key_of[4], (LEVELS,), jnp.float32, math.log(0.3), math.log(1.5))), 0.3, 1.5),
    }


KERN = (0.0625, 0.25, 0.375, 0.25, 0.0625)


def lookup(scene_ids, table):
    acc = jnp.zeros(scene_ids.shape, jnp.float32)
    for scene in range(SCENES):
        acc = acc + jnp.where(scene_ids == scene, table[scene], jnp.float32(0.0))
    return acc


def reduce_padded(padded):
    rows_out = padded.shape[-2] - 4
    cols_out = padded.shape[-1] - 4
    rows = KERN[0] * padded[..., 0:rows_out:2, :]
    for tap in range(1, 5):
        rows = rows + KERN[tap] * padded[..., tap:tap + rows_out:2, :]
    result = KERN[0] * rows[..., 0:cols_out:2]
    for tap in range(1, 5):
        result = result + KERN[tap] * rows[..., tap:tap + cols_out:2]
    return result


def expand_padded(padded):
    count = padded.shape[-2] - 2
    even = (padded[..., 0:count, :] + 6.0 * padded[..., 1:count + 1, :] + padded[..., 2:count + 2, :]) * 0.125
    odd = (padded[..., 1:count + 1, :] + padded[..., 2:count + 2, :]) * 0.5
    rows = jnp.stack([even, odd], axis=-2)
    rows = rows.reshape(rows.shape[:-3] + (2 * count, rows.shape[-1]))
    width = rows.shape[-1] - 2
    even = (rows[..., 0:width] + 6.0 * rows[..., 1:width + 1] + rows[..., 2:width + 2]) * 0.125
    odd = (rows[..., 1:width + 1] + rows[..., 2:width + 2]) * 0.5
    result = jnp.stack([even, odd], axis=-1)
    return result.reshape(result.shape[:-2] + (2 * width,))


def reference(heights, scene_ids, scene_offset, scene_weight, band_gain):
    weight = lookup(scene_ids, scene_weight)
    offset = lookup(scene_ids, scene_offset)
    numer = weight * (heights + offset)
    denom = weight
    ratios = [numer / denom]
    for level in range(LEVELS):
        numer = reduce_padded(jnp.pad(numer, 2))
        denom = reduce_padded(jnp.pad(denom, 2))
        ratios.append(numer / denom)
    top_mean = jnp.sum(numer) / jnp.sum(denom)
    collapsed = jnp.zeros_like(ratios[LEVELS]) + top_mean
    for level in range(LEVELS - 1, -1, -1):
        band = ratios[level] - expand_padded(jnp.pad(ratios[level + 1], 1))
        collapsed = band_gain[level] * band + expand_padded(jnp.pad(collapsed, 1))
    return collapsed
```

```python
import functools

import jax
import jax.numpy as jnp
import numpy as np
from jax import lax
from jax.experimental import pallas as pl
from jax.experimental.pallas import tpu as pltpu
from jax.sharding import PartitionSpec as P

F32, BF16 = jnp.float32, jnp.bfloat16
FAR = 1 << 20
HALO = 16
SIDE = 128
EDGE3 = 24
TAPS = (0.375, 0.25, 0.0625)
LEVELS = 6


def reach(count):
    weights = np.ones(count >> LEVELS, np.float64)
    for _ in range(LEVELS):
        fine = np.zeros(2 * weights.size + 4, np.float64)
        for tap, value in zip(range(-2, 3), (0.0625, 0.25, 0.375, 0.25, 0.0625)):
            fine[2 + tap : 2 + tap + 2 * weights.size : 2] += value * weights
        weights = fine[2:-2]
    return weights.astype(np.float32)


def split(x):
    high = x.astype(BF16)
    return high, (x - high.astype(F32)).astype(BF16)


def right(x, c):
    high, low = split(x)
    return jnp.dot(high, c, preferred_element_type=F32) + jnp.dot(
        low, c, preferred_element_type=F32
    )


def left(r, x):
    high, low = split(x)
    return jnp.dot(r, high, preferred_element_type=F32) + jnp.dot(
        r, low, preferred_element_type=F32
    )


def band(distance, scale):
    far = jnp.abs(distance)
    value = jnp.where(far == 2, TAPS[2] * scale, 0.0)
    value = jnp.where(far == 1, TAPS[1] * scale, value)
    value = jnp.where(far == 0, TAPS[0] * scale, value)
    return value.astype(F32).astype(BF16)


def kernel(
    sizes, off_hbm, wgt_hbm, gain_hbm, h_ref, s_ref, u_ref, v_ref, out_ref,
    off_ref, wgt_ref, gain_ref, wide, q0, h_buf, s_buf, u_buf, v_buf, nh, nl, dh, dl, b3, part, slots,
    own_sem, send0, recv0, send3, recv3, psend, precv,
):
    nr, nc, nx, ny, nz, rows_total, cols_total = sizes
    cx, cy, cz = lax.axis_index("gx"), lax.axis_index("gy"), lax.axis_index("gz")
    row = cy * nz + cz
    blocks = ny * nz
    w3 = nc // 8
    t3 = nr // 8

    def device(drow, dcol):
        target = row + drow
        return {"gx": cx + dcol, "gy": target // nz, "gz": target % nz}

    has = {-1: (row > 0, cx > 0), 0: None, 1: (row < blocks - 1, cx < nx - 1)}

    def there(drow, dcol):
        ok = None
        if drow:
            ok = has[drow][0]
        if dcol:
            ok = has[dcol][1] if ok is None else jnp.logical_and(ok, has[dcol][1])
        return ok

    dirs = [(a, b) for a in (-1, 0, 1) for b in (-1, 0, 1) if a or b]
    axes = (("gx", nx, cx), ("gz", nz, cz), ("gy", ny, cy))

    own = []
    for i, (src, dst) in enumerate(
        (
            (h_ref, h_buf.at[pl.ds(0, nr), pl.ds(0, nc)]),
            (s_ref, s_buf.at[pl.ds(0, nr), pl.ds(0, nc)]),
            (u_ref.at[row], u_buf),
            (v_ref.at[cx], v_buf),
            (off_hbm, off_ref),
            (wgt_hbm, wgt_ref),
            (gain_hbm, gain_ref),
        )
    ):
        copy = pltpu.make_async_copy(src, dst, own_sem.at[i])
        copy.start()
        own.append(copy)

    barrier = pltpu.get_barrier_semaphore()
    for d in dirs:
        @pl.when(there(*d))
        def _():
            pl.semaphore_signal(barrier, inc=1, device_id=device(*d))
    for name, count, me in axes:
        for step in range(1, count):
            pl.semaphore_signal(barrier, inc=1, device_id={name: (me + step) % count})

    def iota(n, dim):
        return lax.broadcasted_iota(jnp.int32, (n, 1) if dim == 0 else (1, n), dim)

    def fold(index, first, total, level):
        base = first >> level
        ok = jnp.logical_and(index + base >= 0, index + base < (total >> level))
        return jnp.where(ok, index, FAR)

    row0, col0 = row * nr, cx * nc
    r1, r2 = nr // 2 + 16, nr // 4 + 16
    c1, c2 = nc // 2 + 128, nc // 4 + 128
    r3, r4, r5, r6 = t3 + 2 * EDGE3, nr // 16 + 32, nr // 32 + 16, nr // 64 + 8

    def rows_at(level, dim):
        if level == 0:
            p = iota(nr + 2 * HALO, dim)
            return jnp.where(p < nr, p, jnp.where(p < nr + HALO, p - nr - HALO, p - HALO))
        count, shift = ((r1, 8), (r2, 8), (r3, EDGE3), (r4, 16), (r5, 8), (r6, 4))[level - 1]
        return iota(count, dim) - shift

    def cols_at(level, dim):
        if level == 0:
            p = iota(nc + 2 * SIDE, dim)
            return jnp.where(p < nc, p, jnp.where(p < nc + SIDE, p - nc - SIDE, p - SIDE))
        if level < 3:
            return iota((c1, c2)[level - 1], dim) - 8
        if level == 3:
            p = iota(6 * w3, dim)
            return (p // (2 * w3) - 1) * w3 + p % w3
        return iota(2 * w3, dim) % w3 - (16, 8, 4)[level - 4]

    def kind(count, dim):
        return (iota(count, dim) // w3) % 2

    def reduce_rows(level):
        out = fold(rows_at(level + 1, 0), row0, rows_total, level + 1)
        return band(rows_at(level, 1) - 2 * out, 1.0)

    def reduce_cols(level):
        out = fold(cols_at(level + 1, 1), col0, cols_total, level + 1)
        distance = cols_at(level, 0) - 2 * out
        if level >= 3:
            same = kind(distance.shape[0], 0) == kind(distance.shape[1], 1)
            distance = jnp.where(same, distance, FAR)
        return band(distance, 1.0)

    def expand_rows(level):
        out = iota(nr, 0) if level == 0 else rows_at(level, 0)
        return band(2 * rows_at(level + 1, 1) - out, 2.0)

    def expand_cols(level):
        out = iota(nc, 1) if level == 0 else cols_at(level, 1)
        return band(2 * cols_at(level + 1, 0) - out, 2.0)

    lane128 = lax.broadcasted_iota(jnp.int32, (8, 128), 1)

    def spread(table):
        row = jnp.zeros((8, 128), F32)
        for i in range(table.shape[0]):
            row = jnp.where(lane128 == i, table[i], row)
        return row

    def lookup(ids, table):
        n, m = ids.shape
        return jnp.concatenate(
            [
                jnp.concatenate(
                    [
                        jnp.take_along_axis(table, ids[r : r + 8, c : c + 128], axis=1)
                        for c in range(0, m, 128)
                    ],
                    axis=1,
                )
                for r in range(0, n, 8)
            ],
            axis=0,
        )

    def level0(rows, cols, valid):
        ids = s_buf[rows, cols]
        weight = lookup(ids, wgt_row)
        moved = h_buf[rows, cols] + lookup(ids, off_row)
        numer = weight * moved
        if valid is not None:
            weight = jnp.where(valid, weight, 0.0)
            numer = jnp.where(valid, numer, 0.0)
        nh[rows, cols], nl[rows, cols] = split(numer)
        dh[rows, cols], dl[rows, cols] = split(weight)
        return moved

    for copy in own:
        copy.wait()
    wgt_row, off_row = spread(wgt_ref), spread(off_ref)

    step = 32

    def own_rows(i, carry):
        rows = pl.ds(pl.multiple_of(i * step, step), step)
        moved = level0(rows, pl.ds(0, nc), None)
        for c in range(nc // 128):
            q0[c, rows, :] = moved[:, c * 128 : (c + 1) * 128]
        return carry

    lax.fori_loop(0, nr // step, own_rows, 0)

    near = sum(there(*d).astype(jnp.int32) for d in dirs)
    pl.semaphore_wait(barrier, near + (nx + ny + nz - 3))

    def rim(i, a, d):
        drow, dcol = d
        src, dst = ((h_ref, h_buf), (s_ref, s_buf))[a]
        rs = {-1: (0, nr + HALO, HALO), 0: (0, 0, nr), 1: (nr - HALO, nr, HALO)}[drow]
        cs = {-1: (0, nc + SIDE, SIDE), 0: (0, 0, nc), 1: (nc - SIDE, nc, SIDE)}[dcol]
        return pltpu.make_async_remote_copy(
            src_ref=src.at[pl.ds(rs[0], rs[2]), pl.ds(cs[0], cs[2])],
            dst_ref=dst.at[pl.ds(rs[1], rs[2]), pl.ds(cs[1], cs[2])],
            send_sem=send0.at[2 * i + a],
            recv_sem=recv0.at[2 * i + a],
            device_id=device(*d),
        )

    for i, d in enumerate(dirs):
        @pl.when(there(*d))
        def _():
            for a in range(2):
                rim(i, a, d).start()

    def dot(a, b):
        return jnp.dot(a, b, preferred_element_type=F32)

    own_out = iota(2 * w3, 1)
    in2 = cols_at(2, 0)
    pick_n = band(jnp.where(own_out < w3, in2 - 2 * own_out, FAR), 1.0)
    pick_d = band(jnp.where(own_out < w3, FAR, in2 - 2 * (own_out - w3)), 1.0)
    own_rows3 = band(rows_at(2, 1) - 2 * iota(t3, 0), 1.0)
    reduce0, rows1 = reduce_rows(0), reduce_rows(1)
    rows03 = dot(dot(own_rows3, rows1).astype(BF16), reduce0)
    rows03 = jnp.concatenate(split(rows03), axis=0)
    u_high, u_low = split(u_buf[...])
    pick = iota(16, 0)
    u_rows = jnp.where(
        pick == 0, u_high.astype(F32), jnp.where(pick == 1, u_low.astype(F32), 0.0)
    ).astype(BF16)
    top = jnp.concatenate([rows03[:, :nr], u_rows], axis=0)

    def own_part(high, low):
        rows, cols = pl.ds(0, nr), pl.ds(0, nc)
        return dot(top, high[rows, cols]) + dot(top, low[rows, cols])

    tn, td = own_part(nh, nl), own_part(dh, dl)
    v_row = v_buf[...]
    sum_n = jnp.sum(tn[2 * t3 :, :] * v_row)
    sum_d = jnp.sum(td[2 * t3 :, :] * v_row)

    tile_row = lax.broadcasted_iota(jnp.int32, (8, 128), 0)
    part[0] = jnp.where(tile_row == 0, sum_n, jnp.where(tile_row == 1, sum_d, 0.0))

    starts = (0, nx - 1, nx + nz - 2)

    def phase(k):
        name, count, me = axes[k]
        return [
            pltpu.make_async_remote_copy(
                src_ref=part.at[k],
                dst_ref=slots.at[starts[k] + s - 1],
                send_sem=psend.at[starts[k] + s - 1],
                recv_sem=precv.at[starts[k] + s - 1],
                device_id={name: (me + s) % count},
            )
            for s in range(1, count)
        ]

    def finish(k):
        total = part[k]
        for s, copy in enumerate(phase(k)):
            copy.wait()
            total = total + slots[starts[k] + s]
        return total

    for copy in phase(0):
        copy.start()


    def take(ds):
        for i, d in enumerate(dirs):
            if d in ds:
                @pl.when(there(*d))
                def _():
                    for a in range(2):
                        rim(i, a, d).wait_send()

                @pl.when(there(-d[0], -d[1]))
                def _():
                    for a in range(2):
                        rim(i, a, d).wait_recv()

    def yes(flag):
        return flag.astype(jnp.int32)

    up, down = yes(row > 0), yes(row < blocks - 1)
    west, east = yes(cx > 0), yes(cx < nx - 1)
    side_ok = jnp.where(iota(2 * SIDE, 1) < SIDE, west, east)
    rim_ok = jnp.where(iota(2 * HALO, 0) < HALO, up, down)
    body, rim_r = pl.ds(0, nr), pl.ds(nr, 2 * HALO)
    middle, side_c = pl.ds(0, nc), pl.ds(nc, 2 * SIDE)

    take([d for d in dirs if d[0] == 0])

    def side_rows(i, carry):
        rows = pl.ds(pl.multiple_of(i * step, step), step)
        level0(rows, side_c, jnp.broadcast_to(side_ok, (step, 2 * SIDE)) > 0)
        return carry

    lax.fori_loop(0, nr // step, side_rows, 0)

    cols0, cols1 = reduce_cols(0), reduce_cols(1)
    cols02 = dot(cols0, cols1).astype(BF16)
    cols03 = [split(dot(cols02, pick)) for pick in (pick_n, pick_d)]

    def side_part(t, high, low):
        t_side = dot(rows03[:, :nr], high[body, side_c]) + dot(rows03[:, :nr], low[body, side_c])
        t = jnp.concatenate([t[: 2 * t3], t_side], axis=1)
        return t[:t3] + t[t3:]

    tn, td = side_part(tn, nh, nl), side_part(td, dh, dl)

    part[1] = finish(0)
    for copy in phase(1):
        copy.start()

    half, start = nr // 4, nr // 2 - 32
    reduce0_b = band(
        start + iota(nr - start, 1) - 2 * fold(iota(r1 - half, 0) + (half - 8), row0, rows_total, 1), 1.0
    )

    def level1(x):
        t = [dot(reduce0[:half, : nr // 2], part_[pl.ds(0, nr // 2), :]) for part_ in x]
        b = [dot(reduce0_b, part_[pl.ds(start, nr - start), :]) for part_ in x]
        t = jnp.concatenate([t[0] + t[1], b[0] + b[1]], axis=0)
        low, high = split(t)

        def wide(k0, k1, n0, n1):
            return dot(low[:, k0:k1], cols0[k0:k1, n0:n1]) + dot(high[:, k0:k1], cols0[k0:k1, n0:n1])

        edge = nc // 2
        return jnp.concatenate(
            [
                wide(0, nc + SIDE, 0, edge),
                wide(nc - SIDE, nc, edge, c1) + wide(nc + SIDE, nc + 2 * SIDE, edge, c1),
            ],
            axis=1,
        )

    n1, d1 = level1((nh, nl)), level1((dh, dl))

    take([d for d in dirs if d[0] != 0])
    level0(rim_r, middle, jnp.broadcast_to(rim_ok, (2 * HALO, nc)) > 0)
    level0(rim_r, side_c, jnp.broadcast_to(rim_ok * side_ok, (2 * HALO, 2 * SIDE)) > 0)

    def rim_part(t, high, low, cols):
        e = dot(rows03[:, nr:], high[rim_r, :]) + dot(rows03[:, nr:], low[rim_r, :])
        t = t + e[:t3] + e[t3:]
        t_high, t_low = split(t)
        return dot(t_high, cols[0]) + dot(t_low, cols[0]) + dot(t_high, cols[1])

    b3[1, pl.ds(EDGE3, t3), :] = rim_part(tn, nh, nl, cols03[0]) + rim_part(td, dh, dl, cols03[1])

    def rim3(i, d):
        drow, dcol = d
        rs = {
            -1: (EDGE3, EDGE3 + t3, EDGE3),
            0: (EDGE3, EDGE3, t3),
            1: (t3, 0, EDGE3),
        }[drow]
        return pltpu.make_async_remote_copy(
            src_ref=b3.at[1, pl.ds(rs[0], rs[2]), :],
            dst_ref=b3.at[1 - dcol, pl.ds(rs[1], rs[2]), :],
            send_sem=send3.at[i],
            recv_sem=recv3.at[i],
            device_id=device(*d),
        )

    for i, d in enumerate(dirs):
        @pl.when(there(*d))
        def _():
            rim3(i, d).start()

    def ends(count):
        p = iota(32, 0)
        return jnp.where(p < 16, p, count - 32 + p)

    rim_in = iota(2 * HALO, 1)
    rim_in = rim_in + jnp.where(rim_in < HALO, -HALO, nr - HALO)
    ends0 = band(rim_in - 2 * fold(ends(r1) - 8, row0, rows_total, 1), 1.0)

    def patch(x, high, low):
        e = left(ends0, dot(high[rim_r, :], cols0) + dot(low[rim_r, :], cols0))
        n = x.shape[0]
        return jnp.concatenate([x[:16] + e[:16], x[16 : n - 16], x[n - 16 :] + e[16:]], axis=0)

    n1, d1 = patch(n1, nh, nl), patch(d1, dh, dl)
    part[2] = finish(1)
    for copy in phase(2):
        copy.start()
    q1 = jnp.where(d1 > 0, n1 / d1, 0.0)
    n2, d2 = left(rows1, right(n1, cols1)), left(rows1, right(d1, cols1))
    q2 = jnp.where(d2 > 0, n2 / d2, 0.0)

    rows_ = [None, None, None] + [reduce_rows(level) for level in (3, 4, 5)]
    cols_ = [None, None, None] + [reduce_cols(level) for level in (3, 4, 5)]
    up_rows = [None] + [expand_rows(level) for level in range(1, 6)]
    up_cols = [None] + [expand_cols(level) for level in range(1, 6)]

    for i, d in enumerate(dirs):
        @pl.when(there(*d))
        def _():
            rim3(i, d).wait_send()

        @pl.when(there(-d[0], -d[1]))
        def _():
            rim3(i, d).wait_recv()

    p3 = iota(r3, 0)
    ok3 = jnp.where(p3 < EDGE3, up, jnp.where(p3 < EDGE3 + t3, 1, down))
    lane = iota(2 * w3, 1)

    def ratio(packed):
        weights = pltpu.roll(packed, w3, axis=1)
        ok = jnp.logical_and(weights > 0, jnp.broadcast_to(lane, packed.shape) < w3)
        return jnp.where(ok, packed / weights, 0.0), ok

    pieces = []
    for block, flag in ((0, west), (1, None), (2, east)):
        ok = ok3 if flag is None else ok3 * flag
        piece = b3[block]
        pieces.append(jnp.where(jnp.broadcast_to(ok, piece.shape) > 0, piece, 0.0))
    packed = jnp.concatenate(pieces, axis=1)
    q3 = [ratio(piece) for piece in pieces]
    q3, ok_3 = [q for q, _ in q3], [jnp.where(ok, 1.0, 0.0) for _, ok in q3]
    q3, ok_3 = jnp.concatenate(q3, axis=1), jnp.concatenate(ok_3, axis=1) > 0

    v4 = left(rows_[3], right(packed, cols_[3]))
    v5 = left(rows_[4], right(v4, cols_[4]))
    v6 = left(rows_[5], right(v5, cols_[5]))
    q4, ok_4 = ratio(v4)
    q5, ok_5 = ratio(v5)
    q6, ok_6 = ratio(v6)

    total = finish(2)
    top_sum = jnp.sum(jnp.where(tile_row == 0, total, 0.0), axis=0, keepdims=True)
    top_weight = jnp.sum(jnp.where(tile_row == 1, total, 0.0), axis=0, keepdims=True)
    top_mean = (top_sum / top_weight)[:, :1]

    z = jnp.where(ok_6, top_mean - gain_ref[5] * q6, 0.0)
    levels = ((5, q5, ok_5), (4, q4, ok_4), (3, q3, ok_3), (2, q2, d2 > 0), (1, q1, d1 > 0))
    for level, q, ok in levels:
        grown = left(up_rows[level], right(z, up_cols[level]))
        z = jnp.where(ok, grown + (gain_ref[level] - gain_ref[level - 1]) * q, 0.0)
    full = right(z, expand_cols(0))
    tiles = nc // 128
    for c in range(tiles):
        wide[c] = full[:, c * 128 : (c + 1) * 128]
    gain = gain_ref[0]
    chunk = 32
    for c in range(tiles):
        for m in range(0, nr // 2, chunk):
            x, y, w = (wide[c, pl.ds(m + k, chunk), :] for k in (7, 8, 9))
            even, odd = pl.ds(2 * m, chunk, stride=2), pl.ds(2 * m + 1, chunk, stride=2)
            q0[c, even, :] = gain * q0[c, even, :] + (0.125 * (x + w) + 0.75 * y)
            q0[c, odd, :] = gain * q0[c, odd, :] + 0.5 * (y + w)
            out_ref[pl.ds(2 * m, 2 * chunk), c * 128 : (c + 1) * 128] = q0[c, pl.ds(2 * m, 2 * chunk), :]


def local(mesh_shape, heights, scene_ids, scene_offset, scene_weight, band_gain):
    nx, ny, nz = mesh_shape
    nr, nc = heights.shape
    rows_total, cols_total = nr * ny * nz, nc * nx
    u = jnp.asarray(reach(rows_total).reshape(ny * nz, 1, nr))
    v = jnp.asarray(reach(cols_total).reshape(nx, 1, nc))
    sizes = (nr, nc, nx, ny, nz, rows_total, cols_total)
    ext = (nr + 2 * HALO, nc + 2 * SIDE)
    peers = nx + ny + nz - 3
    hbm = pl.BlockSpec(memory_space=pltpu.HBM)
    return pl.pallas_call(
        functools.partial(kernel, sizes),
        out_shape=pltpu.VMEM((nr, nc), F32),
        in_specs=[hbm] * 7,
        out_specs=pl.BlockSpec(memory_space=pltpu.VMEM),
        scratch_shapes=[
            pltpu.SMEM(scene_offset.shape, F32),
            pltpu.SMEM(scene_weight.shape, F32),
            pltpu.SMEM(band_gain.shape, F32),
            pltpu.VMEM((nc // 128, nr // 2 + 16, 128), F32),
            pltpu.VMEM((nc // 128, nr, 128), F32),
            pltpu.VMEM(ext, F32),
            pltpu.VMEM(ext, jnp.int32),
            pltpu.VMEM((1, nr), F32),
            pltpu.VMEM((1, nc), F32),
            pltpu.VMEM(ext, BF16),
            pltpu.VMEM(ext, BF16),
            pltpu.VMEM(ext, BF16),
            pltpu.VMEM(ext, BF16),
            pltpu.VMEM((3, nr // 8 + 2 * EDGE3, nc // 4), F32),
            pltpu.VMEM((3, 8, 128), F32),
            pltpu.VMEM((peers, 8, 128), F32),
            pltpu.SemaphoreType.DMA((7,)),
            pltpu.SemaphoreType.DMA((16,)),
            pltpu.SemaphoreType.DMA((16,)),
            pltpu.SemaphoreType.DMA((8,)),
            pltpu.SemaphoreType.DMA((8,)),
            pltpu.SemaphoreType.DMA((peers,)),
            pltpu.SemaphoreType.DMA((peers,)),
        ],
        compiler_params=pltpu.CompilerParams(collective_id=0, has_side_effects=True),
    )(scene_offset, scene_weight, band_gain, heights, scene_ids, u, v)


def solution(mesh):
    placed = (P(("gy", "gz"), "gx"), P(("gy", "gz"), "gx"), P(), P(), P())
    shape = tuple(mesh.shape[name] for name in ("gx", "gy", "gz"))
    return jax.shard_map(
        functools.partial(local, shape), mesh=mesh, in_specs=placed,
        out_specs=P(("gy", "gz"), "gx"), check_vma=False,
    )
```

```python
import functools

import jax
import jax.numpy as jnp
import numpy as np
from jax import lax
from jax.experimental import pallas as pl
from jax.experimental.pallas import tpu as pltpu
from jax.sharding import PartitionSpec as P

F32, BF16 = jnp.float32, jnp.bfloat16
FAR = 1 << 20
HALO = 16
LANES = 128
LEVELS = 6
UP3, DOWN3 = 32, 32


def reach(count, levels):
    weights = np.ones(count >> levels, np.float64)
    for _ in range(levels):
        fine = np.zeros(2 * weights.size + 4, np.float64)
        for tap, value in zip(range(-2, 3), (0.0625, 0.25, 0.375, 0.25, 0.0625)):
            fine[2 + tap : 2 + tap + 2 * weights.size : 2] += value * weights
        weights = fine[2:-2]
    return weights


class Axis:
    def __init__(self, n, at, count):
        self.n, self.at, self.count = n, at, count

    def inside(self, index, level):
        place = index + self.at * (self.n >> level)
        return (place >= 0) & (place < self.count * (self.n >> level))

    def shrink(self, fine, coarse, level):
        far = np.abs(fine[:, None] - 2 * coarse[None, :])
        value = np.select([far == 0, far == 1, far == 2], [0.375, 0.25, 0.0625], 0.0)
        return value * self.inside(coarse, level)[None, :]

    def grow(self, coarse, fine, level):
        far = np.abs(2 * coarse[:, None] - fine[None, :])
        value = np.select([far == 0, far == 1, far == 2], [0.75, 0.5, 0.125], 0.0)
        return value * self.inside(fine, level)[None, :]

    def window(self, level, edge):
        return np.arange(-edge, (self.n >> level) + edge)

    def deep(self, lanes):
        out = self.out()
        w4, w5 = self.window(4, 30), self.window(5, 14)
        to4 = self.shrink(lanes, w4, 4)
        to5 = to4 @ self.shrink(w4, w5, 5)
        same = (lanes[:, None] == out[0][None, :]) * self.inside(out[0], 3)[None, :]
        parts = [
            same * 1.0,
            self.shrink(lanes, out[1], 4),
            to4 @ self.shrink(w4, out[2], 5),
            to5 @ self.shrink(w5, out[3], 6),
        ]
        return np.concatenate(parts, axis=1) * self.inside(lanes, 3)[:, None]

    def out(self):
        low = -4
        return [low + np.arange(size) for size in self.sizes()]

    def sizes(self):
        return [self.n // 8 + 8, self.n // 16 + 8, self.n // 32 + 8, self.n // 64 + 16]

    def back(self):
        o3, o4, o5, o6 = self.out()
        w4, w5 = self.window(4, 4), self.window(5, 4)
        from4 = self.grow(w4, o3, 3)
        from5 = self.grow(w5, w4, 4) @ from4
        parts = [
            np.eye(o3.size) * self.inside(o3, 3)[None, :],
            self.grow(o4, o3, 3),
            self.grow(o5, w4, 4) @ from4,
            self.grow(o6, w5, 5) @ from5,
        ]
        ones = self.inside(o6, 6) @ parts[3]
        return np.concatenate(parts, axis=0), ones

    def sums(self):
        weights = reach(self.count * (self.n >> 3), LEVELS - 3)
        place = self.out()[0] + self.at * (self.n >> 3)
        ok = (place >= 0) & (place < weights.size)
        return np.where(ok, weights[np.clip(place, 0, weights.size - 1)], 0.0)


def pad(x, shape):
    return np.pad(x, [(0, size - have) for size, have in zip(shape, x.shape)])


def halves(x):
    high = x.astype(np.float32).astype(jnp.bfloat16)
    low = (x - high.astype(np.float64)).astype(np.float32).astype(jnp.bfloat16)
    return high, low


def edged(n, low, size):
    ends = np.concatenate([np.arange(-4, 0), n + np.arange(4)])
    return np.concatenate([np.arange(n), ends, np.full(size - n - 8, FAR)]) + low


def col_tables(n, at, count):
    ax = Axis(n, at, count)
    if count == 2:
        sides = [1 if at == 0 else -1]
    else:
        sides = [-1, 1]
    lane = np.arange(LANES)
    own = np.arange(n)
    side = [lane - LANES if d < 0 else n + lane for d in sides]
    near = [lane if d < 0 else n - LANES + lane for d in sides]
    out1 = edged(n // 2, 0, n // 2 + LANES)
    out2 = edged(n // 4, 0, n // 4 + LANES)
    w1, w2 = ax.window(1, 16), ax.window(2, 8)
    c0 = ax.shrink(own, out1[: n // 2], 1)
    extra = []
    for k in range(len(sides)):
        block = np.concatenate(
            [ax.shrink(side[k], out1, 1), ax.shrink(near[k], out1, 1) * (out1 != out1.clip(0, n // 2 - 1))],
            axis=0,
        )
        extra.append(block)
    extra = np.concatenate(extra, axis=0)
    raw = np.concatenate([own] + side)
    c01 = ax.shrink(raw, w1, 1) @ ax.shrink(w1, out2, 2)
    o3 = ax.out()[0]
    c03 = ax.shrink(own, w1, 1) @ ax.shrink(w1, w2, 2) @ ax.shrink(w2, o3, 3)
    c03 = np.concatenate([pad(x.astype(np.float64), (n, LANES)) for x in halves(c03)], axis=1)
    three = np.concatenate([o3, np.full(LANES - o3.size, FAR)])
    sources = np.concatenate([three] + [three + d * (n // 8) for d in sides])
    stack = sum(ax.sizes())
    call = np.stack([pad(x.astype(np.float64), (sources.size, 256)) for x in halves(ax.deep(sources))])
    back, ones = ax.back()
    ec = np.stack([pad(x.astype(np.float64), (256, LANES)) for x in halves(back)])
    return dict(
        c0=c0, extra=extra, c01=c01, c03=c03, call=call, ec=ec,
        e2=ax.grow(three, out2, 2), e1=ax.grow(out2, out1, 1), e0=ax.grow(out1, own, 0),
    ), pad(ones[None], (1, LANES)), pad(ax.sums()[None], (1, LANES))


def row_tables(n, at, count):
    ax = Axis(n, at, count)
    o3 = ax.out()[0]
    t = n // 8
    rows = np.concatenate([o3[-UP3:] - t, o3, o3[:DOWN3] + t])
    deep = ax.deep(rows).T
    high, low = (x.astype(np.float64) for x in halves(deep))
    size6 = ax.sizes()[3]
    rall = np.concatenate([high, low[-size6:]], axis=0)
    rall = pad(rall, (-(-rall.shape[0] // 16) * 16, -(-rows.size // 16) * 16))
    back, ones = ax.back()
    er = np.stack([x.astype(np.float64) for x in halves(back.T)])
    return dict(rall=rall, er=er), ones[:, None], ax.sums()[:, None]


def tables(nr, nc, nx, blocks):
    def places(count):
        return (0, 1) if count == 2 else (0, 1, count - 1)

    cols = [col_tables(nc, at, nx) for at in places(nx)]
    rows = [row_tables(nr, at, blocks) for at in places(blocks)]

    def cast(x):
        return jnp.asarray(np.asarray(x, np.float32)).astype(BF16)

    by_col = {k: cast(np.stack([c[0][k] for c in cols])) for k in cols[0][0]}
    by_row = {k: cast(np.stack([r[0][k] for r in rows])) for k in rows[0][0]}
    both = np.stack([np.stack([np.stack([r[i] * c[i] for i in (1, 2)]) for c in cols]) for r in rows])
    return by_col, by_row, jnp.asarray(both.astype(np.float32))


def split(x):
    high = x.astype(BF16)
    return high, (x - high.astype(F32)).astype(BF16)


def dot(a, b):
    return jnp.dot(a, b, preferred_element_type=F32)


def right(x, c):
    high, low = split(x)
    return dot(high, c) + dot(low, c)


COLS = ("c03", "c0", "extra", "c01", "call", "ec", "e2", "e1", "e0")
ROWS = ("rall", "er")
CHUNKS = 4


def kernel(
    sizes, off_hbm, wgt_hbm, gain_hbm, h_ref, s_ref, *rest
):
    nr, nc, nx, ny, nz, ns = sizes
    names = COLS + ROWS + ("both",)
    tables_hbm, rest = dict(zip(names, rest)), rest[len(names):]
    out_ref, rest = rest[0], rest[1:]
    tab, rest = dict(zip(names, rest)), rest[len(names):]
    (
        off_ref, wgt_ref, gain_ref, h_buf, s_buf, q0, num, den, n1, d1, n2, d2, n3, d3,
        b3, z3b, z2b, z1b, wide, part, slots,
        own_sem, tab_sem, send0, recv0, send3, recv3, psend, precv,
    ) = rest
    cx, cy, cz = lax.axis_index("gx"), lax.axis_index("gy"), lax.axis_index("gz")
    row = cy * nz + cz
    blocks = ny * nz
    own_tiles = nc // LANES
    t3 = nr // 8
    m3 = t3 + 8

    def kind(at, count):
        return at if count == 2 else jnp.where(at == 0, 0, jnp.where(at == count - 1, 2, 1))

    ct, rt = kind(cx, nx), kind(row, blocks)

    loads = []
    step = nr // CHUNKS
    for k in range(CHUNKS):
        rows = pl.ds(k * step, step)
        for a, (src, dst) in enumerate(((h_ref, h_buf), (s_ref, s_buf))):
            loads.append(
                pltpu.make_async_copy(
                    src.at[rows, :],
                    dst.at[pl.ds(HALO + k * step, step), pl.ds(0, nc)],
                    own_sem.at[2 * k + a],
                )
            )
    small = [
        pltpu.make_async_copy(src, dst, own_sem.at[2 * CHUNKS + a])
        for a, (src, dst) in enumerate(((off_hbm, off_ref), (wgt_hbm, wgt_ref), (gain_hbm, gain_ref)))
    ]
    fetch = {}
    for i, name in enumerate(names):
        src = tables_hbm[name]
        src = src.at[ct] if name in COLS else src.at[rt] if name in ROWS else src.at[rt, ct]
        fetch[name] = pltpu.make_async_copy(src, tab[name], tab_sem.at[i])
    for copy in loads[:2] + small + loads[2:]:
        copy.start()

    up, down = row > 0, row < blocks - 1
    send_row, recv_row = {0: None, 1: down, 2: up}, {0: None, 1: up, 2: down}
    if ns == 1:
        send_col, recv_col = {0: None, 1: None}, {0: None, 1: None}
        to_col = {0: cx, 1: 1 - cx}
        src_col = {1: pl.multiple_of((1 - cx) * (nc - LANES), LANES)}
        near_tile = {1: (1 - cx) * (own_tiles - 1)}
    else:
        send_col = {0: None, 1: cx < nx - 1, 2: cx > 0}
        recv_col = {0: None, 1: cx > 0, 2: cx < nx - 1}
        to_col = {0: cx, 1: cx + 1, 2: cx - 1}
        src_col = {1: nc - LANES, 2: 0}
        near_tile = {1: 0, 2: own_tiles - 1}
    kinds = [(rp, cp) for rp in (0, 1, 2) for cp in range(1 + ns) if rp or cp]

    def device(rp, cp):
        target = row + {0: 0, 1: 1, 2: -1}[rp]
        return {"gx": to_col[cp], "gy": target // nz, "gz": target % nz}

    def also(a, b):
        return b if a is None else a if b is None else jnp.logical_and(a, b)

    def sends(rp, cp):
        return also(send_row[rp], send_col[cp])

    def comes(rp, cp):
        return also(recv_row[rp], recv_col[cp])

    def given(flag, body):
        if flag is None:
            body()
        else:
            pl.when(flag)(body)

    axes = (("gx", nx, cx), ("gz", nz, cz), ("gy", ny, cy))
    barrier = pltpu.get_barrier_semaphore()
    for d in kinds:
        given(sends(*d), lambda: pl.semaphore_signal(barrier, inc=1, device_id=device(*d)))
    for name, count, me in axes:
        for s in range(1, count):
            pl.semaphore_signal(barrier, inc=1, device_id={name: (me + s) % count})

    for copy in fetch.values():
        copy.start()

    zero = jnp.zeros((HALO, LANES), F32)
    for x in (num, den):
        for c in range(own_tiles + ns):
            x[c, 0:HALO, :] = zero
            x[c, nr + HALO : nr + 2 * HALO, :] = zero
            x[c, nr + 2 * HALO :, :] = zero
    zero = jnp.zeros((8, LANES), F32)
    for x in (n1, d1, n2, d2):
        for c in range(own_tiles + ns):
            x[c, 0:8, :] = zero
            x[c, x.shape[1] - 8 :, :] = zero
    z3b[m3:, :] = zero
    for k in range(1 + ns):
        for a in range(2):
            b3[k, a, UP3 + m3 + DOWN3 :, :] = zero

    def rim(i, a):
        rp, cp = kinds[i]
        src, dst = ((h_ref, h_buf), (s_ref, s_buf))[a]
        rs = {0: (0, HALO, nr), 1: (nr - HALO, 0, HALO), 2: (0, nr + HALO, HALO)}[rp]
        cs = (0, 0, nc) if cp == 0 else (src_col[cp], nc + (cp - 1) * LANES, LANES)
        return pltpu.make_async_remote_copy(
            src_ref=src.at[pl.ds(rs[0], rs[2]), pl.ds(cs[0], cs[2])],
            dst_ref=dst.at[pl.ds(rs[1], rs[2]), pl.ds(cs[1], cs[2])],
            send_sem=send0.at[2 * i + a],
            recv_sem=recv0.at[2 * i + a],
            device_id=device(rp, cp),
        )

    def rim3(i):
        rp, cp = kinds[i]
        rs = {0: (UP3, UP3, m3), 1: (UP3 + m3 - UP3, 0, UP3), 2: (UP3, UP3 + m3, DOWN3)}[rp]
        return pltpu.make_async_remote_copy(
            src_ref=b3.at[0, :, pl.ds(rs[0], rs[2]), :],
            dst_ref=b3.at[cp, :, pl.ds(rs[1], rs[2]), :],
            send_sem=send3.at[i],
            recv_sem=recv3.at[i],
            device_id=device(rp, cp),
        )

    lane8 = lax.broadcasted_iota(jnp.int32, (8, LANES), 1)
    line8 = lax.broadcasted_iota(jnp.int32, (8, LANES), 0)

    def spread(table):
        line = jnp.zeros((8, LANES), F32)
        for i in range(table.shape[0]):
            line = jnp.where(lane8 == i, table[i], line)
        return line

    for copy in small:
        copy.wait()
    wgt_row, off_row = spread(wgt_ref), spread(off_ref)

    def level0(base, count, c):
        rows = pl.ds(base, count)
        ids = s_buf[rows, c * LANES : (c + 1) * LANES]

        def look(table):
            return jnp.concatenate(
                [jnp.take_along_axis(table, ids[r : r + 8], axis=1) for r in range(0, count, 8)], axis=0
            )

        weight = look(wgt_row)
        moved = h_buf[rows, c * LANES : (c + 1) * LANES] + look(off_row)
        num[c, rows, :] = weight * moved
        den[c, rows, :] = weight
        return moved

    near = sum(jnp.int32(1) if comes(*d) is None else comes(*d).astype(jnp.int32) for d in kinds)

    def meet():
        pl.semaphore_wait(barrier, near + (nx + ny + nz - 3))
        for i, d in enumerate(kinds):
            @functools.partial(given, sends(*d))
            def _():
                for a in range(2):
                    rim(i, a).start()

    meet()

    inner = 32
    for k in range(CHUNKS):
        with jax.named_scope("level0_%d" % k):
            loads[2 * k].wait()
            loads[2 * k + 1].wait()

            def some(i, carry):
                base = pl.multiple_of(HALO + k * step + i * inner, 16)
                for c in range(own_tiles):
                    q0[c, pl.ds(base - HALO, inner), :] = level0(base, inner, c)
                return carry

            lax.fori_loop(0, step // inner, some, 0)


    def taps(src, c, start, count):
        x = [src[c, pl.ds(start + a, count, stride=2), :] for a in range(-2, 3)]
        return 0.375 * x[2] + (0.25 * (x[1] + x[3]) + 0.0625 * (x[0] + x[4]))

    def hold(x, c, p, first):
        if first:
            ok = jnp.logical_or(line8 >= 4, up)
        else:
            ok = jnp.logical_or(line8 < 4, down)
        x[c, p : p + 8, :] = jnp.where(ok, x[c, p : p + 8, :], 0.0)

    last1, last2 = nr // 2 + 8, nr // 4 + 8

    def ends1(x, c):
        hold(x, c, 8, True)
        hold(x, c, last1, False)

    def ends2(x, c):
        hold(x, c, 8, True)
        hold(x, c, last2, False)

    def rows1(src, dst, c, p, count):
        dst[c, p : p + count, :] = taps(src, c, 2 * p - 8, count)

    def rows2(src, dst, c, p, count):
        dst[c, p : p + count, :] = taps(src, c, 2 * p - 12, count)

    with jax.named_scope("rowpyr"):
        for src, one, two, three in ((num, n1, n2, n3), (den, d1, d2, d3)):
            for c in range(own_tiles):
                rows1(src, one, c, 8, nr // 2 + 16)
                ends1(one, c)
                rows2(one, two, c, 8, nr // 4 + 8)
                ends2(two, c)
                three[c] = taps(two, c, 4, m3)

    def wide_of(x, rows, tiles):
        return jnp.concatenate([x[c, rows, :] for c in tiles], axis=1)

    own_range = range(own_tiles)
    with jax.named_scope("p3"):
        fetch["c03"].wait()
        x = jnp.concatenate([wide_of(n3, slice(None), own_range), wide_of(d3, slice(None), own_range)], axis=0)
        x = right(x, tab["c03"][...])
        x = x[:, :LANES] + x[:, LANES:]
        b3[0, 0, UP3 : UP3 + m3, :] = x[:m3]
        b3[0, 1, UP3 : UP3 + m3, :] = x[m3:]
        for i, d in enumerate(kinds):
            given(sends(*d), lambda: rim3(i).start())
        fetch["both"].wait()
        reach3 = tab["both"][1]
        sum_n, sum_d = jnp.sum(x[:m3] * reach3), jnp.sum(x[m3:] * reach3)
        part[0] = jnp.where(line8 == 0, sum_n, jnp.where(line8 == 1, sum_d, 0.0))

    starts = (0, nx - 1, nx + nz - 2)

    def phase(k):
        name, count, me = axes[k]
        return [
            pltpu.make_async_remote_copy(
                src_ref=part.at[k],
                dst_ref=slots.at[starts[k] + s - 1],
                send_sem=psend.at[starts[k] + s - 1],
                recv_sem=precv.at[starts[k] + s - 1],
                device_id={name: (me + s) % count},
            )
            for s in range(1, count)
        ]

    def finish(k):
        total = part[k]
        for s, copy in enumerate(phase(k)):
            copy.wait()
            total = total + slots[starts[k] + s]
        return total

    for copy in phase(0):
        copy.start()

    def take(i):
        @functools.partial(given, sends(*kinds[i]))
        def _():
            for a in range(2):
                rim(i, a).wait_send()

        @functools.partial(given, comes(*kinds[i]))
        def _():
            for a in range(2):
                rim(i, a).wait_recv()

    with jax.named_scope("w_side"):
        for i, d in enumerate(kinds):
            if d[0] == 0:
                take(i)

    def cleared(c, base, count):
        for x in (num, den):
            x[c, pl.ds(base, count), :] = jnp.zeros((count, LANES), F32)

    with jax.named_scope("side"):
        for k in range(1, 1 + ns):
            c = own_tiles + k - 1

            def side():
                def some(i, carry):
                    level0(pl.multiple_of(HALO + i * inner, 16), inner, c)
                    return carry

                lax.fori_loop(0, nr // inner, some, 0)

            given(recv_col[k], side)
            if recv_col[k] is not None:
                pl.when(jnp.logical_not(recv_col[k]))(lambda: cleared(c, HALO, nr))

    with jax.named_scope("w_phase0"):
        part[1] = finish(0)
        for copy in phase(1):
            copy.start()

    with jax.named_scope("w_rims"):
        for i, d in enumerate(kinds):
            if d[0] != 0:
                take(i)
    with jax.named_scope("rims"):
        for rp, base in ((1, 0), (2, nr + HALO)):
            for cp in range(1 + ns):
                tiles = own_range if cp == 0 else (own_tiles + cp - 1,)

                def edge():
                    for c in tiles:
                        level0(base, HALO, c)

                given(comes(rp, cp), edge)

        for src, one, two in ((num, n1, n2), (den, d1, d2)):
            for c in range(own_tiles + ns):
                if c < own_tiles:
                    rows1(src, one, c, 8, 8)
                    rows1(src, one, c, last1, 16)
                else:
                    rows1(src, one, c, 8, nr // 2 + 16)
                ends1(one, c)
                if c < own_tiles:
                    rows2(one, two, c, 8, 8)
                    rows2(one, two, c, last2, 8)
                else:
                    rows2(one, two, c, 8, nr // 4 + 8)
                ends2(two, c)

    def ratio(n, d):
        return jnp.where(d > 0, n / d, 0.0)

    all_range = range(own_tiles + ns)
    body1, body2 = slice(8, nr // 2 + 24), slice(8, nr // 4 + 24)

    def level1(x):
        edge = jnp.concatenate(
            [y for k in range(1, 1 + ns) for y in (x[own_tiles + k - 1, body1, :], x[near_tile[k], body1, :])],
            axis=1,
        )
        own = right(wide_of(x, body1, own_range), tab["c0"][...])
        edge = right(edge, tab["extra"][...])
        half = nc // 2
        return jnp.concatenate([own + edge[:, :half], edge[:, half:]], axis=1)

    with jax.named_scope("q1"):
        fetch["c0"].wait()
        fetch["extra"].wait()
        q1 = ratio(level1(n1), level1(d1))
    with jax.named_scope("q2"):
        fetch["c01"].wait()
        q2 = ratio(
            right(wide_of(n2, body2, all_range), tab["c01"][...]),
            right(wide_of(d2, body2, all_range), tab["c01"][...]),
        )

    with jax.named_scope("w_phase1"):
        part[2] = finish(1)
        for copy in phase(2):
            copy.start()

    with jax.named_scope("w_b3"):
        for i, d in enumerate(kinds):
            given(sends(*d), lambda: rim3(i).wait_send())
            given(comes(*d), lambda: rim3(i).wait_recv())
        for i, (rp, cp) in enumerate(kinds):
            flag = comes(rp, cp)
            if flag is not None:
                rs = {0: (UP3, m3), 1: (0, UP3), 2: (UP3 + m3, DOWN3)}[rp]

                def clear():
                    b3[cp, :, rs[0] : rs[0] + rs[1], :] = jnp.zeros((2, rs[1], LANES), F32)

                pl.when(jnp.logical_not(flag))(clear)
        for name in ("call", "ec", "e2", "e1", "e0", "rall", "er"):
            fetch[name].wait()

    s3, s4, s5, s6 = (nr // 8 + 8, nr // 16 + 8, nr // 32 + 8, nr // 64 + 16)
    stack = s3 + s4 + s5 + s6
    with jax.named_scope("deep"):
        packed = []
        for a in range(2):
            x = jnp.concatenate([b3[k, a] for k in range(1 + ns)], axis=1)
            high, low = split(x)
            rall = tab["rall"][...]
            x = dot(rall, high) + dot(rall, low)
            packed += [x[: stack - s6], x[stack - s6 : stack] + x[stack : stack + s6]]
        high, low = split(jnp.concatenate(packed, axis=0))
        x = dot(high, tab["call"][0]) + dot(low, tab["call"][0]) + dot(high, tab["call"][1])

        def level_of(shape, dim, cuts):
            index = lax.broadcasted_iota(jnp.int32, shape, dim)
            return sum((index >= cut).astype(jnp.int32) for cut in cuts)

        c3, c4, c5 = nc // 8 + 8, nc // 16 + 8, nc // 32 + 8
        shape = (stack, 256)
        at_row = level_of(shape, 0, (s3, s3 + s4, s3 + s4 + s5))
        at_col = level_of(shape, 1, (c3, c3 + c4, c3 + c4 + c5))
        gains = [gain_ref[level] - gain_ref[level - 1] for level in (3, 4, 5)] + [-gain_ref[5]]
        factor = jnp.where(
            at_row == 0, gains[0], jnp.where(at_row == 1, gains[1], jnp.where(at_row == 2, gains[2], gains[3]))
        )
        d = x[stack:]
        x = jnp.where(jnp.logical_and(at_row == at_col, d > 0), factor * (x[:stack] / d), 0.0)
        high, low = split(x)
        er = tab["er"]
        x = dot(er[0], high) + dot(er[0], low) + dot(er[1], high)
        high, low = split(x)
        ec = tab["ec"]
        z3 = dot(high, ec[0]) + dot(low, ec[0]) + dot(high, ec[1])

    with jax.named_scope("w_phase2"):
        total = finish(2)
    with jax.named_scope("z2"):
        top_sum = jnp.sum(jnp.where(line8 == 0, total, 0.0), axis=0, keepdims=True)
        top_weight = jnp.sum(jnp.where(line8 == 1, total, 0.0), axis=0, keepdims=True)
        top_mean = top_sum / top_weight
        z3b[0:m3, :] = z3 + top_mean * tab["both"][0]

        def grow_rows(src, dst, put, get, count):
            x, y, w = (src[get + (slice(k, k + count), slice(None))] for k in (1, 2, 3))
            dst[put + (pl.ds(0, count, stride=2), slice(None))] = 0.125 * (x + w) + 0.75 * y
            dst[put + (pl.ds(1, count, stride=2), slice(None))] = 0.5 * (y + w)

        def block(x, put, p, first):
            ok = jnp.logical_or(line8 >= 4, up) if first else jnp.logical_or(line8 < 4, down)
            x[put + (slice(p, p + 8), slice(None))] = jnp.where(ok, x[put + (slice(p, p + 8), slice(None))], 0.0)

        grow_rows(z3b, z2b, (0,), (), nr // 8 + 8)
        block(z2b, (0,), 0, True)
        block(z2b, (0,), nr // 4, False)
        z2 = right(z2b[0], tab["e2"][...]) + (gain_ref[2] - gain_ref[1]) * q2
        tiles2 = z2.shape[1] // LANES
        for c in range(tiles2):
            z2b[c] = z2[:, c * LANES : (c + 1) * LANES]
    with jax.named_scope("z1"):
        for c in range(tiles2):
            grow_rows(z2b, z1b, (c,), (c,), nr // 4 + 8)
            block(z1b, (c,), 0, True)
            block(z1b, (c,), nr // 2, False)
        z1 = right(wide_of(z1b, slice(None), range(tiles2)), tab["e1"][...]) + (gain_ref[1] - gain_ref[0]) * q1
    with jax.named_scope("e0"):
        full = right(z1, tab["e0"][...])
        for c in own_range:
            wide[c] = full[:, c * LANES : (c + 1) * LANES]
    with jax.named_scope("out"):
        gain = gain_ref[0]
        chunk = 32
        for c in own_range:
            for m in range(0, nr // 2, chunk):
                x, y, w = (wide[c, pl.ds(m + k, chunk), :] for k in (3, 4, 5))
                even, odd = pl.ds(2 * m, chunk, stride=2), pl.ds(2 * m + 1, chunk, stride=2)
                q0[c, even, :] = gain * q0[c, even, :] + (0.125 * (x + w) + 0.75 * y)
                q0[c, odd, :] = gain * q0[c, odd, :] + 0.5 * (y + w)
                out_ref[pl.ds(2 * m, 2 * chunk), c * LANES : (c + 1) * LANES] = q0[c, pl.ds(2 * m, 2 * chunk), :]


def local(mesh_shape, heights, scene_ids, scene_offset, scene_weight, band_gain):
    nx, ny, nz = mesh_shape
    nr, nc = heights.shape
    ns = 1 if nx == 2 else 2
    by_col, by_row, both = tables(nr, nc, nx, ny * nz)
    given = [by_col[k] for k in COLS] + [by_row[k] for k in ROWS] + [both]
    skip = [1] * len(COLS) + [1] * len(ROWS) + [2]
    sizes = (nr, nc, nx, ny, nz, ns)
    ext = (nr + 2 * HALO, nc + ns * LANES)
    own_tiles = nc // LANES
    tiles = own_tiles + ns
    m3 = nr // 8 + 8
    rows_b = -(-(UP3 + m3 + DOWN3) // 16) * 16
    if rows_b == UP3 + m3 + DOWN3:
        rows_b += 16
    peers = nx + ny + nz - 3
    messages = 3 * (1 + ns) - 1
    hbm = pl.BlockSpec(memory_space=pltpu.HBM)
    return pl.pallas_call(
        functools.partial(kernel, sizes),
        out_shape=pltpu.VMEM((nr, nc), F32),
        in_specs=[hbm] * (5 + len(given)),
        out_specs=pl.BlockSpec(memory_space=pltpu.VMEM),
        scratch_shapes=[pltpu.VMEM(x.shape[k:], x.dtype) for x, k in zip(given, skip)]
        + [
            pltpu.SMEM(scene_offset.shape, F32),
            pltpu.SMEM(scene_weight.shape, F32),
            pltpu.SMEM(band_gain.shape, F32),
            pltpu.VMEM(ext, F32),
            pltpu.VMEM(ext, jnp.int32),
            pltpu.VMEM((own_tiles, nr, LANES), F32),
        ]
        + [pltpu.VMEM((tiles, nr + 3 * HALO, LANES), F32)] * 2
        + [pltpu.VMEM((tiles, nr // 2 + 32, LANES), F32)] * 2
        + [pltpu.VMEM((tiles, nr // 4 + 24, LANES), F32)] * 2
        + [pltpu.VMEM((own_tiles, m3, LANES), F32)] * 2
        + [
            pltpu.VMEM((1 + ns, 2, rows_b, LANES), F32),
            pltpu.VMEM((m3 + 8, LANES), F32),
            pltpu.VMEM((nc // 4 // LANES + 1, nr // 4 + 16, LANES), F32),
            pltpu.VMEM((nc // 4 // LANES + 1, nr // 2 + 16, LANES), F32),
            pltpu.VMEM((own_tiles, nr // 2 + 16, LANES), F32),
            pltpu.VMEM((3, 8, LANES), F32),
            pltpu.VMEM((peers, 8, LANES), F32),
            pltpu.SemaphoreType.DMA((2 * CHUNKS + 3,)),
            pltpu.SemaphoreType.DMA((len(given),)),
            pltpu.SemaphoreType.DMA((2 * messages,)),
            pltpu.SemaphoreType.DMA((2 * messages,)),
            pltpu.SemaphoreType.DMA((messages,)),
            pltpu.SemaphoreType.DMA((messages,)),
            pltpu.SemaphoreType.DMA((peers,)),
            pltpu.SemaphoreType.DMA((peers,)),
        ],
        compiler_params=pltpu.CompilerParams(collective_id=0, has_side_effects=True),
    )(scene_offset, scene_weight, band_gain, heights, scene_ids, *given)


def solution(mesh):
    placed = (P(("gy", "gz"), "gx"), P(("gy", "gz"), "gx"), P(), P(), P())
    shape = tuple(mesh.shape[name] for name in ("gx", "gy", "gz"))
    return jax.shard_map(
        functools.partial(local, shape), mesh=mesh, in_specs=placed,
        out_specs=P(("gy", "gz"), "gx"), check_vma=False,
    )
```

```python
import functools

import jax
import jax.numpy as jnp
import numpy as np
from jax import lax
from jax.experimental import pallas as pl
from jax.experimental.pallas import tpu as pltpu
from jax.sharding import PartitionSpec as P

F32, BF16 = jnp.float32, jnp.bfloat16
FAR = 1 << 20
HALO = 16
LANES = 128
LEVELS = 6
MIDDLE = (3, 4, 5)


def reach(count, levels):
    weights = np.ones(count >> levels, np.float64)
    for _ in range(levels):
        fine = np.zeros(2 * weights.size + 4, np.float64)
        for tap, value in zip(range(-2, 3), (0.0625, 0.25, 0.375, 0.25, 0.0625)):
            fine[2 + tap : 2 + tap + 2 * weights.size : 2] += value * weights
        weights = fine[2:-2]
    return weights


class Axis:
    def __init__(self, n, at, count):
        self.n, self.at, self.count = n, at, count

    def inside(self, index, level):
        place = index + self.at * (self.n >> level)
        return (place >= 0) & (place < self.count * (self.n >> level))

    def shrink(self, fine, coarse, level):
        far = np.abs(fine[:, None] - 2 * coarse[None, :])
        value = np.select([far == 0, far == 1, far == 2], [0.375, 0.25, 0.0625], 0.0)
        return value * self.inside(coarse, level)[None, :]

    def grow(self, coarse, fine, level):
        far = np.abs(2 * coarse[:, None] - fine[None, :])
        value = np.select([far == 0, far == 1, far == 2], [0.75, 0.5, 0.125], 0.0)
        return value * self.inside(fine, level)[None, :]

    def window(self, level, edge):
        return np.arange(-edge, (self.n >> level) + edge)

    def deep(self, lanes, shift=0):
        out = [x + shift * (self.n >> level) for level, x in zip((3, 4, 5, 6), self.out())]
        w4, w5 = self.window(4, 30), self.window(5, 14)
        to4 = self.shrink(lanes, w4, 4)
        to5 = to4 @ self.shrink(w4, w5, 5)
        same = (lanes[:, None] == out[0][None, :]) * self.inside(out[0], 3)[None, :]
        parts = [
            same * 1.0,
            self.shrink(lanes, out[1], 4),
            to4 @ self.shrink(w4, out[2], 5),
            to5 @ self.shrink(w5, out[3], 6),
        ]
        return np.concatenate(parts, axis=1) * self.inside(lanes, 3)[:, None]

    def out(self):
        low = -4
        return [low + np.arange(size) for size in self.sizes()]

    def sizes(self):
        return [self.n // 8 + 8, self.n // 16 + 8, self.n // 32 + 8, self.n // 64 + 16]

    def back(self):
        o3, o4, o5, o6 = self.out()
        w4, w5 = self.window(4, 4), self.window(5, 4)
        from4 = self.grow(w4, o3, 3)
        from5 = self.grow(w5, w4, 4) @ from4
        parts = [
            np.eye(o3.size) * self.inside(o3, 3)[None, :],
            self.grow(o4, o3, 3),
            self.grow(o5, w4, 4) @ from4,
            self.grow(o6, w5, 5) @ from5,
        ]
        return np.concatenate(parts, axis=0)

    def sums(self):
        return reach(self.count * self.n, LEVELS)[self.at * self.n : (self.at + 1) * self.n]

    def ones(self, level):
        x = self.inside(self.window(6, 4), 6) * 1.0
        for k in range(5, level - 1, -1):
            x = x @ self.grow(self.window(k + 1, 4), self.window(k, 4), k)
        return x


def pad(x, shape):
    return np.pad(x, [(0, size - have) for size, have in zip(shape, x.shape)])


def halves(x):
    high = x.astype(np.float32).astype(jnp.bfloat16)
    low = (x - high.astype(np.float64)).astype(np.float32).astype(jnp.bfloat16)
    return high, low


def spaced(n):
    size = -(-(n + 8) // LANES) * LANES
    return np.concatenate([np.arange(-4, n + 4), np.full(size - n - 8, FAR)])


def col_tables(n, at, count):
    ax = Axis(n, at, count)
    shifts = [1 if at == 0 else -1] if count == 2 else [1, -1]
    lane = np.arange(LANES)
    own = np.arange(n)
    out1, out2 = spaced(n // 2), spaced(n // 4)
    w1, w2 = ax.window(1, 16), ax.window(2, 8)
    middle = np.isin(lane, MIDDLE)[None, :]
    s1, s2 = [], []
    for d in shifts:
        near = n - LANES + lane if d > 0 else lane
        over1, over2 = (lane - 4 + (n >> level if d > 0 else 0) for level in (1, 2))
        s1.append(ax.shrink(near, over1, 1) * middle)
        s2.append(ax.shrink(near, w1, 1) @ ax.shrink(w1, over2, 2) * middle)
    s1, s2 = (np.stack([np.stack([x, np.roll(x, LANES // 2, 1)]) for x in y]) for y in (s1, s2))
    o3 = ax.out()[0]
    to2 = ax.shrink(own, w1, 1)
    c03 = to2 @ ax.shrink(w1, w2, 2) @ ax.shrink(w2, o3, 3)
    c03 = np.concatenate([pad(x.astype(np.float64), (n, LANES)) for x in halves(c03)], axis=1)
    three = np.concatenate([o3, np.full(LANES - o3.size, FAR)])
    call = []
    for d in [0] + shifts:
        call.append([pad(x.astype(np.float64), (LANES, 256)) for x in halves(ax.deep(three, d))])
    call = np.stack([np.concatenate([x[k] for x in call], axis=1) for k in range(2)])
    back = ax.back()
    ec = np.stack([pad(x.astype(np.float64), (256, LANES)) for x in halves(back)])
    return dict(
        c1=ax.shrink(own, out1, 1), c2=to2 @ ax.shrink(w1, out2, 2), s1=s1, s2=s2, c03=c03, call=call,
        ec=ec, e2=ax.grow(three, out2, 2), e1=ax.grow(out2, out1, 1), e0=ax.grow(out1, own, 0),
    ), dict(line=np.stack([ax.sums(), ax.ones(0)[4:-4]]))


def row_tables(n, at, count):
    ax = Axis(n, at, count)
    o3 = ax.out()[0]
    deep = ax.deep(o3).T
    high, low = (x.astype(np.float64) for x in halves(deep))
    size6 = ax.sizes()[3]
    rall = np.concatenate([high, low[-size6:]], axis=0)
    rall = pad(rall, (-(-rall.shape[0] // 16) * 16, o3.size))
    back = ax.back()
    er = np.stack([x.astype(np.float64) for x in halves(back.T)])
    first = np.repeat(ax.sums()[:, None], LANES, 1)
    second = np.repeat(pad(ax.ones(1), (n // 2 + 16,))[:, None], LANES, 1)
    return dict(rall=rall, er=er), dict(first=first, second=second)


def tables(nr, nc, nx, blocks):
    def places(count):
        return (0, 1) if count == 2 else (0, 1, count - 1)

    cols = [col_tables(nc, at, nx) for at in places(nx)]
    rows = [row_tables(nr, at, blocks) for at in places(blocks)]

    def cast(x):
        return jnp.asarray(np.asarray(x, np.float32)).astype(BF16)

    def keep(x):
        return jnp.asarray(np.asarray(x, np.float32))

    out = {}
    for some in (cols, rows):
        for k in some[0][0]:
            out[k] = cast(np.stack([x[0][k] for x in some]))
        for k in some[0][1]:
            out[k] = keep(np.stack([x[1][k] for x in some]))
    return out


def split(x):
    high = x.astype(BF16)
    return high, (x - high.astype(F32)).astype(BF16)


def dot(a, b):
    return jnp.dot(a, b, preferred_element_type=F32)


def right(x, c):
    high, low = split(x)
    return dot(high, c) + dot(low, c)


COLS = ("line", "c03", "call", "c1", "c2", "s1", "s2", "ec", "e2", "e1", "e0")
ROWS = ("first", "rall", "er", "second")
CHUNKS = 4


def kernel(
    sizes, off_hbm, wgt_hbm, gain_hbm, h_ref, s_ref, *rest
):
    nr, nc, nx, ny, nz, ns = sizes
    names = COLS + ROWS
    tables_hbm, rest = dict(zip(names, rest)), rest[len(names):]
    out_ref, rest = rest[0], rest[1:]
    tab, rest = dict(zip(names, rest)), rest[len(names):]
    (
        off_ref, wgt_ref, gain_ref, h_buf, s_buf, q0, num, den, n1, d1, n2, d2, n3, d3,
        x1, x2, g, y1, y2, side_s, side_r, edge_s, edge_r, z3b, z2b, z1b, wide, part, slots,
        own_sem, tab_sem, send0, recv0, psend, precv,
    ) = rest
    cx, cy, cz = lax.axis_index("gx"), lax.axis_index("gy"), lax.axis_index("gz")
    row = cy * nz + cz
    blocks = ny * nz
    own_tiles = nc // LANES
    t3 = nr // 8
    m3 = t3 + 8

    def kind(at, count):
        return at if count == 2 else jnp.where(at == 0, 0, jnp.where(at == count - 1, 2, 1))

    ct, rt = kind(cx, nx), kind(row, blocks)

    loads = []
    step = nr // CHUNKS
    for k in range(CHUNKS):
        rows = pl.ds(k * step, step)
        for a, (src, dst) in enumerate(((h_ref, h_buf), (s_ref, s_buf))):
            loads.append(
                pltpu.make_async_copy(
                    src.at[rows, :],
                    dst.at[pl.ds(HALO + k * step, step), pl.ds(0, nc)],
                    own_sem.at[2 * k + a],
                )
            )
    small = [
        pltpu.make_async_copy(src, dst, own_sem.at[2 * CHUNKS + a])
        for a, (src, dst) in enumerate(((off_hbm, off_ref), (wgt_hbm, wgt_ref), (gain_hbm, gain_ref)))
    ]
    fetch = {}
    for i, name in enumerate(names):
        src = tables_hbm[name]
        src = src.at[ct] if name in COLS else src.at[rt]
        fetch[name] = pltpu.make_async_copy(src, tab[name], tab_sem.at[i])
    early = ["first", "line"]
    for copy in loads[:2] + small + [fetch[name] for name in early] + loads[2:]:
        copy.start()

    up, down = row > 0, row < blocks - 1
    send_row, recv_row = {0: None, 1: down, 2: up}, {0: None, 1: up, 2: down}
    if ns == 1:
        send_col, recv_col = {0: None, 1: None}, {0: None, 1: None}
        to_col = {0: cx, 1: 1 - cx}
        near_tile = {1: (1 - cx) * (own_tiles - 1)}
        into1, into2 = {1: (1 - cx) * (x1.shape[1] - 1)}, {1: (1 - cx) * (x2.shape[1] - 1)}
    else:
        send_col = {0: None, 1: cx < nx - 1, 2: cx > 0}
        recv_col = {0: None, 1: cx > 0, 2: cx < nx - 1}
        to_col = {0: cx, 1: cx + 1, 2: cx - 1}
        near_tile = {1: own_tiles - 1, 2: 0}
        into1, into2 = {1: 0, 2: x1.shape[1] - 1}, {1: 0, 2: x2.shape[1] - 1}
    kinds = [(rp, cp) for rp in (0, 1, 2) for cp in range(1 + ns) if rp or cp]

    def device(rp, cp):
        target = row + {0: 0, 1: 1, 2: -1}[rp]
        return {"gx": to_col[cp], "gy": target // nz, "gz": target % nz}

    def also(a, b):
        return b if a is None else a if b is None else jnp.logical_and(a, b)

    def sends(rp, cp):
        return also(send_row[rp], send_col[cp])

    def comes(rp, cp):
        return also(recv_row[rp], recv_col[cp])

    def given(flag, body):
        if flag is None:
            body()
        else:
            pl.when(flag)(body)

    everyone = nx * blocks
    me = row * nx + cx

    def peer(s):
        other = (me + s) % everyone
        line = other // nx
        return {"gx": other % nx, "gy": line // nz, "gz": line % nz}

    barrier = pltpu.get_barrier_semaphore()

    def greet(s, carry):
        pl.semaphore_signal(barrier, inc=1, device_id=peer(s))
        return carry

    lax.fori_loop(1, everyone, greet, 0)

    for name, copy in fetch.items():
        if name not in early:
            copy.start()

    zero = jnp.zeros((HALO, LANES), F32)
    for x in (num, den):
        for c in range(own_tiles):
            x[c, 0:HALO, :] = zero
            x[c, nr + HALO : nr + 2 * HALO, :] = zero
            x[c, nr + 2 * HALO :, :] = zero
    zero = jnp.zeros((8, LANES), F32)
    for x in (n1, d1, n2, d2):
        for c in range(own_tiles):
            x[c, 0:8, :] = zero
            x[c, x.shape[1] - 8 :, :] = zero
    z3b[m3:, :] = zero

    def edge(i):
        rp, cp = kinds[i]
        if rp == 0:
            src, dst = side_s.at[cp - 1], side_r.at[cp - 1]
        elif cp == 0:
            src, dst = edge_s.at[rp - 1, 0], edge_r.at[rp - 1, 0]
        else:
            src, dst = edge_s.at[rp - 1, cp, pl.ds(0, 4)], edge_r.at[rp - 1, cp, pl.ds(0, 4)]
        return pltpu.make_async_remote_copy(
            src_ref=src, dst_ref=dst, send_sem=send0.at[i], recv_sem=recv0.at[i], device_id=device(rp, cp)
        )

    lane8 = lax.broadcasted_iota(jnp.int32, (8, LANES), 1)
    line8 = lax.broadcasted_iota(jnp.int32, (8, LANES), 0)

    def spread(table):
        line = jnp.zeros((8, LANES), F32)
        for i in range(table.shape[0]):
            line = jnp.where(lane8 == i, table[i], line)
        return line

    for copy in small:
        copy.wait()
    wgt_row = spread(wgt_ref)

    def tree(ids, table):
        values = [table[i] for i in range(table.shape[0])]
        bit = 1
        while len(values) > 1:
            mask = (ids & bit) != 0
            values = [jnp.where(mask, values[i + 1], values[i]) for i in range(0, len(values), 2)]
            bit *= 2
        return values[0]

    def level0(base, count, c):
        rows = pl.ds(base, count)
        ids = s_buf[rows, c * LANES : (c + 1) * LANES]
        weight = jnp.concatenate(
            [jnp.take_along_axis(wgt_row, ids[r : r + 8], axis=1) for r in range(0, count, 8)], axis=0
        )
        moved = h_buf[rows, c * LANES : (c + 1) * LANES] + tree(ids, off_ref)
        numer = weight * moved
        num[c, rows, :] = numer
        den[c, rows, :] = weight
        return moved, numer, weight

    def summary(s):
        return pltpu.make_async_remote_copy(
            src_ref=part,
            dst_ref=slots.at[s - 1],
            send_sem=psend.at[s - 1],
            recv_sem=precv.at[s - 1],
            device_id=peer(s),
        )

    def send_edges(wanted):
        for i, d in enumerate(kinds):
            if wanted(d):
                given(sends(*d), lambda: edge(i).start())

    with jax.named_scope("level0"):
        fetch["first"].wait()
        sums = [[0.0] * own_tiles, [0.0] * own_tiles]
        for k in range(CHUNKS):
            loads[2 * k].wait()
            loads[2 * k + 1].wait()
            weights = tab["first"][k * step : (k + 1) * step, :]
            for c in range(own_tiles):
                moved, numer, weight = level0(HALO + k * step, step, c)
                q0[c, k * step : (k + 1) * step, :] = moved
                for a, x in enumerate((numer, weight)):
                    x = (x * weights).reshape(step // 8, 8, LANES)
                    sums[a][c] = sums[a][c] + jnp.sum(x, axis=0)
        fetch["line"].wait()
        flat = []
        for a in range(2):
            x = sum(sums[a][c] * tab["line"][0:1, c * LANES : (c + 1) * LANES] for c in range(own_tiles))
            x = jnp.sum(x, axis=0, keepdims=True)
            flat.append(x + pltpu.roll(x, LANES // 2, axis=1))
        lane1 = lax.broadcasted_iota(jnp.int32, (1, LANES), 1)
        part[...] = jnp.where(lane1 < LANES // 2, flat[0], flat[1])

    with jax.named_scope("meet"):
        pl.semaphore_wait(barrier, everyone - 1)

    def tell(s, carry):
        summary(s).start()
        return carry

    lax.fori_loop(1, everyone, tell, 0)

    def taps(src, c, start, count):
        x = [src[c, pl.ds(start + a, count, stride=2), :] for a in range(-2, 3)]
        return 0.375 * x[2] + (0.25 * (x[1] + x[3]) + 0.0625 * (x[0] + x[4]))

    def hold(x, c, p, first):
        if first:
            ok = jnp.logical_or(line8 >= 4, up)
        else:
            ok = jnp.logical_or(line8 < 4, down)
        x[c, p : p + 8, :] = jnp.where(ok, x[c, p : p + 8, :], 0.0)

    last1, last2 = nr // 2 + 8, nr // 4 + 8

    def ends1(x, c):
        hold(x, c, 8, True)
        hold(x, c, last1, False)

    def ends2(x, c):
        hold(x, c, 8, True)
        hold(x, c, last2, False)

    def rows1(src, dst, c, p, count):
        dst[c, p : p + count, :] = taps(src, c, 2 * p - 8, count)

    def rows2(src, dst, c, p, count):
        dst[c, p : p + count, :] = taps(src, c, 2 * p - 12, count)

    with jax.named_scope("rowpyr"):
        for src, one, two, three in ((num, n1, n2, n3), (den, d1, d2, d3)):
            for c in range(own_tiles):
                rows1(src, one, c, 8, nr // 2 + 16)
                ends1(one, c)
                rows2(one, two, c, 8, nr // 4 + 8)
                ends2(two, c)
                three[c] = taps(two, c, 4, m3)

    def wide_of(x, rows, tiles):
        return jnp.concatenate([x[c, rows, :] for c in tiles], axis=1)

    own_range = range(own_tiles)
    size1, size2 = x1.shape[2], x2.shape[2]
    s3, s4, s5, s6 = (nr // 8 + 8, nr // 16 + 8, nr // 32 + 8, nr // 64 + 16)
    stack = s3 + s4 + s5 + s6
    tops = (0, s3, s3 + s4, s3 + s4 + s5)
    bottoms = tuple(top + (nr >> level) for top, level in zip(tops, (3, 4, 5, 6)))

    def level_of(shape, dim, cuts):
        index = lax.broadcasted_iota(jnp.int32, shape, dim)
        return sum((index >= cut).astype(jnp.int32) for cut in cuts)

    c3, c4, c5 = nc // 8 + 8, nc // 16 + 8, nc // 32 + 8
    lane_cuts = (c3, c3 + c4, c3 + c4 + c5)
    middle = jnp.logical_and(line8 >= MIDDLE[0], line8 <= MIDDLE[-1])

    def pack(n, d):
        return jnp.where(middle, n, pltpu.roll(d, 4, axis=0))

    def unpack(x):
        return jnp.where(middle, x, 0.0), jnp.where(middle, pltpu.roll(x, 4, axis=0), 0.0)

    def unpack_lanes(x):
        low = lax.broadcasted_iota(jnp.int32, x.shape, 1) < LANES // 2
        return jnp.where(low, x, 0.0), jnp.where(low, pltpu.roll(x, LANES // 2, axis=1), 0.0)

    with jax.named_scope("p3"):
        fetch["c03"].wait()
        fetch["rall"].wait()
        x = jnp.concatenate([wide_of(n3, slice(None), own_range), wide_of(d3, slice(None), own_range)], axis=0)
        x = right(x, tab["c03"][...])
        x = x[:, :LANES] + x[:, LANES:]
        high, low = split(jnp.concatenate([x[:m3], x[m3:]], axis=1))
        rall = tab["rall"][...]
        x = dot(rall, high) + dot(rall, low)
        x = jnp.concatenate([x[: stack - s6], x[stack - s6 : stack] + x[stack : stack + s6]], axis=0)
        fetch["call"].wait()
        high, low = split(jnp.concatenate([x[:, :LANES], x[:, LANES:]], axis=0))
        x = dot(high, tab["call"][0]) + dot(low, tab["call"][0]) + dot(high, tab["call"][1])

    base_g = size1 + size2

    with jax.named_scope("g_pack"):
        for c in range(2):
            index = lane8 + c * LANES
            for k in range(1 + ns):
                piece = [x[a * stack : (a + 1) * stack, k * 256 + c * LANES : k * 256 + (c + 1) * LANES] for a in (0, 1)]
                for a in range(2):
                    if k == 0:
                        g[a, c] = piece[a]
                    else:
                        side_s[k - 1, base_g + (2 * a + c) * stack : base_g + (2 * a + c + 1) * stack, :] = piece[a]
                for rp, firsts in ((1, bottoms), (2, tops)):
                    line = []
                    for a in range(2):
                        b = [piece[a][f : f + 8] for f in firsts]
                        line.append(
                            jnp.where(
                                index < lane_cuts[0], b[0],
                                jnp.where(index < lane_cuts[1], b[1], jnp.where(index < lane_cuts[2], b[2], b[3])),
                            )
                        )
                    edge_s[rp - 1, k, (5 if k == 0 else 2) + c] = pack(*line)

    body1, body2 = slice(8, 8 + size1), slice(8, 8 + size2)

    with jax.named_scope("x_side"):
        fetch["s1"].wait()
        fetch["s2"].wait()
        for k in range(1, 1 + ns):
            for base, n, d, body, name, at in (
                (0, n1, d1, body1, "s1", nr // 2), (size1, n2, d2, body2, "s2", nr // 4),
            ):
                x = right(n[near_tile[k], body, :], tab[name][k - 1, 0])
                x = x + right(d[near_tile[k], body, :], tab[name][k - 1, 1])
                side_s[k - 1, base : base + x.shape[0], :] = x
                edge_s[0, k, 0 if base == 0 else 1] = x[at : at + 8]
                edge_s[1, k, 0 if base == 0 else 1] = x[0:8]

    with jax.named_scope("x_own"):
        for n, d, body, name, dst, at, first in (
            (n1, d1, body1, "c1", x1, nr // 2, 0), (n2, d2, body2, "c2", x2, nr // 4, 3),
        ):
            fetch[name].wait()
            both = [right(wide_of(x, body, own_range), tab[name][...]) for x in (n, d)]
            for c in range(dst.shape[1]):
                both_c = [x[:, c * LANES : (c + 1) * LANES] for x in both]
                for a in range(2):
                    dst[a, c] = both_c[a]
                edge_s[0, 0, first + c] = pack(*(x[at : at + 8] for x in both_c))
                edge_s[1, 0, first + c] = pack(*(x[0:8] for x in both_c))

    with jax.named_scope("send"):
        send_edges(lambda d: d[0] != 0)
        send_edges(lambda d: d[0] == 0)

    def ratio(n, d):
        return jnp.where(d > 0, n / d, 0.0)

    def await_edges(wanted):
        for i, d in enumerate(kinds):
            if wanted(d):
                given(sends(*d), lambda: edge(i).wait_send())
                given(comes(*d), lambda: edge(i).wait_recv())

    def q_rows(x, y, rows, gain):
        for c in range(x.shape[1]):
            y[rows, c * LANES : (c + 1) * LANES] = gain * ratio(x[0, c, rows, :], x[1, c, rows, :])

    gain1, gain2 = gain_ref[1] - gain_ref[0], gain_ref[2] - gain_ref[1]

    with jax.named_scope("w_side"):
        await_edges(lambda d: d[0] == 0)
    with jax.named_scope("add_side"):
        for k in range(1, 1 + ns):
            def add():
                for base, size, x, into in ((0, size1, x1, into1[k]), (size1, size2, x2, into2[k])):
                    more = unpack_lanes(side_r[k - 1, base : base + size, :])
                    for a in range(2):
                        x[a, into] = x[a, into] + more[a]
                for a in range(2):
                    for c in range(2):
                        base = base_g + (2 * a + c) * stack
                        g[a, c] = g[a, c] + side_r[k - 1, base : base + stack, :]

            given(recv_col[k], add)
    with jax.named_scope("q"):
        q_rows(x1, y1, slice(0, size1), gain1)
        q_rows(x2, y2, slice(0, size2), gain2)

    with jax.named_scope("w_edges"):
        await_edges(lambda d: d[0] != 0)
        for name in ("ec", "e2", "e1", "e0", "er", "second"):
            fetch[name].wait()
    with jax.named_scope("edges"):
        for rp, at1, at2, firsts in ((1, 0, 0, tops), (2, nr // 2, nr // 4, bottoms)):
            for cp in range(1 + ns):

                def add():
                    if cp == 0:
                        for first, x, at in ((0, x1, at1), (3, x2, at2)):
                            for c in range(x.shape[1]):
                                for a, more in enumerate(unpack(edge_r[rp - 1, 0, first + c])):
                                    x[a, c, at : at + 8, :] = x[a, c, at : at + 8, :] + more
                    else:
                        for first, x, at, into in ((0, x1, at1, into1[cp]), (1, x2, at2, into2[cp])):
                            for a, more in enumerate(unpack_lanes(edge_r[rp - 1, cp, first])):
                                x[a, into, at : at + 8, :] = x[a, into, at : at + 8, :] + more
                    for c in range(2):
                        for a, more in enumerate(unpack(edge_r[rp - 1, cp, (5 if cp == 0 else 2) + c])):
                            for f in firsts:
                                g[a, c, f : f + 8, :] = g[a, c, f : f + 8, :] + more

                given(comes(rp, cp), add)
        for x, y, at, gain in ((x1, y1, nr // 2, gain1), (x2, y2, nr // 4, gain2)):
            q_rows(x, y, slice(0, 8), gain)
            q_rows(x, y, slice(at, at + 8), gain)

    with jax.named_scope("deep"):
        shape = (stack, 256)
        at_row = level_of(shape, 0, tops[1:])
        at_col = level_of(shape, 1, lane_cuts)
        gains = [gain_ref[level] - gain_ref[level - 1] for level in (3, 4, 5)] + [-gain_ref[5]]
        factor = jnp.where(
            at_row == 0, gains[0], jnp.where(at_row == 1, gains[1], jnp.where(at_row == 2, gains[2], gains[3]))
        )
        n, d = (jnp.concatenate([g[a, 0], g[a, 1]], axis=1) for a in range(2))
        x = jnp.where(jnp.logical_and(at_row == at_col, d > 0), factor * (n / d), 0.0)
        high, low = split(x)
        er = tab["er"]
        x = dot(er[0], high) + dot(er[0], low) + dot(er[1], high)
        high, low = split(x)
        ec = tab["ec"]
        z3 = dot(high, ec[0]) + dot(low, ec[0]) + dot(high, ec[1])

    with jax.named_scope("z2"):
        z3b[0:m3, :] = z3

        def grow_rows(src, dst, put, get, count):
            x, y, w = (src[get + (slice(k, k + count), slice(None))] for k in (1, 2, 3))
            dst[put + (pl.ds(0, count, stride=2), slice(None))] = 0.125 * (x + w) + 0.75 * y
            dst[put + (pl.ds(1, count, stride=2), slice(None))] = 0.5 * (y + w)

        def block(x, put, p, first):
            ok = jnp.logical_or(line8 >= 4, up) if first else jnp.logical_or(line8 < 4, down)
            x[put + (slice(p, p + 8), slice(None))] = jnp.where(ok, x[put + (slice(p, p + 8), slice(None))], 0.0)

        grow_rows(z3b, z2b, (0,), (), nr // 8 + 8)
        block(z2b, (0,), 0, True)
        block(z2b, (0,), nr // 4, False)
        z2 = right(z2b[0], tab["e2"][...]) + y2[...]
        tiles2 = z2.shape[1] // LANES
        for c in range(tiles2):
            z2b[c] = z2[:, c * LANES : (c + 1) * LANES]
    with jax.named_scope("z1"):
        for c in range(tiles2):
            grow_rows(z2b, z1b, (c,), (c,), nr // 4 + 8)
            block(z1b, (c,), 0, True)
            block(z1b, (c,), nr // 2, False)
        z1 = right(wide_of(z1b, slice(None), range(tiles2)), tab["e1"][...]) + y1[...]
    with jax.named_scope("e0"):
        full = right(z1, tab["e0"][...])

    with jax.named_scope("w_top"):
        def hear(s, carry):
            summary(s).wait()
            return carry

        lax.fori_loop(1, everyone, hear, 0)
    with jax.named_scope("top"):
        total = part[...] + jnp.sum(slots[...], axis=0)
        top_sum = jnp.sum(jnp.where(lane1 < LANES // 2, total, 0.0), axis=1, keepdims=True)
        top_weight = jnp.sum(jnp.where(lane1 < LANES // 2, 0.0, total), axis=1, keepdims=True)
        top_line = (top_sum / top_weight) * tab["line"][1:2, :]
        for c in own_range:
            cols = slice(c * LANES, (c + 1) * LANES)
            wide[c] = full[:, cols] + tab["second"][...] * top_line[:, cols]
    with jax.named_scope("out"):
        gain = gain_ref[0]
        chunk = 32
        for c in own_range:
            for m in range(0, nr // 2, chunk):
                x, y, w = (wide[c, pl.ds(m + k, chunk), :] for k in (3, 4, 5))
                even, odd = pl.ds(2 * m, chunk, stride=2), pl.ds(2 * m + 1, chunk, stride=2)
                q0[c, even, :] = gain * q0[c, even, :] + (0.125 * (x + w) + 0.75 * y)
                q0[c, odd, :] = gain * q0[c, odd, :] + 0.5 * (y + w)
                out_ref[pl.ds(2 * m, 2 * chunk), c * LANES : (c + 1) * LANES] = q0[c, pl.ds(2 * m, 2 * chunk), :]


def local(mesh_shape, heights, scene_ids, scene_offset, scene_weight, band_gain):
    nx, ny, nz = mesh_shape
    nr, nc = heights.shape
    ns = 1 if nx == 2 else 2
    made = tables(nr, nc, nx, ny * nz)
    given = [made[k] for k in COLS + ROWS]
    sizes = (nr, nc, nx, ny, nz, ns)
    ext = (nr + 2 * HALO, nc)
    tiles = nc // LANES
    own_tiles = tiles
    m3 = nr // 8 + 8
    size1, size2, stack = nr // 2 + 16, nr // 4 + 16, nr // 8 + nr // 16 + nr // 32 + nr // 64 + 40
    tiles1, tiles2 = nc // 2 // LANES + 1, nc // 4 // LANES + 1
    beside = size1 + size2 + 4 * stack
    peers = nx * ny * nz - 1
    messages = 3 * (1 + ns) - 1
    hbm = pl.BlockSpec(memory_space=pltpu.HBM)
    return pl.pallas_call(
        functools.partial(kernel, sizes),
        out_shape=pltpu.VMEM((nr, nc), F32),
        in_specs=[hbm] * (5 + len(given)),
        out_specs=pl.BlockSpec(memory_space=pltpu.VMEM),
        scratch_shapes=[pltpu.VMEM(x.shape[1:], x.dtype) for x in given]
        + [
            pltpu.SMEM(scene_offset.shape, F32),
            pltpu.SMEM(scene_weight.shape, F32),
            pltpu.SMEM(band_gain.shape, F32),
            pltpu.VMEM(ext, F32),
            pltpu.VMEM(ext, jnp.int32),
            pltpu.VMEM((own_tiles, nr, LANES), F32),
        ]
        + [pltpu.VMEM((tiles, nr + 3 * HALO, LANES), F32)] * 2
        + [pltpu.VMEM((tiles, nr // 2 + 32, LANES), F32)] * 2
        + [pltpu.VMEM((tiles, nr // 4 + 24, LANES), F32)] * 2
        + [pltpu.VMEM((own_tiles, m3, LANES), F32)] * 2
        + [
            pltpu.VMEM((2, tiles1, size1, LANES), F32),
            pltpu.VMEM((2, tiles2, size2, LANES), F32),
            pltpu.VMEM((2, 2, stack, LANES), F32),
            pltpu.VMEM((size1, tiles1 * LANES), F32),
            pltpu.VMEM((size2, tiles2 * LANES), F32),
            pltpu.VMEM((ns, beside, LANES), F32),
            pltpu.VMEM((ns, beside, LANES), F32),
            pltpu.VMEM((2, 1 + ns, 7, 8, LANES), F32),
            pltpu.VMEM((2, 1 + ns, 7, 8, LANES), F32),
            pltpu.VMEM((m3 + 8, LANES), F32),
            pltpu.VMEM((tiles2, nr // 4 + 16, LANES), F32),
            pltpu.VMEM((tiles2, nr // 2 + 16, LANES), F32),
            pltpu.VMEM((own_tiles, nr // 2 + 16, LANES), F32),
            pltpu.VMEM((1, LANES), F32),
            pltpu.VMEM((peers, 1, LANES), F32),
            pltpu.SemaphoreType.DMA((2 * CHUNKS + 3,)),
            pltpu.SemaphoreType.DMA((len(given),)),
            pltpu.SemaphoreType.DMA((messages,)),
            pltpu.SemaphoreType.DMA((messages,)),
            pltpu.SemaphoreType.DMA((peers,)),
            pltpu.SemaphoreType.DMA((peers,)),
        ],
        compiler_params=pltpu.CompilerParams(collective_id=0, has_side_effects=True),
    )(scene_offset, scene_weight, band_gain, heights, scene_ids, *given)


def solution(mesh):
    placed = (P(("gy", "gz"), "gx"), P(("gy", "gz"), "gx"), P(), P(), P())
    shape = tuple(mesh.shape[name] for name in ("gx", "gy", "gz"))
    return jax.shard_map(
        functools.partial(local, shape), mesh=mesh, in_specs=placed,
        out_specs=P(("gy", "gz"), "gx"), check_vma=False,
    )
```

```python
import functools

import jax
import jax.numpy as jnp
import numpy as np
from jax import lax
from jax.experimental import pallas as pl
from jax.experimental.pallas import tpu as pltpu
from jax.sharding import PartitionSpec as P

F32, BF16 = jnp.float32, jnp.bfloat16
FAR = 1 << 20
HALO = 16
LANES = 128
LEVELS = 6
MIDDLE = (3, 4, 5)


def reach(count, levels):
    weights = np.ones(count >> levels, np.float64)
    for _ in range(levels):
        fine = np.zeros(2 * weights.size + 4, np.float64)
        for tap, value in zip(range(-2, 3), (0.0625, 0.25, 0.375, 0.25, 0.0625)):
            fine[2 + tap : 2 + tap + 2 * weights.size : 2] += value * weights
        weights = fine[2:-2]
    return weights


class Axis:
    def __init__(self, n, at, count):
        self.n, self.at, self.count = n, at, count

    def inside(self, index, level):
        place = index + self.at * (self.n >> level)
        return (place >= 0) & (place < self.count * (self.n >> level))

    def shrink(self, fine, coarse, level):
        far = np.abs(fine[:, None] - 2 * coarse[None, :])
        value = np.select([far == 0, far == 1, far == 2], [0.375, 0.25, 0.0625], 0.0)
        return value * self.inside(coarse, level)[None, :]

    def grow(self, coarse, fine, level):
        far = np.abs(2 * coarse[:, None] - fine[None, :])
        value = np.select([far == 0, far == 1, far == 2], [0.75, 0.5, 0.125], 0.0)
        return value * self.inside(fine, level)[None, :]

    def window(self, level, edge):
        return np.arange(-edge, (self.n >> level) + edge)

    def deep(self, lanes, shift=0):
        out = [x + shift * (self.n >> level) for level, x in zip((3, 4, 5, 6), self.out())]
        w4, w5 = self.window(4, 30), self.window(5, 14)
        to4 = self.shrink(lanes, w4, 4)
        to5 = to4 @ self.shrink(w4, w5, 5)
        same = (lanes[:, None] == out[0][None, :]) * self.inside(out[0], 3)[None, :]
        parts = [
            same * 1.0,
            self.shrink(lanes, out[1], 4),
            to4 @ self.shrink(w4, out[2], 5),
            to5 @ self.shrink(w5, out[3], 6),
        ]
        return np.concatenate(parts, axis=1) * self.inside(lanes, 3)[:, None]

    def out(self):
        low = -4
        return [low + np.arange(size) for size in self.sizes()]

    def sizes(self):
        return [self.n // 8 + 8, self.n // 16 + 8, self.n // 32 + 8, self.n // 64 + 16]

    def back(self):
        o3, o4, o5, o6 = self.out()
        w4, w5 = self.window(4, 4), self.window(5, 4)
        from4 = self.grow(w4, o3, 3)
        from5 = self.grow(w5, w4, 4) @ from4
        parts = [
            np.eye(o3.size) * self.inside(o3, 3)[None, :],
            self.grow(o4, o3, 3),
            self.grow(o5, w4, 4) @ from4,
            self.grow(o6, w5, 5) @ from5,
        ]
        return np.concatenate(parts, axis=0)

    def sums(self):
        return reach(self.count * self.n, LEVELS)[self.at * self.n : (self.at + 1) * self.n]

    def ones(self, level):
        x = self.inside(self.window(6, 4), 6) * 1.0
        for k in range(5, level - 1, -1):
            x = x @ self.grow(self.window(k + 1, 4), self.window(k, 4), k)
        return x


def pad(x, shape):
    return np.pad(x, [(0, size - have) for size, have in zip(shape, x.shape)])


def halves(x):
    high = x.astype(np.float32).astype(jnp.bfloat16)
    low = (x - high.astype(np.float64)).astype(np.float32).astype(jnp.bfloat16)
    return high, low


def spaced(n):
    size = -(-(n + 8) // LANES) * LANES
    return np.concatenate([np.arange(-4, n + 4), np.full(size - n - 8, FAR)])


def col_tables(n, at, count):
    ax = Axis(n, at, count)
    shifts = [1 if at == 0 else -1] if count == 2 else [1, -1]
    lane = np.arange(LANES)
    own = np.arange(n)
    out1, out2 = spaced(n // 2), spaced(n // 4)
    w1, w2 = ax.window(1, 16), ax.window(2, 8)
    middle = np.isin(lane, MIDDLE)[None, :]
    s1, s2 = [], []
    for d in shifts:
        near = n - LANES + lane if d > 0 else lane
        over1, over2 = (lane - 4 + (n >> level if d > 0 else 0) for level in (1, 2))
        s1.append(ax.shrink(near, over1, 1) * middle)
        s2.append(ax.shrink(near, w1, 1) @ ax.shrink(w1, over2, 2) * middle)
    s1, s2 = (np.stack([np.stack([x, np.roll(x, LANES // 2, 1)]) for x in y]) for y in (s1, s2))
    o3 = ax.out()[0]
    to2 = ax.shrink(own, w1, 1)
    c03 = to2 @ ax.shrink(w1, w2, 2) @ ax.shrink(w2, o3, 3)
    c03 = np.concatenate([pad(x.astype(np.float64), (n, LANES)) for x in halves(c03)], axis=1)
    three = np.concatenate([o3, np.full(LANES - o3.size, FAR)])
    call = []
    for d in [0] + shifts:
        call.append([pad(x.astype(np.float64), (LANES, 256)) for x in halves(ax.deep(three, d))])
    call = np.stack([np.concatenate([x[k] for x in call], axis=1) for k in range(2)])
    back = ax.back()
    ec = np.stack([pad(x.astype(np.float64), (256, LANES)) for x in halves(back)])
    return dict(
        c1=ax.shrink(own, out1, 1), c2=to2 @ ax.shrink(w1, out2, 2), s1=s1, s2=s2, c03=c03, call=call,
        ec=ec, e2=ax.grow(three, out2, 2), e1=ax.grow(out2, out1, 1), e0=ax.grow(out1, own, 0),
    ), dict(line=np.stack([ax.sums(), ax.ones(0)[4:-4]]))


def row_tables(n, at, count):
    ax = Axis(n, at, count)
    o3 = ax.out()[0]
    deep = ax.deep(o3).T
    high, low = (x.astype(np.float64) for x in halves(deep))
    size6 = ax.sizes()[3]
    rall = np.concatenate([high, low[-size6:]], axis=0)
    rall = pad(rall, (-(-rall.shape[0] // 16) * 16, o3.size))
    back = ax.back()
    er = np.stack([x.astype(np.float64) for x in halves(back.T)])
    first = np.repeat(ax.sums()[:, None], LANES, 1)
    second = np.repeat(pad(ax.ones(1), (n // 2 + 16,))[:, None], LANES, 1)
    return dict(rall=rall, er=er), dict(first=first, second=second)


def tables(nr, nc, nx, blocks):
    def places(count):
        return (0, 1) if count == 2 else (0, 1, count - 1)

    cols = [col_tables(nc, at, nx) for at in places(nx)]
    rows = [row_tables(nr, at, blocks) for at in places(blocks)]

    def cast(x):
        return jnp.asarray(np.asarray(x, np.float32)).astype(BF16)

    def keep(x):
        return jnp.asarray(np.asarray(x, np.float32))

    out = {}
    for some in (cols, rows):
        for k in some[0][0]:
            out[k] = cast(np.stack([x[0][k] for x in some]))
        for k in some[0][1]:
            out[k] = keep(np.stack([x[1][k] for x in some]))
    return out


def merge(made):
    arrays, places = [], {}
    for at, group in enumerate(COLS + ROWS):
        lanes = max(made[name].shape[-1] for name in group)
        parts, start = [], 0
        for name in group:
            x = made[name]
            rows, width = x.shape[-2:]
            x = x.reshape(x.shape[0], -1, rows, width)
            tall = -(-rows // 16) * 16 if len(group) > 1 else rows
            x = jnp.pad(x, ((0, 0), (0, 0), (0, tall - rows), (0, lanes - width)))
            places[name] = (at, start, tall, rows, width)
            start += x.shape[1] * tall
            parts.append(x.reshape(x.shape[0], -1, lanes))
        arrays.append(jnp.concatenate(parts, axis=1))
    return arrays, places


def split(x):
    high = x.astype(BF16)
    return high, (x - high.astype(F32)).astype(BF16)


def dot(a, b):
    return jnp.dot(a, b, preferred_element_type=F32)


def right(x, c):
    high, low = split(x)
    return dot(high, c) + dot(low, c)


COLS = (("call", "e0"), ("c03", "c2", "e2"), ("c1", "e1"), ("s1", "s2", "ec"), ("line",))
ROWS = (("rall", "er"), ("first",), ("second",))
OWN_TILES, SIDE_TILES = 5, 2
CHUNKS = 4


def kernel(
    sizes, places, off_hbm, wgt_hbm, gain_hbm, h_ref, s_ref, *rest
):
    nr, nc, nx, ny, nz, ns = sizes
    count = len(COLS) + len(ROWS)
    tables_hbm, rest = rest[:count], rest[count:]
    out_ref, rest = rest[0], rest[1:]
    tab, rest = rest[:count], rest[count:]
    (
        off_ref, wgt_ref, gain_ref, h_buf, s_buf, q0, num, den, n1, d1, n2, d2, n3, d3,
        x1, x2, g, y1, y2, side_s, side_r, edge_s, edge_r, z3b, z2b, z1b, wide, part, slots,
        own_sem, tab_sem, send0, recv0, psend, precv,
    ) = rest
    cx, cy, cz = lax.axis_index("gx"), lax.axis_index("gy"), lax.axis_index("gz")
    row = cy * nz + cz
    blocks = ny * nz
    own_tiles = nc // LANES
    t3 = nr // 8
    m3 = t3 + 8

    def kind(at, count):
        return at if count == 2 else jnp.where(at == 0, 0, jnp.where(at == count - 1, 2, 1))

    ct, rt = kind(cx, nx), kind(row, blocks)

    loads = []
    step = nr // CHUNKS
    for k in range(CHUNKS):
        rows = pl.ds(k * step, step)
        for a, (src, dst) in enumerate(((h_ref, h_buf), (s_ref, s_buf))):
            loads.append(
                pltpu.make_async_copy(
                    src.at[rows, :],
                    dst.at[pl.ds(HALO + k * step, step), pl.ds(0, nc)],
                    own_sem.at[k],
                )
            )
    small = [
        pltpu.make_async_copy(src, dst, own_sem.at[CHUNKS + a])
        for a, (src, dst) in enumerate(((off_hbm, off_ref), (wgt_hbm, wgt_ref), (gain_hbm, gain_ref)))
    ]
    fetch = [
        pltpu.make_async_copy(src.at[ct if i < len(COLS) else rt], tab[i], tab_sem.at[i])
        for i, src in enumerate(tables_hbm)
    ]
    early = (places["line"][0], places["first"][0])
    ready = set()

    def await_tables(*names):
        for name in names:
            if places[name][0] not in ready:
                ready.add(places[name][0])
                fetch[places[name][0]].wait()

    def table(name, k=0, rows=None):
        at, start, tall, height, width = places[name]
        first, last = rows or (0, height)
        return tab[at][start + k * tall + first : start + k * tall + last, :width]

    for copy in loads[:2] + small + [fetch[i] for i in early] + loads[2:]:
        copy.start()

    up, down = row > 0, row < blocks - 1
    send_row, recv_row = {0: None, 1: down, 2: up}, {0: None, 1: up, 2: down}
    if ns == 1:
        send_col, recv_col = {0: None, 1: None}, {0: None, 1: None}
        to_col = {0: cx, 1: 1 - cx}
        near_tile = {1: (1 - cx) * (own_tiles - 1)}
        into1, into2 = {1: (1 - cx) * (x1.shape[1] - 1)}, {1: (1 - cx) * (x2.shape[1] - 1)}
    else:
        send_col = {0: None, 1: cx < nx - 1, 2: cx > 0}
        recv_col = {0: None, 1: cx > 0, 2: cx < nx - 1}
        to_col = {0: cx, 1: cx + 1, 2: cx - 1}
        near_tile = {1: own_tiles - 1, 2: 0}
        into1, into2 = {1: 0, 2: x1.shape[1] - 1}, {1: 0, 2: x2.shape[1] - 1}
    kinds = [(rp, cp) for rp in (0, 1, 2) for cp in range(1 + ns) if rp or cp]

    def device(rp, cp):
        target = row + {0: 0, 1: 1, 2: -1}[rp]
        return {"gx": to_col[cp], "gy": target // nz, "gz": target % nz}

    def also(a, b):
        return b if a is None else a if b is None else jnp.logical_and(a, b)

    def sends(rp, cp):
        return also(send_row[rp], send_col[cp])

    def comes(rp, cp):
        return also(recv_row[rp], recv_col[cp])

    def given(flag, body):
        if flag is None:
            body()
        else:
            pl.when(flag)(body)

    everyone = nx * blocks
    me = row * nx + cx

    def peer(s):
        other = (me + s) % everyone
        line = other // nx
        return {"gx": other % nx, "gy": line // nz, "gz": line % nz}

    barrier = pltpu.get_barrier_semaphore()

    def greet(s, carry):
        pl.semaphore_signal(barrier, inc=1, device_id=peer(s))
        return carry

    lax.fori_loop(1, everyone, greet, 0)

    for i, copy in enumerate(fetch):
        if i not in early:
            copy.start()

    zero = jnp.zeros((HALO, LANES), F32)
    for x in (num, den):
        for c in range(own_tiles):
            x[c, 0:HALO, :] = zero
            x[c, nr + HALO : nr + 2 * HALO, :] = zero
            x[c, nr + 2 * HALO :, :] = zero
    zero = jnp.zeros((8, LANES), F32)
    for x in (n1, d1, n2, d2):
        for c in range(own_tiles):
            x[c, 0:8, :] = zero
            x[c, x.shape[1] - 8 :, :] = zero
    z3b[m3:, :] = zero

    def edge(i):
        rp, cp = kinds[i]
        if rp == 0:
            src, dst = side_s.at[cp - 1], side_r.at[cp - 1]
        else:
            place = pl.ds(0, OWN_TILES) if cp == 0 else pl.ds(0, SIDE_TILES)
            src, dst = edge_s.at[rp - 1, cp, place], edge_r.at[rp - 1, cp, place]
        return pltpu.make_async_remote_copy(
            src_ref=src, dst_ref=dst, send_sem=send0.at[i], recv_sem=recv0.at[i], device_id=device(rp, cp)
        )

    lane8 = lax.broadcasted_iota(jnp.int32, (8, LANES), 1)
    line8 = lax.broadcasted_iota(jnp.int32, (8, LANES), 0)

    def spread(table):
        line = jnp.zeros((8, LANES), F32)
        for i in range(table.shape[0]):
            line = jnp.where(lane8 == i, table[i], line)
        return line

    for copy in small:
        copy.wait()
    wgt_row = spread(wgt_ref)

    def tree(ids, table):
        values = [table[i] for i in range(table.shape[0])]
        bit = 1
        while len(values) > 1:
            mask = (ids & bit) != 0
            values = [jnp.where(mask, values[i + 1], values[i]) for i in range(0, len(values), 2)]
            bit *= 2
        return values[0]

    def level0(base, count, c):
        rows = pl.ds(base, count)
        ids = s_buf[rows, c * LANES : (c + 1) * LANES]
        weight = jnp.concatenate(
            [jnp.take_along_axis(wgt_row, ids[r : r + 8], axis=1) for r in range(0, count, 8)], axis=0
        )
        moved = h_buf[rows, c * LANES : (c + 1) * LANES] + tree(ids, off_ref)
        numer = weight * moved
        num[c, rows, :] = numer
        den[c, rows, :] = weight
        return moved, numer, weight

    def summary(s):
        return pltpu.make_async_remote_copy(
            src_ref=part,
            dst_ref=slots.at[s - 1],
            send_sem=psend,
            recv_sem=precv,
            device_id=peer(s),
        )

    def send_edges(wanted):
        for i, d in enumerate(kinds):
            if wanted(d):
                given(sends(*d), lambda: edge(i).start())

    with jax.named_scope("level0"):
        await_tables("line", "first")
        line = table("line")
        sums = [[0.0] * own_tiles, [0.0] * own_tiles]
        for k in range(CHUNKS):
            both = pl.ds(0, 2 * step)
            pltpu.make_async_copy(h_ref.at[both, :], h_buf.at[both, pl.ds(0, nc)], own_sem.at[k]).wait()
            weights = table("first", 0, (k * step, (k + 1) * step))
            for c in range(own_tiles):
                moved, numer, weight = level0(HALO + k * step, step, c)
                q0[c, k * step : (k + 1) * step, :] = moved
                for a, x in enumerate((numer, weight)):
                    x = (x * weights).reshape(step // 8, 8, LANES)
                    sums[a][c] = sums[a][c] + jnp.sum(x, axis=0)
        flat = []
        for a in range(2):
            x = sum(sums[a][c] * line[0:1, c * LANES : (c + 1) * LANES] for c in range(own_tiles))
            x = jnp.sum(x, axis=0, keepdims=True)
            flat.append(x + pltpu.roll(x, LANES // 2, axis=1))
        lane1 = lax.broadcasted_iota(jnp.int32, (1, LANES), 1)
        part[...] = jnp.where(lane1 < LANES // 2, flat[0], flat[1])

    def meet():
        with jax.named_scope("meet"):
            pl.semaphore_wait(barrier, everyone - 1)

        def tell(s, carry):
            summary(s).start()
            return carry

        lax.fori_loop(1, everyone, tell, 0)

    def taps(src, c, start, count):
        x = [src[c, pl.ds(start + a, count, stride=2), :] for a in range(-2, 3)]
        return 0.375 * x[2] + (0.25 * (x[1] + x[3]) + 0.0625 * (x[0] + x[4]))

    def hold(x, c, p, first):
        if first:
            ok = jnp.logical_or(line8 >= 4, up)
        else:
            ok = jnp.logical_or(line8 < 4, down)
        x[c, p : p + 8, :] = jnp.where(ok, x[c, p : p + 8, :], 0.0)

    last1, last2 = nr // 2 + 8, nr // 4 + 8

    def ends1(x, c):
        hold(x, c, 8, True)
        hold(x, c, last1, False)

    def ends2(x, c):
        hold(x, c, 8, True)
        hold(x, c, last2, False)

    def rows1(src, dst, c, p, count):
        dst[c, p : p + count, :] = taps(src, c, 2 * p - 8, count)

    def rows2(src, dst, c, p, count):
        dst[c, p : p + count, :] = taps(src, c, 2 * p - 12, count)

    with jax.named_scope("rowpyr"):
        for src, one, two, three in ((num, n1, n2, n3), (den, d1, d2, d3)):
            for c in range(own_tiles):
                rows1(src, one, c, 8, nr // 2 + 16)
                ends1(one, c)
                rows2(one, two, c, 8, nr // 4 + 8)
                ends2(two, c)
                three[c] = taps(two, c, 4, m3)

    meet()
    def wide_of(x, rows, tiles):
        return jnp.concatenate([x[c, rows, :] for c in tiles], axis=1)

    own_range = range(own_tiles)
    size1, size2 = x1.shape[2], x2.shape[2]
    s3, s4, s5, s6 = (nr // 8 + 8, nr // 16 + 8, nr // 32 + 8, nr // 64 + 16)
    stack = s3 + s4 + s5 + s6
    tops = (0, s3, s3 + s4, s3 + s4 + s5)
    bottoms = tuple(top + (nr >> level) for top, level in zip(tops, (3, 4, 5, 6)))

    def level_of(shape, dim, cuts):
        index = lax.broadcasted_iota(jnp.int32, shape, dim)
        return sum((index >= cut).astype(jnp.int32) for cut in cuts)

    c3, c4, c5 = nc // 8 + 8, nc // 16 + 8, nc // 32 + 8
    lane_cuts = (c3, c3 + c4, c3 + c4 + c5)
    middle = jnp.logical_and(line8 >= MIDDLE[0], line8 <= MIDDLE[-1])

    def pack(n, d):
        return jnp.where(middle, n, pltpu.roll(d, 4, axis=0))

    def unpack(x):
        return jnp.where(middle, x, 0.0), jnp.where(middle, pltpu.roll(x, 4, axis=0), 0.0)

    def unpack_lanes(x):
        low = lax.broadcasted_iota(jnp.int32, x.shape, 1) < LANES // 2
        return jnp.where(low, x, 0.0), jnp.where(low, pltpu.roll(x, LANES // 2, axis=1), 0.0)

    with jax.named_scope("p3"):
        await_tables("c03", "rall", "call")
        x = jnp.concatenate([wide_of(n3, slice(None), own_range), wide_of(d3, slice(None), own_range)], axis=0)
        x = right(x, table("c03"))
        x = x[:, :LANES] + x[:, LANES:]
        high, low = split(jnp.concatenate([x[:m3], x[m3:]], axis=1))
        rall = table("rall")
        x = dot(rall, high) + dot(rall, low)
        x = jnp.concatenate([x[: stack - s6], x[stack - s6 : stack] + x[stack : stack + s6]], axis=0)
        high, low = split(jnp.concatenate([x[:, :LANES], x[:, LANES:]], axis=0))
        x = dot(high, table("call", 0)) + dot(low, table("call", 0)) + dot(high, table("call", 1))

    base_g = size1 + size2

    def own_lines(x1_, x2_, g_):
        last = x1_[2] + pltpu.roll(x2_[1], 8, axis=1) + pltpu.roll(g_[1], 16, axis=1)
        return [x1_[0], x1_[1], x2_[0], g_[0], last]

    def ends(x, c, last):
        return jnp.concatenate([x[c, 8:16, :], x[c, last : last + 8, :]], axis=0)

    with jax.named_scope("edge_own"):
        await_tables("s1", "s2", "c1", "c2")

        def own_ends(n, d, last, name):
            y = jnp.concatenate(
                [jnp.concatenate([ends(x, c, last) for c in own_range], axis=1) for x in (n, d)], axis=0
            )
            return right(y, table(name))

        own1, own2 = own_ends(n1, d1, last1, "c1"), own_ends(n2, d2, last2, "c2")

    def tile(x, at, c):
        return x[at : at + 8, c * LANES : (c + 1) * LANES]

    with jax.named_scope("g_pack"):
        for k in range(1 + ns):
            piece = [
                [x[a * stack : (a + 1) * stack, k * 256 + c * LANES : k * 256 + (c + 1) * LANES] for c in (0, 1)]
                for a in (0, 1)
            ]
            for a in range(2):
                for c in range(2):
                    if k == 0:
                        g[a, c] = piece[a][c]
                    else:
                        side_s[k - 1, base_g + (2 * a + c) * stack : base_g + (2 * a + c + 1) * stack, :] = piece[a][c]
            for rp, firsts in ((1, bottoms), (2, tops)):
                deep = []
                for a in range(2):
                    lines = []
                    for c in range(2):
                        index = lane8 + c * LANES
                        b = [piece[a][c][f : f + 8] for f in firsts]
                        lines.append(
                            jnp.where(
                                index < lane_cuts[0], b[0],
                                jnp.where(index < lane_cuts[1], b[1], jnp.where(index < lane_cuts[2], b[2], b[3])),
                            )
                        )
                    deep.append(lines)
                at = 8 * (2 - rp)
                if k == 0:
                    packed = [
                        own_lines(
                            [tile(own1, 16 * a + at, c) for c in range(3)],
                            [tile(own2, 16 * a + at, c) for c in range(2)],
                            deep[a],
                        )
                        for a in range(2)
                    ]
                    for t in range(OWN_TILES):
                        edge_s[rp - 1, 0, t] = pack(packed[0][t], packed[1][t])
                else:
                    lines = []
                    for n, d, last, name in ((n1, d1, last1, "s1"), (n2, d2, last2, "s2")):
                        first = 8 if rp == 2 else last
                        y = right(n[near_tile[k], first : first + 8, :], table(name, 2 * (k - 1) + 0))
                        lines.append(y + right(d[near_tile[k], first : first + 8, :], table(name, 2 * (k - 1) + 1)))
                    edge_s[rp - 1, k, 0] = pack(deep[0][0], deep[1][0])
                    edge_s[rp - 1, k, 1] = (
                        lines[0] + pltpu.roll(lines[1], 8, axis=1)
                        + pltpu.roll(pack(deep[0][1], deep[1][1]), 16, axis=1)
                    )

    with jax.named_scope("send"):
        send_edges(lambda d: d[0] != 0)

    body1, body2 = slice(8, 8 + size1), slice(8, 8 + size2)

    with jax.named_scope("x_side"):
        for k in range(1, 1 + ns):
            for base, n, d, body, name in ((0, n1, d1, body1, "s1"), (size1, n2, d2, body2, "s2")):
                y = right(n[near_tile[k], body, :], table(name, 2 * (k - 1) + 0))
                y = y + right(d[near_tile[k], body, :], table(name, 2 * (k - 1) + 1))
                side_s[k - 1, base : base + y.shape[0], :] = y
        send_edges(lambda d: d[0] == 0)

    with jax.named_scope("x_own"):
        for n, d, body, name, dst in ((n1, d1, body1, "c1", x1), (n2, d2, body2, "c2", x2)):
            for a, y in enumerate((n, d)):
                y = right(wide_of(y, body, own_range), table(name))
                for c in range(dst.shape[1]):
                    dst[a, c] = y[:, c * LANES : (c + 1) * LANES]

    def ratio(n, d):
        return jnp.where(d > 0, n / d, 0.0)

    def await_edges(wanted):
        for i, d in enumerate(kinds):
            if wanted(d):
                given(sends(*d), lambda: edge(i).wait_send())
                given(comes(*d), lambda: edge(i).wait_recv())

    def q_rows(x, y, rows, gain):
        for c in range(x.shape[1]):
            y[rows, c * LANES : (c + 1) * LANES] = gain * ratio(x[0, c, rows, :], x[1, c, rows, :])

    gain1, gain2 = gain_ref[1] - gain_ref[0], gain_ref[2] - gain_ref[1]

    with jax.named_scope("w_side"):
        await_edges(lambda d: d[0] == 0)
    with jax.named_scope("add_side"):
        for k in range(1, 1 + ns):
            def add():
                for base, size, x, into in ((0, size1, x1, into1[k]), (size1, size2, x2, into2[k])):
                    more = unpack_lanes(side_r[k - 1, base : base + size, :])
                    for a in range(2):
                        x[a, into] = x[a, into] + more[a]
                for a in range(2):
                    for c in range(2):
                        base = base_g + (2 * a + c) * stack
                        g[a, c] = g[a, c] + side_r[k - 1, base : base + stack, :]

            given(recv_col[k], add)
    with jax.named_scope("q"):
        q_rows(x1, y1, slice(0, size1), gain1)
        q_rows(x2, y2, slice(0, size2), gain2)

    with jax.named_scope("w_edges"):
        await_edges(lambda d: d[0] != 0)
        await_tables("ec", "e2", "e1", "e0", "er", "second")
    packed_lanes = jnp.logical_and(lane8 % (LANES // 2) >= MIDDLE[0], lane8 % (LANES // 2) <= MIDDLE[-1])
    with jax.named_scope("edges"):
        for rp, at1, at2, firsts in ((1, 0, 0, tops), (2, nr // 2, nr // 4, bottoms)):
            for cp in range(1 + ns):

                def add():
                    got = edge_r.at[rp - 1, cp]
                    tail = unpack(got[OWN_TILES - 1]) if cp == 0 else None
                    if cp == 0:
                        adds1 = [unpack(got[0]), unpack(got[1]), [jnp.where(lane8 < 8, y, 0.0) for y in tail]]
                        adds2 = [
                            unpack(got[2]),
                            [jnp.where(lane8 < 8, pltpu.roll(y, LANES - 8, axis=1), 0.0) for y in tail],
                        ]
                        for x, at, adds in ((x1, at1, adds1), (x2, at2, adds2)):
                            for c, more in enumerate(adds):
                                for a in range(2):
                                    x[a, c, at : at + 8, :] = x[a, c, at : at + 8, :] + more[a]
                        deep = [unpack(got[3]), tail]
                    else:
                        y = got[1]
                        both = ((x1, at1, into1[cp], y), (x2, at2, into2[cp], pltpu.roll(y, LANES - 8, axis=1)))
                        for x, at, into, part_ in both:
                            for a, more in enumerate(unpack_lanes(jnp.where(packed_lanes, part_, 0.0))):
                                x[a, into, at : at + 8, :] = x[a, into, at : at + 8, :] + more
                        deep = [unpack(got[0]), unpack(y)]
                    deep[1] = [jnp.where(lane8 < 32, pltpu.roll(y, LANES - 16, axis=1), 0.0) for y in deep[1]]
                    for c in range(2):
                        for a, more in enumerate(deep[c]):
                            for f in firsts:
                                g[a, c, f : f + 8, :] = g[a, c, f : f + 8, :] + more

                given(comes(rp, cp), add)
        for x, y, at, gain in ((x1, y1, nr // 2, gain1), (x2, y2, nr // 4, gain2)):
            q_rows(x, y, slice(0, 8), gain)
            q_rows(x, y, slice(at, at + 8), gain)

    with jax.named_scope("deep"):
        shape = (stack, 256)
        at_row = level_of(shape, 0, tops[1:])
        at_col = level_of(shape, 1, lane_cuts)
        gains = [gain_ref[level] - gain_ref[level - 1] for level in (3, 4, 5)] + [-gain_ref[5]]
        factor = jnp.where(
            at_row == 0, gains[0], jnp.where(at_row == 1, gains[1], jnp.where(at_row == 2, gains[2], gains[3]))
        )
        n, d = (jnp.concatenate([g[a, 0], g[a, 1]], axis=1) for a in range(2))
        x = jnp.where(jnp.logical_and(at_row == at_col, d > 0), factor * (n / d), 0.0)
        high, low = split(x)
        er = [table("er", k) for k in (0, 1)]
        x = dot(er[0], high) + dot(er[0], low) + dot(er[1], high)
        high, low = split(x)
        ec = [table("ec", k) for k in (0, 1)]
        z3 = dot(high, ec[0]) + dot(low, ec[0]) + dot(high, ec[1])

    with jax.named_scope("z2"):
        z3b[0:m3, :] = z3

        def grow_rows(src, dst, put, get, count):
            x, y, w = (src[get + (slice(k, k + count), slice(None))] for k in (1, 2, 3))
            dst[put + (pl.ds(0, count, stride=2), slice(None))] = 0.125 * (x + w) + 0.75 * y
            dst[put + (pl.ds(1, count, stride=2), slice(None))] = 0.5 * (y + w)

        def block(x, put, p, first):
            ok = jnp.logical_or(line8 >= 4, up) if first else jnp.logical_or(line8 < 4, down)
            x[put + (slice(p, p + 8), slice(None))] = jnp.where(ok, x[put + (slice(p, p + 8), slice(None))], 0.0)

        grow_rows(z3b, z2b, (0,), (), nr // 8 + 8)
        block(z2b, (0,), 0, True)
        block(z2b, (0,), nr // 4, False)
        z2 = right(z2b[0], table("e2")) + y2[...]
        tiles2 = z2.shape[1] // LANES
        for c in range(tiles2):
            z2b[c] = z2[:, c * LANES : (c + 1) * LANES]
    with jax.named_scope("z1"):
        for c in range(tiles2):
            grow_rows(z2b, z1b, (c,), (c,), nr // 4 + 8)
            block(z1b, (c,), 0, True)
            block(z1b, (c,), nr // 2, False)
        z1 = right(wide_of(z1b, slice(None), range(tiles2)), table("e1")) + y1[...]
    with jax.named_scope("e0"):
        full = right(z1, table("e0"))

    with jax.named_scope("w_top"):
        everything = pltpu.make_async_copy(slots, slots, precv)
        everything.wait()
        pltpu.make_async_copy(slots, slots, psend).wait()
    with jax.named_scope("top"):
        total = part[...] + jnp.sum(slots[...], axis=0)
        top_sum = jnp.sum(jnp.where(lane1 < LANES // 2, total, 0.0), axis=1, keepdims=True)
        top_weight = jnp.sum(jnp.where(lane1 < LANES // 2, 0.0, total), axis=1, keepdims=True)
        top_line = (top_sum / top_weight) * line[1:2, :]
        for c in own_range:
            cols = slice(c * LANES, (c + 1) * LANES)
            wide[c] = full[:, cols] + table("second") * top_line[:, cols]
    with jax.named_scope("out"):
        gain = gain_ref[0]
        chunk = 32
        for c in own_range:
            for m in range(0, nr // 2, chunk):
                x, y, w = (wide[c, pl.ds(m + k, chunk), :] for k in (3, 4, 5))
                even, odd = pl.ds(2 * m, chunk, stride=2), pl.ds(2 * m + 1, chunk, stride=2)
                q0[c, even, :] = gain * q0[c, even, :] + (0.125 * (x + w) + 0.75 * y)
                q0[c, odd, :] = gain * q0[c, odd, :] + 0.5 * (y + w)
                out_ref[pl.ds(2 * m, 2 * chunk), c * LANES : (c + 1) * LANES] = q0[c, pl.ds(2 * m, 2 * chunk), :]


def local(mesh_shape, heights, scene_ids, scene_offset, scene_weight, band_gain):
    nx, ny, nz = mesh_shape
    nr, nc = heights.shape
    ns = 1 if nx == 2 else 2
    made = tables(nr, nc, nx, ny * nz)
    given, places = merge(made)
    sizes = (nr, nc, nx, ny, nz, ns)
    ext = (nr + 2 * HALO, nc)
    tiles = nc // LANES
    own_tiles = tiles
    m3 = nr // 8 + 8
    size1, size2, stack = nr // 2 + 16, nr // 4 + 16, nr // 8 + nr // 16 + nr // 32 + nr // 64 + 40
    tiles1, tiles2 = nc // 2 // LANES + 1, nc // 4 // LANES + 1
    beside = size1 + size2 + 4 * stack
    peers = nx * ny * nz - 1
    messages = 3 * (1 + ns) - 1
    hbm = pl.BlockSpec(memory_space=pltpu.HBM)
    return pl.pallas_call(
        functools.partial(kernel, sizes, places),
        out_shape=pltpu.VMEM((nr, nc), F32),
        in_specs=[hbm] * (5 + len(given)),
        out_specs=pl.BlockSpec(memory_space=pltpu.VMEM),
        scratch_shapes=[pltpu.VMEM(x.shape[1:], x.dtype) for x in given]
        + [
            pltpu.SMEM(scene_offset.shape, F32),
            pltpu.SMEM(scene_weight.shape, F32),
            pltpu.SMEM(band_gain.shape, F32),
            pltpu.VMEM(ext, F32),
            pltpu.VMEM(ext, jnp.int32),
            pltpu.VMEM((own_tiles, nr, LANES), F32),
        ]
        + [pltpu.VMEM((tiles, nr + 3 * HALO, LANES), F32)] * 2
        + [pltpu.VMEM((tiles, nr // 2 + 32, LANES), F32)] * 2
        + [pltpu.VMEM((tiles, nr // 4 + 24, LANES), F32)] * 2
        + [pltpu.VMEM((own_tiles, m3, LANES), F32)] * 2
        + [
            pltpu.VMEM((2, tiles1, size1, LANES), F32),
            pltpu.VMEM((2, tiles2, size2, LANES), F32),
            pltpu.VMEM((2, 2, stack, LANES), F32),
            pltpu.VMEM((size1, tiles1 * LANES), F32),
            pltpu.VMEM((size2, tiles2 * LANES), F32),
            pltpu.VMEM((ns, beside, LANES), F32),
            pltpu.VMEM((ns, beside, LANES), F32),
            pltpu.VMEM((2, 1 + ns, OWN_TILES, 8, LANES), F32),
            pltpu.VMEM((2, 1 + ns, OWN_TILES, 8, LANES), F32),
            pltpu.VMEM((m3 + 8, LANES), F32),
            pltpu.VMEM((tiles2, nr // 4 + 16, LANES), F32),
            pltpu.VMEM((tiles2, nr // 2 + 16, LANES), F32),
            pltpu.VMEM((own_tiles, nr // 2 + 16, LANES), F32),
            pltpu.VMEM((1, LANES), F32),
            pltpu.VMEM((peers, 1, LANES), F32),
            pltpu.SemaphoreType.DMA((CHUNKS + 3,)),
            pltpu.SemaphoreType.DMA((len(given),)),
            pltpu.SemaphoreType.DMA((messages,)),
            pltpu.SemaphoreType.DMA((messages,)),
            pltpu.SemaphoreType.DMA(()),
            pltpu.SemaphoreType.DMA(()),
        ],
        compiler_params=pltpu.CompilerParams(collective_id=0, has_side_effects=True),
    )(scene_offset, scene_weight, band_gain, heights, scene_ids, *given)


def solution(mesh):
    placed = (P(("gy", "gz"), "gx"), P(("gy", "gz"), "gx"), P(), P(), P())
    shape = tuple(mesh.shape[name] for name in ("gx", "gy", "gz"))
    return jax.shard_map(
        functools.partial(local, shape), mesh=mesh, in_specs=placed,
        out_specs=P(("gy", "gz"), "gx"), check_vma=False,
    )
```

```python
import functools

import jax
import jax.numpy as jnp
import numpy as np
from jax import lax
from jax.experimental import pallas as pl
from jax.experimental.pallas import tpu as pltpu
from jax.sharding import PartitionSpec as P

F32, BF16 = jnp.float32, jnp.bfloat16
FAR = 1 << 20
HALO = 16
LANES = 128
LEVELS = 6
MIDDLE = (3, 4, 5)


def reach(count, levels):
    weights = np.ones(count >> levels, np.float64)
    for _ in range(levels):
        fine = np.zeros(2 * weights.size + 4, np.float64)
        for tap, value in zip(range(-2, 3), (0.0625, 0.25, 0.375, 0.25, 0.0625)):
            fine[2 + tap : 2 + tap + 2 * weights.size : 2] += value * weights
        weights = fine[2:-2]
    return weights


class Axis:
    def __init__(self, n, at, count):
        self.n, self.at, self.count = n, at, count

    def inside(self, index, level):
        place = index + self.at * (self.n >> level)
        return (place >= 0) & (place < self.count * (self.n >> level))

    def shrink(self, fine, coarse, level):
        far = np.abs(fine[:, None] - 2 * coarse[None, :])
        value = np.select([far == 0, far == 1, far == 2], [0.375, 0.25, 0.0625], 0.0)
        return value * self.inside(coarse, level)[None, :]

    def grow(self, coarse, fine, level):
        far = np.abs(2 * coarse[:, None] - fine[None, :])
        value = np.select([far == 0, far == 1, far == 2], [0.75, 0.5, 0.125], 0.0)
        return value * self.inside(fine, level)[None, :]

    def window(self, level, edge):
        return np.arange(-edge, (self.n >> level) + edge)

    def deep(self, lanes, shift=0):
        out = [x + shift * (self.n >> level) for level, x in zip((3, 4, 5, 6), self.out())]
        w4, w5 = self.window(4, 30), self.window(5, 14)
        to4 = self.shrink(lanes, w4, 4)
        to5 = to4 @ self.shrink(w4, w5, 5)
        same = (lanes[:, None] == out[0][None, :]) * self.inside(out[0], 3)[None, :]
        parts = [
            same * 1.0,
            self.shrink(lanes, out[1], 4),
            to4 @ self.shrink(w4, out[2], 5),
            to5 @ self.shrink(w5, out[3], 6),
        ]
        return np.concatenate(parts, axis=1) * self.inside(lanes, 3)[:, None]

    def out(self):
        low = -4
        return [low + np.arange(size) for size in self.sizes()]

    def sizes(self):
        return [self.n // 8 + 8, self.n // 16 + 8, self.n // 32 + 8, self.n // 64 + 16]

    def back(self):
        o3, o4, o5, o6 = self.out()
        w4, w5 = self.window(4, 4), self.window(5, 4)
        from4 = self.grow(w4, o3, 3)
        from5 = self.grow(w5, w4, 4) @ from4
        parts = [
            np.eye(o3.size) * self.inside(o3, 3)[None, :],
            self.grow(o4, o3, 3),
            self.grow(o5, w4, 4) @ from4,
            self.grow(o6, w5, 5) @ from5,
        ]
        return np.concatenate(parts, axis=0)

    def sums(self, level, place):
        weights = reach(self.count * (self.n >> level), LEVELS - level)
        place = place + self.at * (self.n >> level)
        return np.where((place >= 0) & (place < weights.size), weights[np.clip(place, 0, weights.size - 1)], 0.0)

    def ones(self, level):
        x = self.inside(self.window(6, 4), 6) * 1.0
        for k in range(5, level - 1, -1):
            x = x @ self.grow(self.window(k + 1, 4), self.window(k, 4), k)
        return x


def pad(x, shape):
    return np.pad(x, [(0, size - have) for size, have in zip(shape, x.shape)])


def halves(x):
    high = x.astype(np.float32).astype(jnp.bfloat16)
    low = (x - high.astype(np.float64)).astype(np.float32).astype(jnp.bfloat16)
    return high, low


def spaced(n):
    size = -(-(n + 8) // LANES) * LANES
    return np.concatenate([np.arange(-4, n + 4), np.full(size - n - 8, FAR)])


def col_tables(n, at, count):
    ax = Axis(n, at, count)
    shifts = [1 if at == 0 else -1] if count == 2 else [1, -1]
    lane = np.arange(LANES)
    own = np.arange(n)
    out1, out2 = spaced(n // 2), spaced(n // 4)
    w1, w2 = ax.window(1, 16), ax.window(2, 8)
    middle = np.isin(lane, MIDDLE)[None, :]
    s1, s2 = [], []
    for d in shifts:
        near = n - LANES + lane if d > 0 else lane
        over1, over2 = (lane - 4 + (n >> level if d > 0 else 0) for level in (1, 2))
        s1.append(ax.shrink(near, over1, 1) * middle)
        s2.append(ax.shrink(near, w1, 1) @ ax.shrink(w1, over2, 2) * middle)
    s1, s2 = (np.stack([np.stack([x, np.roll(x, LANES // 2, 1)]) for x in y]) for y in (s1, s2))
    o3 = ax.out()[0]
    to2 = ax.shrink(own, w1, 1)
    c03 = to2 @ ax.shrink(w1, w2, 2) @ ax.shrink(w2, o3, 3)
    c03 = np.concatenate([pad(x.astype(np.float64), (n, LANES)) for x in halves(c03)], axis=1)
    three = np.concatenate([o3, np.full(LANES - o3.size, FAR)])
    call = []
    for d in [0] + shifts:
        call.append([pad(x.astype(np.float64), (LANES, 256)) for x in halves(ax.deep(three, d))])
    call = np.stack([np.concatenate([x[k] for x in call], axis=1) for k in range(2)])
    back = ax.back()
    to0 = ax.grow(w2, w1, 1) @ ax.grow(w1, own, 0)
    ec0 = np.stack([pad(x.astype(np.float64), (256, n)) for x in halves(back @ ax.grow(o3, w2, 2) @ to0)])
    return dict(
        c1=ax.shrink(own, out1, 1), c2=to2 @ ax.shrink(w1, out2, 2), s1=s1, s2=s2, c03=c03, call=call,
        ec0=ec0, e1=ax.grow(out2, out1, 1), e0=ax.grow(out1, own, 0),
    ), dict(line=np.stack([ax.sums(0, own), ax.ones(0)[4:-4]]))


def row_tables(n, at, count):
    ax = Axis(n, at, count)
    o3 = ax.out()[0]
    deep = ax.deep(o3).T
    high, low = (x.astype(np.float64) for x in halves(deep))
    size6 = ax.sizes()[3]
    rall = np.concatenate([high, low[-size6:]], axis=0)
    rall = pad(rall, (-(-rall.shape[0] // 16) * 16, o3.size))
    back = ax.back()
    er = np.stack([x.astype(np.float64) for x in halves(back.T)])
    first = np.repeat(ax.sums(3, o3)[:, None], LANES, 1)
    w2 = ax.window(2, 8)
    r12 = (ax.grow(o3, w2, 2) @ ax.grow(w2, np.arange(-4, n // 2 + 12), 1)).T
    second = np.repeat(pad(ax.ones(1), (n // 2 + 16,))[:, None], LANES, 1)
    return dict(rall=rall, er=er, r12=r12), dict(first=first, second=second)


def tables(nr, nc, nx, blocks):
    def places(count):
        return (0, 1) if count == 2 else (0, 1, count - 1)

    cols = [col_tables(nc, at, nx) for at in places(nx)]
    rows = [row_tables(nr, at, blocks) for at in places(blocks)]

    def cast(x):
        return jnp.asarray(np.asarray(x, np.float32)).astype(BF16)

    def keep(x):
        return jnp.asarray(np.asarray(x, np.float32))

    out = {}
    for some in (cols, rows):
        for k in some[0][0]:
            out[k] = cast(np.stack([x[0][k] for x in some]))
        for k in some[0][1]:
            out[k] = keep(np.stack([x[1][k] for x in some]))
    return out


def merge(made):
    arrays, places = [], {}
    for at, group in enumerate(COLS + ROWS):
        lanes = max(made[name].shape[-1] for name in group)
        parts, start = [], 0
        for name in group:
            x = made[name]
            rows, width = x.shape[-2:]
            x = x.reshape(x.shape[0], -1, rows, width)
            tall = -(-rows // 16) * 16 if len(group) > 1 else rows
            x = jnp.pad(x, ((0, 0), (0, 0), (0, tall - rows), (0, lanes - width)))
            places[name] = (at, start, tall, rows, width)
            start += x.shape[1] * tall
            parts.append(x.reshape(x.shape[0], -1, lanes))
        arrays.append(jnp.concatenate(parts, axis=1))
    return arrays, places


def split(x):
    high = x.astype(BF16)
    return high, (x - high.astype(F32)).astype(BF16)


def dot(a, b):
    return jnp.dot(a, b, preferred_element_type=F32)


def right(x, c):
    high, low = split(x)
    return dot(high, c) + dot(low, c)


COLS = (("c03", "c2"), ("call", "e0"), ("c1", "e1"), ("s1", "s2"), ("ec0",), ("line",))
ROWS = (("rall", "er", "r12"), ("first", "second"))
OWN_TILES, SIDE_TILES = 5, 2
CHUNKS = 4


def kernel(
    sizes, places, off_hbm, wgt_hbm, gain_hbm, h_ref, s_ref, *rest
):
    nr, nc, nx, ny, nz, ns = sizes
    count = len(COLS) + len(ROWS)
    tables_hbm, rest = rest[:count], rest[count:]
    out_ref, rest = rest[0], rest[1:]
    tab, rest = rest[:count], rest[count:]
    (
        off_ref, wgt_ref, gain_ref, h_buf, s_buf, q0, num, den, n1, d1, n2, d2, n3, d3,
        x1, x2, g, factor, y1, y2, side_s, side_r, edge_s, edge_r, z2b, z1b, wide, part, slots,
        own_sem, tab_sem, send0, recv0, psend, precv,
    ) = rest
    cx, cy, cz = lax.axis_index("gx"), lax.axis_index("gy"), lax.axis_index("gz")
    row = cy * nz + cz
    blocks = ny * nz
    own_tiles = nc // LANES
    t3 = nr // 8
    m3 = t3 + 8

    def kind(at, count):
        return at if count == 2 else jnp.where(at == 0, 0, jnp.where(at == count - 1, 2, 1))

    ct, rt = kind(cx, nx), kind(row, blocks)

    loads = []
    step = nr // CHUNKS
    for k in range(CHUNKS):
        rows = pl.ds(k * step, step)
        for a, (src, dst) in enumerate(((h_ref, h_buf), (s_ref, s_buf))):
            loads.append(
                pltpu.make_async_copy(
                    src.at[rows, :],
                    dst.at[pl.ds(HALO + k * step, step), pl.ds(0, nc)],
                    own_sem.at[k],
                )
            )
    small = [
        pltpu.make_async_copy(src, dst, own_sem.at[CHUNKS + a])
        for a, (src, dst) in enumerate(((off_hbm, off_ref), (wgt_hbm, wgt_ref), (gain_hbm, gain_ref)))
    ]
    fetch = [
        pltpu.make_async_copy(src.at[ct if i < len(COLS) else rt], tab[i], tab_sem.at[i])
        for i, src in enumerate(tables_hbm)
    ]
    ready = set()

    def await_tables(*names):
        for name in names:
            if places[name][0] not in ready:
                ready.add(places[name][0])
                fetch[places[name][0]].wait()

    def table(name, k=0, rows=None):
        at, start, tall, height, width = places[name]
        first, last = rows or (0, height)
        return tab[at][start + k * tall + first : start + k * tall + last, :width]

    for copy in loads[:2] + small + loads[2:]:
        copy.start()

    up, down = row > 0, row < blocks - 1
    send_row, recv_row = {0: None, 1: down, 2: up}, {0: None, 1: up, 2: down}
    if ns == 1:
        send_col, recv_col = {0: None, 1: None}, {0: None, 1: None}
        to_col = {0: cx, 1: 1 - cx}
        near_tile = {1: (1 - cx) * (own_tiles - 1)}
        into1, into2 = {1: (1 - cx) * (x1.shape[1] - 1)}, {1: (1 - cx) * (x2.shape[1] - 1)}
    else:
        send_col = {0: None, 1: cx < nx - 1, 2: cx > 0}
        recv_col = {0: None, 1: cx > 0, 2: cx < nx - 1}
        to_col = {0: cx, 1: cx + 1, 2: cx - 1}
        near_tile = {1: own_tiles - 1, 2: 0}
        into1, into2 = {1: 0, 2: x1.shape[1] - 1}, {1: 0, 2: x2.shape[1] - 1}
    kinds = [(rp, cp) for rp in (0, 1, 2) for cp in range(1 + ns) if rp or cp]

    def device(rp, cp):
        target = row + {0: 0, 1: 1, 2: -1}[rp]
        return {"gx": to_col[cp], "gy": target // nz, "gz": target % nz}

    def also(a, b):
        return b if a is None else a if b is None else jnp.logical_and(a, b)

    def sends(rp, cp):
        return also(send_row[rp], send_col[cp])

    def comes(rp, cp):
        return also(recv_row[rp], recv_col[cp])

    def given(flag, body):
        if flag is None:
            body()
        else:
            pl.when(flag)(body)

    everyone = nx * blocks
    me = row * nx + cx

    def peer(s):
        other = (me + s) % everyone
        line = other // nx
        return {"gx": other % nx, "gy": line // nz, "gz": line % nz}

    def places_of(at, count):
        return [jnp.where(at + d < count, at + d, at + d - count) for d in range(count)]

    def others(body):
        if everyone <= 64:
            xs, ys, zs = places_of(cx, nx), places_of(cy, ny), places_of(cz, nz)
            for s in range(1, everyone):
                line = s // nx
                body(s, {"gx": xs[s % nx], "gy": ys[line // nz], "gz": zs[line % nz]})
        else:
            def step_(s, carry):
                body(s, peer(s))
                return carry

            lax.fori_loop(1, everyone, step_, 0)

    barrier = pltpu.get_barrier_semaphore()
    others(lambda s, who: pl.semaphore_signal(barrier, inc=1, device_id=who))

    for copy in fetch:
        copy.start()

    zero = jnp.zeros((HALO, LANES), F32)
    for x in (num, den):
        for c in range(own_tiles):
            x[c, 0:HALO, :] = zero
            x[c, nr + HALO : nr + 2 * HALO, :] = zero
            x[c, nr + 2 * HALO :, :] = zero
    zero = jnp.zeros((8, LANES), F32)
    for x in (n1, d1, n2, d2):
        for c in range(own_tiles):
            x[c, 0:8, :] = zero
            x[c, x.shape[1] - 8 :, :] = zero

    def edge(i):
        rp, cp = kinds[i]
        if rp == 0:
            src, dst = side_s.at[cp - 1], side_r.at[cp - 1]
        else:
            place = pl.ds(0, OWN_TILES) if cp == 0 else pl.ds(0, SIDE_TILES)
            src, dst = edge_s.at[rp - 1, cp, place], edge_r.at[rp - 1, cp, place]
        return pltpu.make_async_remote_copy(
            src_ref=src, dst_ref=dst, send_sem=send0.at[i], recv_sem=recv0.at[i], device_id=device(rp, cp)
        )

    lane8 = lax.broadcasted_iota(jnp.int32, (8, LANES), 1)
    line8 = lax.broadcasted_iota(jnp.int32, (8, LANES), 0)

    def spread(table):
        line = jnp.zeros((8, LANES), F32)
        for i in range(table.shape[0]):
            line = jnp.where(lane8 == i, table[i], line)
        return line

    for copy in small:
        copy.wait()
    wgt_row = spread(wgt_ref)

    def tree(ids, table):
        values = [table[i] for i in range(table.shape[0])]
        bit = 1
        while len(values) > 1:
            mask = (ids & bit) != 0
            values = [jnp.where(mask, values[i + 1], values[i]) for i in range(0, len(values), 2)]
            bit *= 2
        return values[0]

    def level0(base, count, c):
        rows = pl.ds(base, count)
        ids = s_buf[rows, c * LANES : (c + 1) * LANES]
        weight = jnp.concatenate(
            [jnp.take_along_axis(wgt_row, ids[r : r + 8], axis=1) for r in range(0, count, 8)], axis=0
        )
        moved = h_buf[rows, c * LANES : (c + 1) * LANES] + tree(ids, off_ref)
        num[c, rows, :] = weight * moved
        den[c, rows, :] = weight
        return moved

    def summary(s, who):
        return pltpu.make_async_remote_copy(
            src_ref=part,
            dst_ref=slots.at[s - 1],
            send_sem=psend,
            recv_sem=precv,
            device_id=who,
        )

    def send_edges(wanted):
        for i, d in enumerate(kinds):
            if wanted(d):
                given(sends(*d), lambda: edge(i).start())

    with jax.named_scope("level0"):
        for k in range(CHUNKS):
            both = pl.ds(0, 2 * step)
            pltpu.make_async_copy(h_ref.at[both, :], h_buf.at[both, pl.ds(0, nc)], own_sem.at[k]).wait()
            for c in range(own_tiles):
                q0[c, k * step : (k + 1) * step, :] = level0(HALO + k * step, step, c)

    lane1 = lax.broadcasted_iota(jnp.int32, (1, LANES), 1)

    def meet():
        with jax.named_scope("meet"):
            pl.semaphore_wait(barrier, everyone - 1)

        others(lambda s, who: summary(s, who).start())

    def taps(src, c, start, count):
        x = [src[c, pl.ds(start + a, count, stride=2), :] for a in range(-2, 3)]
        return 0.375 * x[2] + (0.25 * (x[1] + x[3]) + 0.0625 * (x[0] + x[4]))

    def hold(x, c, p, first):
        if first:
            ok = jnp.logical_or(line8 >= 4, up)
        else:
            ok = jnp.logical_or(line8 < 4, down)
        x[c, p : p + 8, :] = jnp.where(ok, x[c, p : p + 8, :], 0.0)

    last1, last2 = nr // 2 + 8, nr // 4 + 8

    def ends1(x, c):
        hold(x, c, 8, True)
        hold(x, c, last1, False)

    def ends2(x, c):
        hold(x, c, 8, True)
        hold(x, c, last2, False)

    def rows1(src, dst, c, p, count):
        dst[c, p : p + count, :] = taps(src, c, 2 * p - 8, count)

    def rows2(src, dst, c, p, count):
        dst[c, p : p + count, :] = taps(src, c, 2 * p - 12, count)

    with jax.named_scope("rowpyr"):
        for src, one, two, three in ((num, n1, n2, n3), (den, d1, d2, d3)):
            for c in range(own_tiles):
                rows1(src, one, c, 8, nr // 2 + 16)
                ends1(one, c)
                rows2(one, two, c, 8, nr // 4 + 8)
                ends2(two, c)
                three[c] = taps(two, c, 4, m3)

    with jax.named_scope("sums"):
        await_tables("line", "first")
        flat = []
        for x in (n3, d3):
            y = sum(x[c] * table("line", 0, (0, 1))[:, c * LANES : (c + 1) * LANES] for c in range(own_tiles))
            y = jnp.sum(y * table("first"), axis=0, keepdims=True)
            flat.append(y + pltpu.roll(y, LANES // 2, axis=1))
        part[...] = jnp.where(lane1 < LANES // 2, flat[0], flat[1])

    early_half = cz < nz // 2 if nz > 1 else None
    if early_half is None:
        meet()
    else:
        pl.when(jnp.logical_not(early_half))(meet)
    def wide_of(x, rows, tiles):
        return jnp.concatenate([x[c, rows, :] for c in tiles], axis=1)

    own_range = range(own_tiles)
    size1, size2 = x1.shape[2], x2.shape[2]
    s3, s4, s5, s6 = (nr // 8 + 8, nr // 16 + 8, nr // 32 + 8, nr // 64 + 16)
    stack = s3 + s4 + s5 + s6
    tops = (0, s3, s3 + s4, s3 + s4 + s5)
    bottoms = tuple(top + (nr >> level) for top, level in zip(tops, (3, 4, 5, 6)))

    def level_of(shape, dim, cuts):
        index = lax.broadcasted_iota(jnp.int32, shape, dim)
        return sum((index >= cut).astype(jnp.int32) for cut in cuts)

    c3, c4, c5 = nc // 8 + 8, nc // 16 + 8, nc // 32 + 8
    lane_cuts = (c3, c3 + c4, c3 + c4 + c5)
    middle = jnp.logical_and(line8 >= MIDDLE[0], line8 <= MIDDLE[-1])

    def pack(n, d):
        return jnp.where(middle, n, pltpu.roll(d, 4, axis=0))

    def unpack(x):
        return jnp.where(middle, x, 0.0), jnp.where(middle, pltpu.roll(x, 4, axis=0), 0.0)

    def unpack_lanes(x):
        low = lax.broadcasted_iota(jnp.int32, x.shape, 1) < LANES // 2
        return jnp.where(low, x, 0.0), jnp.where(low, pltpu.roll(x, LANES // 2, axis=1), 0.0)

    with jax.named_scope("p3"):
        await_tables("c03", "rall", "call")
        x = jnp.concatenate([wide_of(n3, slice(None), own_range), wide_of(d3, slice(None), own_range)], axis=0)
        x = right(x, table("c03"))
        x = x[:, :LANES] + x[:, LANES:]
        high, low = split(jnp.concatenate([x[:m3], x[m3:]], axis=1))
        rall = table("rall")
        x = dot(rall, high) + dot(rall, low)
        x = jnp.concatenate([x[: stack - s6], x[stack - s6 : stack] + x[stack : stack + s6]], axis=0)
        high, low = split(jnp.concatenate([x[:, :LANES], x[:, LANES:]], axis=0))
        x = dot(high, table("call", 0)) + dot(low, table("call", 0))
        tail = stack - 32
        more = [dot(high[a * stack + tail : (a + 1) * stack], table("call", 1)) for a in range(2)]
        x = jnp.concatenate(
            [y for a in range(2) for y in (x[a * stack : a * stack + tail], x[a * stack + tail : (a + 1) * stack] + more[a])],
            axis=0,
        )

    base_g = size1 + size2

    def own_lines(x1_, x2_, g_):
        last = x1_[2] + pltpu.roll(x2_[1], 8, axis=1) + pltpu.roll(g_[1], 16, axis=1)
        return [x1_[0], x1_[1], x2_[0], g_[0], last]

    def ends(x, c, last):
        return jnp.concatenate([x[c, 8:16, :], x[c, last : last + 8, :]], axis=0)

    with jax.named_scope("edge_own"):
        await_tables("s1", "s2", "c1", "c2")

        def own_ends(n, d, last, name):
            y = jnp.concatenate(
                [jnp.concatenate([ends(x, c, last) for c in own_range], axis=1) for x in (n, d)], axis=0
            )
            return right(y, table(name))

        own1, own2 = own_ends(n1, d1, last1, "c1"), own_ends(n2, d2, last2, "c2")

    with jax.named_scope("edge_side"):
        side_ends = []
        for k in range(1, 1 + ns):
            pair = []
            for n, d, last, name in ((n1, d1, last1, "s1"), (n2, d2, last2, "s2")):
                y = right(ends(n, near_tile[k], last), table(name, 2 * (k - 1)))
                pair.append(y + right(ends(d, near_tile[k], last), table(name, 2 * (k - 1) + 1)))
            side_ends.append(pair)

    def tile(x, at, c):
        return x[at : at + 8, c * LANES : (c + 1) * LANES]

    with jax.named_scope("g_pack"):
        for k in range(1 + ns):
            piece = [
                [x[a * stack : (a + 1) * stack, k * 256 + c * LANES : k * 256 + (c + 1) * LANES] for c in (0, 1)]
                for a in (0, 1)
            ]
            for a in range(2):
                for c in range(2):
                    if k == 0:
                        g[a, c] = piece[a][c]
                    else:
                        side_s[k - 1, base_g + (2 * a + c) * stack : base_g + (2 * a + c + 1) * stack, :] = piece[a][c]
            for rp, firsts in ((1, bottoms), (2, tops)):
                deep = []
                for a in range(2):
                    lines = []
                    for c in range(2):
                        index = lane8 + c * LANES
                        b = [piece[a][c][f : f + 8] for f in firsts]
                        lines.append(
                            jnp.where(
                                index < lane_cuts[0], b[0],
                                jnp.where(index < lane_cuts[1], b[1], jnp.where(index < lane_cuts[2], b[2], b[3])),
                            )
                        )
                    deep.append(lines)
                at = 8 * (2 - rp)
                if k == 0:
                    packed = [
                        own_lines(
                            [tile(own1, 16 * a + at, c) for c in range(3)],
                            [tile(own2, 16 * a + at, c) for c in range(2)],
                            deep[a],
                        )
                        for a in range(2)
                    ]
                    for t in range(OWN_TILES):
                        edge_s[rp - 1, 0, t] = pack(packed[0][t], packed[1][t])
                else:
                    lines = [y[at : at + 8] for y in side_ends[k - 1]]
                    edge_s[rp - 1, k, 0] = pack(deep[0][0], deep[1][0])
                    edge_s[rp - 1, k, 1] = (
                        lines[0] + pltpu.roll(lines[1], 8, axis=1)
                        + pltpu.roll(pack(deep[0][1], deep[1][1]), 16, axis=1)
                    )

    if early_half is not None:
        pl.when(early_half)(meet)

    with jax.named_scope("send"):
        send_edges(lambda d: d[0] != 0)

    body1, body2 = slice(8, 8 + size1), slice(8, 8 + size2)

    with jax.named_scope("x_side"):
        for k in range(1, 1 + ns):
            for base, n, d, body, name in ((0, n1, d1, body1, "s1"), (size1, n2, d2, body2, "s2")):
                y = right(n[near_tile[k], body, :], table(name, 2 * (k - 1) + 0))
                y = y + right(d[near_tile[k], body, :], table(name, 2 * (k - 1) + 1))
                side_s[k - 1, base : base + y.shape[0], :] = y
        send_edges(lambda d: d[0] == 0)

    with jax.named_scope("x_own"):
        for n, d, body, name, dst in ((n1, d1, body1, "c1", x1), (n2, d2, body2, "c2", x2)):
            for a, y in enumerate((n, d)):
                y = right(wide_of(y, body, own_range), table(name))
                for c in range(dst.shape[1]):
                    dst[a, c] = y[:, c * LANES : (c + 1) * LANES]

    def ratio(n, d):
        return jnp.where(d > 0, n / d, 0.0)

    def await_edges(wanted):
        for i, d in enumerate(kinds):
            if wanted(d):
                given(sends(*d), lambda: edge(i).wait_send())
                given(comes(*d), lambda: edge(i).wait_recv())

    def q_rows(x, y, rows, gain):
        for c in range(x.shape[1]):
            y[rows, c * LANES : (c + 1) * LANES] = gain * ratio(x[0, c, rows, :], x[1, c, rows, :])

    gain1, gain2 = gain_ref[1] - gain_ref[0], gain_ref[2] - gain_ref[1]

    with jax.named_scope("w_side"):
        await_edges(lambda d: d[0] == 0)
    with jax.named_scope("add_side"):
        for k in range(1, 1 + ns):
            def add():
                for base, size, x, into in ((0, size1, x1, into1[k]), (size1, size2, x2, into2[k])):
                    more = unpack_lanes(side_r[k - 1, base : base + size, :])
                    for a in range(2):
                        x[a, into] = x[a, into] + more[a]
                for a in range(2):
                    for c in range(2):
                        base = base_g + (2 * a + c) * stack
                        g[a, c] = g[a, c] + side_r[k - 1, base : base + stack, :]

            given(recv_col[k], add)
    with jax.named_scope("q"):
        q_rows(x1, y1, slice(0, size1), gain1)
        q_rows(x2, y2, slice(0, size2), gain2)

    def grow_rows(src, dst, first, count):
        x, y, w = (src[first + k : first + k + count, :] for k in (1, 2, 3))
        dst[pl.ds(2 * first, count, stride=2), :] = 0.125 * (x + w) + 0.75 * y
        dst[pl.ds(2 * first + 1, count, stride=2), :] = 0.5 * (y + w)

    def block(x, c, p, first):
        ok = jnp.logical_or(line8 >= 4, up) if first else jnp.logical_or(line8 < 4, down)
        x[c, p : p + 8, :] = jnp.where(ok, x[c, p : p + 8, :], 0.0)

    tiles2 = range(x2.shape[1])

    def mask_ends():
        for c in tiles2:
            block(z1b, c, 0, True)
            block(z1b, c, nr // 2, False)

    def upward(parts):
        z = jnp.concatenate([jnp.concatenate([z1b[c, p, :] for c in tiles2], axis=1) for p in parts], axis=0)
        z = right(z, table("e1")) + jnp.concatenate([y1[p, :] for p in parts], axis=0)
        return right(z, table("e0"))

    with jax.named_scope("factor"):
        shape = (stack, 256)
        at_row = level_of(shape, 0, tops[1:])
        at_col = level_of(shape, 1, lane_cuts)
        gains = [gain_ref[level] - gain_ref[level - 1] for level in (3, 4, 5)] + [-gain_ref[5]]
        value = jnp.where(
            at_row == 0, gains[0], jnp.where(at_row == 1, gains[1], jnp.where(at_row == 2, gains[2], gains[3]))
        )
        factor[...] = jnp.where(at_row == at_col, value, 0.0)

    with jax.named_scope("base"):
        await_tables("e1", "e0")
        for c in tiles2:
            z2b[c] = y2[:, c * LANES : (c + 1) * LANES]
            grow_rows(z2b.at[c], z1b.at[c], 0, nr // 4 + 8)
        mask_ends()
        base = upward((slice(0, size1),))
        for c in own_range:
            wide[c] = base[:, c * LANES : (c + 1) * LANES]

    with jax.named_scope("w_edges"):
        await_edges(lambda d: d[0] != 0)
        await_tables("ec0", "r12", "er", "second")
    packed_lanes = jnp.logical_and(lane8 % (LANES // 2) >= MIDDLE[0], lane8 % (LANES // 2) <= MIDDLE[-1])
    with jax.named_scope("edges"):
        for rp, at1, at2, firsts in ((1, 0, 0, tops), (2, nr // 2, nr // 4, bottoms)):
            for cp in range(1 + ns):

                def add():
                    got = edge_r.at[rp - 1, cp]
                    tail = unpack(got[OWN_TILES - 1]) if cp == 0 else None
                    if cp == 0:
                        adds1 = [unpack(got[0]), unpack(got[1]), [jnp.where(lane8 < 8, y, 0.0) for y in tail]]
                        adds2 = [
                            unpack(got[2]),
                            [jnp.where(lane8 < 8, pltpu.roll(y, LANES - 8, axis=1), 0.0) for y in tail],
                        ]
                        for x, at, adds in ((x1, at1, adds1), (x2, at2, adds2)):
                            for c, more in enumerate(adds):
                                for a in range(2):
                                    x[a, c, at : at + 8, :] = x[a, c, at : at + 8, :] + more[a]
                        deep = [unpack(got[3]), tail]
                    else:
                        y = got[1]
                        both = ((x1, at1, into1[cp], y), (x2, at2, into2[cp], pltpu.roll(y, LANES - 8, axis=1)))
                        for x, at, into, part_ in both:
                            for a, more in enumerate(unpack_lanes(jnp.where(packed_lanes, part_, 0.0))):
                                x[a, into, at : at + 8, :] = x[a, into, at : at + 8, :] + more
                        deep = [unpack(got[0]), unpack(y)]
                    deep[1] = [jnp.where(lane8 < 32, pltpu.roll(y, LANES - 16, axis=1), 0.0) for y in deep[1]]
                    for c in range(2):
                        for a, more in enumerate(deep[c]):
                            for f in firsts:
                                g[a, c, f : f + 8, :] = g[a, c, f : f + 8, :] + more

                given(comes(rp, cp), add)
        for x, y, at, gain in ((x1, y1, nr // 2, gain1), (x2, y2, nr // 4, gain2)):
            q_rows(x, y, slice(0, 8), gain)
            q_rows(x, y, slice(at, at + 8), gain)
    with jax.named_scope("fix"):
        for c in tiles2:
            for at in (0, nr // 4):
                z2b[c, at : at + 8, :] = y2[at : at + 8, c * LANES : (c + 1) * LANES]
                grow_rows(z2b.at[c], z1b.at[c], at, 8)
        mask_ends()
        parts = (slice(0, 16), slice(nr // 2, nr // 2 + 16))
        base = upward(parts)
        for c in own_range:
            for i, p in enumerate(parts):
                wide[c, p, :] = base[16 * i : 16 * i + 16, c * LANES : (c + 1) * LANES]

    with jax.named_scope("deep"):
        n, d = (jnp.concatenate([g[a, 0], g[a, 1]], axis=1) for a in range(2))
        x = jnp.where(d > 0, factor[...] * (n / d), 0.0)
        high, low = split(x)
        er = [table("er", k) for k in (0, 1)]
        x = dot(er[0], high) + dot(er[0], low) + dot(er[1], high)
        high, low = split(x)
        x = dot(high, table("ec0")) + dot(low, table("ec0")) + dot(high, table("ec0", 1))
        high, low = split(x)
        full = dot(table("r12"), high) + dot(table("r12"), low)

    with jax.named_scope("w_top"):
        everything = pltpu.make_async_copy(slots, slots, precv)
        everything.wait()
        pltpu.make_async_copy(slots, slots, psend).wait()
    with jax.named_scope("top"):
        total = part[...] + jnp.sum(slots[...], axis=0)
        top_sum = jnp.sum(jnp.where(lane1 < LANES // 2, total, 0.0), axis=1, keepdims=True)
        top_weight = jnp.sum(jnp.where(lane1 < LANES // 2, 0.0, total), axis=1, keepdims=True)
        top_line = (top_sum / top_weight) * table("line", 0, (1, 2))
        for c in own_range:
            cols = slice(c * LANES, (c + 1) * LANES)
            wide[c] = wide[c] + (full[:, cols] + table("second") * top_line[:, cols])
    with jax.named_scope("out"):
        gain = gain_ref[0]
        chunk = 32
        for c in own_range:
            for m in range(0, nr // 2, chunk):
                x, y, w = (wide[c, pl.ds(m + k, chunk), :] for k in (3, 4, 5))
                even, odd = pl.ds(2 * m, chunk, stride=2), pl.ds(2 * m + 1, chunk, stride=2)
                q0[c, even, :] = gain * q0[c, even, :] + (0.125 * (x + w) + 0.75 * y)
                q0[c, odd, :] = gain * q0[c, odd, :] + 0.5 * (y + w)
                out_ref[pl.ds(2 * m, 2 * chunk), c * LANES : (c + 1) * LANES] = q0[c, pl.ds(2 * m, 2 * chunk), :]


def local(mesh_shape, heights, scene_ids, scene_offset, scene_weight, band_gain):
    nx, ny, nz = mesh_shape
    nr, nc = heights.shape
    ns = 1 if nx == 2 else 2
    made = tables(nr, nc, nx, ny * nz)
    given, places = merge(made)
    sizes = (nr, nc, nx, ny, nz, ns)
    ext = (nr + 2 * HALO, nc)
    tiles = nc // LANES
    own_tiles = tiles
    m3 = nr // 8 + 8
    size1, size2, stack = nr // 2 + 16, nr // 4 + 16, nr // 8 + nr // 16 + nr // 32 + nr // 64 + 40
    tiles1, tiles2 = nc // 2 // LANES + 1, nc // 4 // LANES + 1
    beside = size1 + size2 + 4 * stack
    peers = nx * ny * nz - 1
    messages = 3 * (1 + ns) - 1
    hbm = pl.BlockSpec(memory_space=pltpu.HBM)
    return pl.pallas_call(
        functools.partial(kernel, sizes, places),
        out_shape=pltpu.VMEM((nr, nc), F32),
        in_specs=[hbm] * (5 + len(given)),
        out_specs=pl.BlockSpec(memory_space=pltpu.VMEM),
        scratch_shapes=[pltpu.VMEM(x.shape[1:], x.dtype) for x in given]
        + [
            pltpu.SMEM(scene_offset.shape, F32),
            pltpu.SMEM(scene_weight.shape, F32),
            pltpu.SMEM(band_gain.shape, F32),
            pltpu.VMEM(ext, F32),
            pltpu.VMEM(ext, jnp.int32),
            pltpu.VMEM((own_tiles, nr, LANES), F32),
        ]
        + [pltpu.VMEM((tiles, nr + 3 * HALO, LANES), F32)] * 2
        + [pltpu.VMEM((tiles, nr // 2 + 32, LANES), F32)] * 2
        + [pltpu.VMEM((tiles, nr // 4 + 24, LANES), F32)] * 2
        + [pltpu.VMEM((own_tiles, m3, LANES), F32)] * 2
        + [
            pltpu.VMEM((2, tiles1, size1, LANES), F32),
            pltpu.VMEM((2, tiles2, size2, LANES), F32),
            pltpu.VMEM((2, 2, stack, LANES), F32),
            pltpu.VMEM((stack, 256), F32),
            pltpu.VMEM((size1, tiles1 * LANES), F32),
            pltpu.VMEM((size2, tiles2 * LANES), F32),
            pltpu.VMEM((ns, beside, LANES), F32),
            pltpu.VMEM((ns, beside, LANES), F32),
            pltpu.VMEM((2, 1 + ns, OWN_TILES, 8, LANES), F32),
            pltpu.VMEM((2, 1 + ns, OWN_TILES, 8, LANES), F32),
            pltpu.VMEM((tiles2, nr // 4 + 16, LANES), F32),
            pltpu.VMEM((tiles2, nr // 2 + 16, LANES), F32),
            pltpu.VMEM((own_tiles, nr // 2 + 16, LANES), F32),
            pltpu.VMEM((1, LANES), F32),
            pltpu.VMEM((peers, 1, LANES), F32),
            pltpu.SemaphoreType.DMA((CHUNKS + 3,)),
            pltpu.SemaphoreType.DMA((len(given),)),
            pltpu.SemaphoreType.DMA((messages,)),
            pltpu.SemaphoreType.DMA((messages,)),
            pltpu.SemaphoreType.DMA(()),
            pltpu.SemaphoreType.DMA(()),
        ],
        compiler_params=pltpu.CompilerParams(collective_id=0, has_side_effects=True),
    )(scene_offset, scene_weight, band_gain, heights, scene_ids, *given)


def solution(mesh):
    placed = (P(("gy", "gz"), "gx"), P(("gy", "gz"), "gx"), P(), P(), P())
    shape = tuple(mesh.shape[name] for name in ("gx", "gy", "gz"))
    return jax.shard_map(
        functools.partial(local, shape), mesh=mesh, in_specs=placed,
        out_specs=P(("gy", "gz"), "gx"), check_vma=False,
    )
```

```python
import functools

import jax
import jax.numpy as jnp
import numpy as np
from jax import lax
from jax.experimental import pallas as pl
from jax.experimental.pallas import tpu as pltpu
from jax.sharding import PartitionSpec as P

F32, BF16 = jnp.float32, jnp.bfloat16
FAR = 1 << 20
HALO = 16
LANES = 128
LEVELS = 6
MIDDLE = (3, 4, 5)


def reach(count, levels):
    weights = np.ones(count >> levels, np.float64)
    for _ in range(levels):
        fine = np.zeros(2 * weights.size + 4, np.float64)
        for tap, value in zip(range(-2, 3), (0.0625, 0.25, 0.375, 0.25, 0.0625)):
            fine[2 + tap : 2 + tap + 2 * weights.size : 2] += value * weights
        weights = fine[2:-2]
    return weights


class Axis:
    def __init__(self, n, at, count):
        self.n, self.at, self.count = n, at, count

    def inside(self, index, level):
        place = index + self.at * (self.n >> level)
        return (place >= 0) & (place < self.count * (self.n >> level))

    def shrink(self, fine, coarse, level):
        far = np.abs(fine[:, None] - 2 * coarse[None, :])
        value = np.select([far == 0, far == 1, far == 2], [0.375, 0.25, 0.0625], 0.0)
        return value * self.inside(coarse, level)[None, :]

    def grow(self, coarse, fine, level):
        far = np.abs(2 * coarse[:, None] - fine[None, :])
        value = np.select([far == 0, far == 1, far == 2], [0.75, 0.5, 0.125], 0.0)
        return value * self.inside(fine, level)[None, :]

    def window(self, level, edge):
        return np.arange(-edge, (self.n >> level) + edge)

    def deep(self, lanes, shift=0):
        out = [x + shift * (self.n >> level) for level, x in zip((3, 4, 5, 6), self.out())]
        w4, w5 = self.window(4, 30), self.window(5, 14)
        to4 = self.shrink(lanes, w4, 4)
        to5 = to4 @ self.shrink(w4, w5, 5)
        same = (lanes[:, None] == out[0][None, :]) * self.inside(out[0], 3)[None, :]
        parts = [
            same * 1.0,
            self.shrink(lanes, out[1], 4),
            to4 @ self.shrink(w4, out[2], 5),
            to5 @ self.shrink(w5, out[3], 6),
        ]
        return np.concatenate(parts, axis=1) * self.inside(lanes, 3)[:, None]

    def out(self):
        low = -4
        return [low + np.arange(size) for size in self.sizes()]

    def sizes(self):
        return [self.n // 8 + 8, self.n // 16 + 8, self.n // 32 + 8, self.n // 64 + 16]

    def back(self):
        o3, o4, o5, o6 = self.out()
        w4, w5 = self.window(4, 4), self.window(5, 4)
        from4 = self.grow(w4, o3, 3)
        from5 = self.grow(w5, w4, 4) @ from4
        parts = [
            np.eye(o3.size) * self.inside(o3, 3)[None, :],
            self.grow(o4, o3, 3),
            self.grow(o5, w4, 4) @ from4,
            self.grow(o6, w5, 5) @ from5,
        ]
        return np.concatenate(parts, axis=0)

    def sums(self, level, place):
        weights = reach(self.count * (self.n >> level), LEVELS - level)
        place = place + self.at * (self.n >> level)
        return np.where((place >= 0) & (place < weights.size), weights[np.clip(place, 0, weights.size - 1)], 0.0)

    def ones(self, level):
        x = self.inside(self.window(6, 4), 6) * 1.0
        for k in range(5, level - 1, -1):
            x = x @ self.grow(self.window(k + 1, 4), self.window(k, 4), k)
        return x


def pad(x, shape):
    return np.pad(x, [(0, size - have) for size, have in zip(shape, x.shape)])


def halves(x):
    high = x.astype(np.float32).astype(jnp.bfloat16)
    low = (x - high.astype(np.float64)).astype(np.float32).astype(jnp.bfloat16)
    return high, low


def spaced(n):
    size = -(-(n + 8) // LANES) * LANES
    return np.concatenate([np.arange(-4, n + 4), np.full(size - n - 8, FAR)])


def col_tables(n, at, count):
    ax = Axis(n, at, count)
    shifts = [1 if at == 0 else -1] if count == 2 else [1, -1]
    lane = np.arange(LANES)
    own = np.arange(n)
    out1, out2 = spaced(n // 2), spaced(n // 4)
    w1, w2 = ax.window(1, 16), ax.window(2, 8)
    middle = np.isin(lane, MIDDLE)[None, :]
    s1, s2 = [], []
    for d in shifts:
        near = n - LANES + lane if d > 0 else lane
        over1, over2 = (lane - 4 + (n >> level if d > 0 else 0) for level in (1, 2))
        s1.append(ax.shrink(near, over1, 1) * middle)
        s2.append(ax.shrink(near, w1, 1) @ ax.shrink(w1, over2, 2) * middle)
    s1, s2 = (np.stack([np.stack([x, np.roll(x, LANES // 2, 1)]) for x in y]) for y in (s1, s2))
    o3 = ax.out()[0]
    to2 = ax.shrink(own, w1, 1)
    c03 = to2 @ ax.shrink(w1, w2, 2) @ ax.shrink(w2, o3, 3)
    c03 = np.concatenate([pad(x.astype(np.float64), (n, LANES)) for x in halves(c03)], axis=1)
    three = np.concatenate([o3, np.full(LANES - o3.size, FAR)])
    call = []
    for d in [0] + shifts:
        call.append([pad(x.astype(np.float64), (LANES, 256)) for x in halves(ax.deep(three, d))])
    call = np.stack([np.concatenate([x[k] for x in call], axis=1) for k in range(2)])
    back = ax.back()
    to0 = ax.grow(w2, w1, 1) @ ax.grow(w1, own, 0)
    ec0 = np.stack([pad(x.astype(np.float64), (256, n)) for x in halves(back @ ax.grow(o3, w2, 2) @ to0)])
    return dict(
        c1=ax.shrink(own, out1, 1), c2=to2 @ ax.shrink(w1, out2, 2), s1=s1, s2=s2, c03=c03, call=call,
        ec0=ec0, e1=ax.grow(out2, out1, 1), e0=ax.grow(out1, own, 0),
    ), dict(line=np.stack([ax.sums(0, own), ax.ones(0)[4:-4]]))


def row_tables(n, at, count):
    ax = Axis(n, at, count)
    o3 = ax.out()[0]
    deep = ax.deep(o3).T
    high, low = (x.astype(np.float64) for x in halves(deep))
    size6 = ax.sizes()[3]
    rall = np.concatenate([high, low[-size6:]], axis=0)
    rall = pad(rall, (-(-rall.shape[0] // 16) * 16, o3.size))
    back = ax.back()
    deep_rows = -(-o3.size // 16) * 16
    er = np.stack([pad(x.astype(np.float64), (deep_rows, x.shape[1])) for x in halves(back.T)])
    first = np.repeat(ax.sums(3, o3)[:, None], LANES, 1)
    w1, w2 = ax.window(1, 8), ax.window(2, 8)
    r012 = (ax.grow(o3, w2, 2) @ ax.grow(w2, w1, 1) @ ax.grow(w1, np.arange(n), 0)).T
    high, low = (pad(x.astype(np.float64), (n, deep_rows)) for x in halves(r012))
    r012 = np.concatenate([high, low, high], axis=1)
    second = np.repeat(pad(ax.ones(3), (deep_rows,))[:, None], LANES, 1)
    return dict(rall=rall, er=er, r012=r012), dict(first=first, second=second)


def tables(nr, nc, nx, blocks):
    def places(count):
        return (0, 1) if count == 2 else (0, 1, count - 1)

    cols = [col_tables(nc, at, nx) for at in places(nx)]
    rows = [row_tables(nr, at, blocks) for at in places(blocks)]

    def cast(x):
        return jnp.asarray(np.asarray(x, np.float32)).astype(BF16)

    def keep(x):
        return jnp.asarray(np.asarray(x, np.float32))

    out = {}
    for some in (cols, rows):
        for k in some[0][0]:
            out[k] = cast(np.stack([x[0][k] for x in some]))
        for k in some[0][1]:
            out[k] = keep(np.stack([x[1][k] for x in some]))
    return out


def merge(made):
    arrays, places = [], {}
    for at, group in enumerate(COLS + ROWS):
        lanes = max(made[name].shape[-1] for name in group)
        parts, start = [], 0
        for name in group:
            x = made[name]
            rows, width = x.shape[-2:]
            x = x.reshape(x.shape[0], -1, rows, width)
            tall = -(-rows // 16) * 16 if len(group) > 1 else rows
            x = jnp.pad(x, ((0, 0), (0, 0), (0, tall - rows), (0, lanes - width)))
            places[name] = (at, start, tall, rows, width)
            start += x.shape[1] * tall
            parts.append(x.reshape(x.shape[0], -1, lanes))
        arrays.append(jnp.concatenate(parts, axis=1))
    return arrays, places


def split(x):
    high = x.astype(BF16)
    return high, (x - high.astype(F32)).astype(BF16)


def dot(a, b):
    return jnp.dot(a, b, preferred_element_type=F32)


def right(x, c):
    high, low = split(x)
    return dot(high, c) + dot(low, c)


COLS = (("c03", "c2"), ("call", "e0"), ("c1", "e1"), ("s1", "s2"), ("ec0",), ("line",))
ROWS = (("rall", "er", "r012"), ("first", "second"))
OWN_TILES, SIDE_TILES = 5, 2
CHUNKS = 4


def kernel(
    sizes, places, off_hbm, wgt_hbm, gain_hbm, h_ref, s_ref, *rest
):
    nr, nc, nx, ny, nz, ns = sizes
    count = len(COLS) + len(ROWS)
    tables_hbm, rest = rest[:count], rest[count:]
    out_ref, rest = rest[0], rest[1:]
    tab, rest = rest[:count], rest[count:]
    (
        off_ref, wgt_ref, gain_ref, h_buf, s_buf, q0, num, den, out0, n1, d1, n2, d2, n3, d3,
        x1, x2, g, factor, y1, y2, side_s, side_r, edge_s, edge_r, z2b, z1b, wide, part, slots,
        own_sem, tab_sem, send0, recv0, psend, precv,
    ) = rest
    cx, cy, cz = lax.axis_index("gx"), lax.axis_index("gy"), lax.axis_index("gz")
    row = cy * nz + cz
    blocks = ny * nz
    own_tiles = nc // LANES
    t3 = nr // 8
    m3 = t3 + 8

    def kind(at, count):
        return at if count == 2 else jnp.where(at == 0, 0, jnp.where(at == count - 1, 2, 1))

    ct, rt = kind(cx, nx), kind(row, blocks)

    loads = []
    step = nr // CHUNKS
    for k in range(CHUNKS):
        rows = pl.ds(k * step, step)
        for a, (src, dst) in enumerate(((h_ref, h_buf), (s_ref, s_buf))):
            loads.append(
                pltpu.make_async_copy(
                    src.at[rows, :],
                    dst.at[pl.ds(HALO + k * step, step), pl.ds(0, nc)],
                    own_sem.at[k],
                )
            )
    small = [
        pltpu.make_async_copy(src, dst, own_sem.at[CHUNKS + a])
        for a, (src, dst) in enumerate(((off_hbm, off_ref), (wgt_hbm, wgt_ref), (gain_hbm, gain_ref)))
    ]
    fetch = [
        pltpu.make_async_copy(src.at[ct if i < len(COLS) else rt], tab[i], tab_sem.at[i])
        for i, src in enumerate(tables_hbm)
    ]
    ready = set()

    def await_tables(*names):
        for name in names:
            if places[name][0] not in ready:
                ready.add(places[name][0])
                fetch[places[name][0]].wait()

    def table(name, k=0, rows=None):
        at, start, tall, height, width = places[name]
        first, last = rows or (0, height)
        return tab[at][start + k * tall + first : start + k * tall + last, :width]

    for copy in loads[:2] + small + loads[2:]:
        copy.start()

    up, down = row > 0, row < blocks - 1
    send_row, recv_row = {0: None, 1: down, 2: up}, {0: None, 1: up, 2: down}
    if ns == 1:
        send_col, recv_col = {0: None, 1: None}, {0: None, 1: None}
        to_col = {0: cx, 1: 1 - cx}
        near_tile = {1: (1 - cx) * (own_tiles - 1)}
        into1, into2 = {1: (1 - cx) * (x1.shape[1] - 1)}, {1: (1 - cx) * (x2.shape[1] - 1)}
    else:
        send_col = {0: None, 1: cx < nx - 1, 2: cx > 0}
        recv_col = {0: None, 1: cx > 0, 2: cx < nx - 1}
        to_col = {0: cx, 1: cx + 1, 2: cx - 1}
        near_tile = {1: own_tiles - 1, 2: 0}
        into1, into2 = {1: 0, 2: x1.shape[1] - 1}, {1: 0, 2: x2.shape[1] - 1}
    kinds = [(rp, cp) for rp in (0, 1, 2) for cp in range(1 + ns) if rp or cp]

    def device(rp, cp):
        target = row + {0: 0, 1: 1, 2: -1}[rp]
        return {"gx": to_col[cp], "gy": target // nz, "gz": target % nz}

    def also(a, b):
        return b if a is None else a if b is None else jnp.logical_and(a, b)

    def sends(rp, cp):
        return also(send_row[rp], send_col[cp])

    def comes(rp, cp):
        return also(recv_row[rp], recv_col[cp])

    def given(flag, body):
        if flag is None:
            body()
        else:
            pl.when(flag)(body)

    everyone = nx * blocks
    me = row * nx + cx

    def peer(s):
        other = (me + s) % everyone
        line = other // nx
        return {"gx": other % nx, "gy": line // nz, "gz": line % nz}

    def places_of(at, count):
        return [jnp.where(at + d < count, at + d, at + d - count) for d in range(count)]

    def others(body):
        if everyone <= 64:
            xs, ys, zs = places_of(cx, nx), places_of(cy, ny), places_of(cz, nz)
            for s in range(1, everyone):
                line = s // nx
                body(s, {"gx": xs[s % nx], "gy": ys[line // nz], "gz": zs[line % nz]})
        else:
            def step_(s, carry):
                body(s, peer(s))
                return carry

            lax.fori_loop(1, everyone, step_, 0)

    barrier = pltpu.get_barrier_semaphore()
    others(lambda s, who: pl.semaphore_signal(barrier, inc=1, device_id=who))

    for copy in fetch:
        copy.start()

    zero = jnp.zeros((HALO, LANES), F32)
    for x in (num, den):
        for c in range(own_tiles):
            x[c, 0:HALO, :] = zero
            x[c, nr + HALO : nr + 2 * HALO, :] = zero
            x[c, nr + 2 * HALO :, :] = zero
    zero = jnp.zeros((8, LANES), F32)
    for x in (n1, d1, n2, d2):
        for c in range(own_tiles):
            x[c, 0:8, :] = zero
            x[c, x.shape[1] - 8 :, :] = zero

    def edge(i):
        rp, cp = kinds[i]
        if rp == 0:
            src, dst = side_s.at[cp - 1], side_r.at[cp - 1]
        else:
            place = pl.ds(0, OWN_TILES) if cp == 0 else pl.ds(0, SIDE_TILES)
            src, dst = edge_s.at[rp - 1, cp, place], edge_r.at[rp - 1, cp, place]
        return pltpu.make_async_remote_copy(
            src_ref=src, dst_ref=dst, send_sem=send0.at[i], recv_sem=recv0.at[i], device_id=device(rp, cp)
        )

    lane8 = lax.broadcasted_iota(jnp.int32, (8, LANES), 1)
    line8 = lax.broadcasted_iota(jnp.int32, (8, LANES), 0)

    def spread(table):
        line = jnp.zeros((8, LANES), F32)
        for i in range(table.shape[0]):
            line = jnp.where(lane8 == i, table[i], line)
        return line

    for copy in small:
        copy.wait()
    wgt_row = spread(wgt_ref)

    def tree(ids, table):
        values = [table[i] for i in range(table.shape[0])]
        bit = 1
        while len(values) > 1:
            mask = (ids & bit) != 0
            values = [jnp.where(mask, values[i + 1], values[i]) for i in range(0, len(values), 2)]
            bit *= 2
        return values[0]

    def level0(base, count, c):
        rows = pl.ds(base, count)
        ids = s_buf[rows, c * LANES : (c + 1) * LANES]
        weight = jnp.concatenate(
            [jnp.take_along_axis(wgt_row, ids[r : r + 8], axis=1) for r in range(0, count, 8)], axis=0
        )
        moved = h_buf[rows, c * LANES : (c + 1) * LANES] + tree(ids, off_ref)
        num[c, rows, :] = weight * moved
        den[c, rows, :] = weight
        return moved

    def summary(s, who):
        return pltpu.make_async_remote_copy(
            src_ref=part,
            dst_ref=slots.at[s - 1],
            send_sem=psend,
            recv_sem=precv,
            device_id=who,
        )

    def send_edges(wanted):
        for i, d in enumerate(kinds):
            if wanted(d):
                given(sends(*d), lambda: edge(i).start())

    lane1 = lax.broadcasted_iota(jnp.int32, (1, LANES), 1)

    def meet():
        with jax.named_scope("meet"):
            pl.semaphore_wait(barrier, everyone - 1)

        others(lambda s, who: summary(s, who).start())

    def taps(src, c, start, count):
        x = [src[c, pl.ds(start + a, count, stride=2), :] for a in range(-2, 3)]
        return 0.375 * x[2] + (0.25 * (x[1] + x[3]) + 0.0625 * (x[0] + x[4]))

    def hold(x, c, p, first):
        if first:
            ok = jnp.logical_or(line8 >= 4, up)
        else:
            ok = jnp.logical_or(line8 < 4, down)
        x[c, p : p + 8, :] = jnp.where(ok, x[c, p : p + 8, :], 0.0)

    last1, last2 = nr // 2 + 8, nr // 4 + 8

    def rows1(src, dst, c, p, count):
        dst[c, p : p + count, :] = taps(src, c, 2 * p - 8, count)

    def rows2(src, dst, c, p, count):
        dst[c, p : p + count, :] = taps(src, c, 2 * p - 12, count)

    pairs = ((num, n1, n2, n3), (den, d1, d2, d3))
    part1, part2 = step // 2, nr // 8

    def group1(k):
        count = part1 if k < CHUNKS - 1 else part1 + 16
        for src, one, _, _ in pairs:
            for c in range(own_tiles):
                rows1(src, one, c, 8 + k * part1, count)
                if k == 0:
                    hold(one, c, 8, True)
                if k == CHUNKS - 1:
                    hold(one, c, last1, False)

    def group2(k):
        for _, one, two, _ in pairs:
            for c in range(own_tiles):
                rows2(one, two, c, 8 + k * part2, part2 + 8 * k)
                hold(two, c, last2 if k else 8, not k)

    with jax.named_scope("level0"):
        for k in range(CHUNKS):
            both = pl.ds(0, 2 * step)
            pltpu.make_async_copy(h_ref.at[both, :], h_buf.at[both, pl.ds(0, nc)], own_sem.at[k]).wait()
            for c in range(own_tiles):
                q0[c, k * step : (k + 1) * step, :] = level0(HALO + k * step, step, c)
            if k:
                group1(k - 1)
            if k == CHUNKS - 1:
                group2(0)

    with jax.named_scope("rowpyr"):
        group1(CHUNKS - 1)
        group2(1)
        for _, _, two, three in pairs:
            for c in range(own_tiles):
                three[c] = taps(two, c, 4, m3)

    with jax.named_scope("sums"):
        await_tables("line", "first")
        flat = []
        for x in (n3, d3):
            y = sum(x[c] * table("line", 0, (0, 1))[:, c * LANES : (c + 1) * LANES] for c in range(own_tiles))
            y = jnp.sum(y * table("first"), axis=0, keepdims=True)
            flat.append(y + pltpu.roll(y, LANES // 2, axis=1))
        part[...] = jnp.where(lane1 < LANES // 2, flat[0], flat[1])

    early_half = cz < nz // 2 if nz > 1 else None
    if early_half is None:
        meet()
    else:
        pl.when(jnp.logical_not(early_half))(meet)
    def wide_of(x, rows, tiles):
        return jnp.concatenate([x[c, rows, :] for c in tiles], axis=1)

    own_range = range(own_tiles)
    size1, size2 = x1.shape[2], x2.shape[2]
    s3, s4, s5, s6 = (nr // 8 + 8, nr // 16 + 8, nr // 32 + 8, nr // 64 + 16)
    stack = s3 + s4 + s5 + s6
    tops = (0, s3, s3 + s4, s3 + s4 + s5)
    bottoms = tuple(top + (nr >> level) for top, level in zip(tops, (3, 4, 5, 6)))

    def level_of(shape, dim, cuts):
        index = lax.broadcasted_iota(jnp.int32, shape, dim)
        return sum((index >= cut).astype(jnp.int32) for cut in cuts)

    c3, c4, c5 = nc // 8 + 8, nc // 16 + 8, nc // 32 + 8
    lane_cuts = (c3, c3 + c4, c3 + c4 + c5)
    middle = jnp.logical_and(line8 >= MIDDLE[0], line8 <= MIDDLE[-1])

    def pack(n, d):
        return jnp.where(middle, n, pltpu.roll(d, 4, axis=0))

    def unpack(x):
        return jnp.where(middle, x, 0.0), jnp.where(middle, pltpu.roll(x, 4, axis=0), 0.0)

    def unpack_lanes(x):
        low = lax.broadcasted_iota(jnp.int32, x.shape, 1) < LANES // 2
        return jnp.where(low, x, 0.0), jnp.where(low, pltpu.roll(x, LANES // 2, axis=1), 0.0)

    with jax.named_scope("p3"):
        await_tables("c03", "rall", "call")
        x = jnp.concatenate([wide_of(n3, slice(None), own_range), wide_of(d3, slice(None), own_range)], axis=0)
        x = right(x, table("c03"))
        x = x[:, :LANES] + x[:, LANES:]
        high, low = split(jnp.concatenate([x[:m3], x[m3:]], axis=1))
        rall = table("rall")
        x = dot(rall, high) + dot(rall, low)
        x = jnp.concatenate([x[: stack - s6], x[stack - s6 : stack] + x[stack : stack + s6]], axis=0)
        def across(y):
            y = jnp.concatenate([y[:, :LANES], y[:, LANES:]], axis=0)
            high, low = split(y)
            return high, dot(high, table("call", 0)) + dot(low, table("call", 0))

        rows_all = x
        high, y = across(jnp.concatenate([x[f : f + 8] for firsts in (bottoms, tops) for f in firsts], axis=0))
        deep_ends = y + dot(high, table("call", 1))

    base_g = size1 + size2

    def own_lines(x1_, x2_, g_):
        last = x1_[2] + pltpu.roll(x2_[1], 8, axis=1) + pltpu.roll(g_[1], 16, axis=1)
        return [x1_[0], x1_[1], x2_[0], g_[0], last]

    def ends(x, c, last):
        return jnp.concatenate([x[c, 8:16, :], x[c, last : last + 8, :]], axis=0)

    with jax.named_scope("edge_own"):
        await_tables("s1", "s2", "c1", "c2")

        def own_ends(n, d, last, name):
            y = jnp.concatenate(
                [jnp.concatenate([ends(x, c, last) for c in own_range], axis=1) for x in (n, d)], axis=0
            )
            return right(y, table(name))

        own1, own2 = own_ends(n1, d1, last1, "c1"), own_ends(n2, d2, last2, "c2")

    with jax.named_scope("edge_side"):
        side_ends = []
        for k in range(1, 1 + ns):
            pair = []
            for n, d, last, name in ((n1, d1, last1, "s1"), (n2, d2, last2, "s2")):
                y = right(ends(n, near_tile[k], last), table(name, 2 * (k - 1)))
                pair.append(y + right(ends(d, near_tile[k], last), table(name, 2 * (k - 1) + 1)))
            side_ends.append(pair)

    def tile(x, at, c):
        return x[at : at + 8, c * LANES : (c + 1) * LANES]

    with jax.named_scope("g_pack"):
        for k in range(1 + ns):
            for rp in (1, 2):
                deep = []
                for a in range(2):
                    lines = []
                    for c in range(2):
                        index = lane8 + c * LANES
                        first = a * 64 + (rp - 1) * 32
                        lane = k * 256 + c * LANES
                        b = [deep_ends[first + 8 * l : first + 8 * l + 8, lane : lane + LANES] for l in range(4)]
                        lines.append(
                            jnp.where(
                                index < lane_cuts[0], b[0],
                                jnp.where(index < lane_cuts[1], b[1], jnp.where(index < lane_cuts[2], b[2], b[3])),
                            )
                        )
                    deep.append(lines)
                at = 8 * (2 - rp)
                if k == 0:
                    packed = [
                        own_lines(
                            [tile(own1, 16 * a + at, c) for c in range(3)],
                            [tile(own2, 16 * a + at, c) for c in range(2)],
                            deep[a],
                        )
                        for a in range(2)
                    ]
                    for t in range(OWN_TILES):
                        edge_s[rp - 1, 0, t] = pack(packed[0][t], packed[1][t])
                else:
                    lines = [y[at : at + 8] for y in side_ends[k - 1]]
                    edge_s[rp - 1, k, 0] = pack(deep[0][0], deep[1][0])
                    edge_s[rp - 1, k, 1] = (
                        lines[0] + pltpu.roll(lines[1], 8, axis=1)
                        + pltpu.roll(pack(deep[0][1], deep[1][1]), 16, axis=1)
                    )

    if early_half is not None:
        pl.when(early_half)(meet)

    with jax.named_scope("send"):
        send_edges(lambda d: d[0] != 0)

    body1, body2 = slice(8, 8 + size1), slice(8, 8 + size2)

    with jax.named_scope("g"):
        high, y = across(rows_all)
        tail = stack - 32
        more = [dot(high[a * stack + tail : (a + 1) * stack], table("call", 1)) for a in range(2)]
        for a in range(2):
            for c in range(2):
                for k in range(1 + ns):
                    lanes_ = slice(k * 256 + c * LANES, k * 256 + (c + 1) * LANES)
                    upper = y[a * stack : a * stack + tail, lanes_]
                    lower = y[a * stack + tail : (a + 1) * stack, lanes_] + more[a][:, lanes_]
                    if k == 0:
                        g[a, c, :tail] = upper
                        g[a, c, tail:] = lower
                    else:
                        first = base_g + (2 * a + c) * stack
                        side_s[k - 1, first : first + tail, :] = upper
                        side_s[k - 1, first + tail : first + stack, :] = lower

    with jax.named_scope("x_side"):
        for k in range(1, 1 + ns):
            for base, n, d, body, name in ((0, n1, d1, body1, "s1"), (size1, n2, d2, body2, "s2")):
                y = right(n[near_tile[k], body, :], table(name, 2 * (k - 1) + 0))
                y = y + right(d[near_tile[k], body, :], table(name, 2 * (k - 1) + 1))
                side_s[k - 1, base : base + y.shape[0], :] = y
        send_edges(lambda d: d[0] == 0)

    with jax.named_scope("x_own"):
        for n, d, body, name, dst in ((n1, d1, body1, "c1", x1), (n2, d2, body2, "c2", x2)):
            for a, y in enumerate((n, d)):
                y = right(wide_of(y, body, own_range), table(name))
                for c in range(dst.shape[1]):
                    dst[a, c] = y[:, c * LANES : (c + 1) * LANES]

    def ratio(n, d):
        return jnp.where(d > 0, n / d, 0.0)

    def await_edges(wanted):
        for i, d in enumerate(kinds):
            if wanted(d):
                given(sends(*d), lambda: edge(i).wait_send())
                given(comes(*d), lambda: edge(i).wait_recv())

    def q_rows(x, y, rows, gain):
        for c in range(x.shape[1]):
            y[rows, c * LANES : (c + 1) * LANES] = gain * ratio(x[0, c, rows, :], x[1, c, rows, :])

    gain1, gain2 = gain_ref[1] - gain_ref[0], gain_ref[2] - gain_ref[1]

    with jax.named_scope("w_side"):
        await_edges(lambda d: d[0] == 0)
    with jax.named_scope("add_side"):
        for k in range(1, 1 + ns):
            def add():
                for base, size, x, into in ((0, size1, x1, into1[k]), (size1, size2, x2, into2[k])):
                    more = unpack_lanes(side_r[k - 1, base : base + size, :])
                    for a in range(2):
                        x[a, into] = x[a, into] + more[a]
                for a in range(2):
                    for c in range(2):
                        base = base_g + (2 * a + c) * stack
                        g[a, c] = g[a, c] + side_r[k - 1, base : base + stack, :]

            given(recv_col[k], add)
    with jax.named_scope("q"):
        q_rows(x1, y1, slice(0, size1), gain1)
        q_rows(x2, y2, slice(0, size2), gain2)

    def grow_rows(src, dst, first, count):
        x, y, w = (src[first + k : first + k + count, :] for k in (1, 2, 3))
        dst[pl.ds(2 * first, count, stride=2), :] = 0.125 * (x + w) + 0.75 * y
        dst[pl.ds(2 * first + 1, count, stride=2), :] = 0.5 * (y + w)

    def block(x, c, p, first):
        ok = jnp.logical_or(line8 >= 4, up) if first else jnp.logical_or(line8 < 4, down)
        x[c, p : p + 8, :] = jnp.where(ok, x[c, p : p + 8, :], 0.0)

    tiles2 = range(x2.shape[1])

    def mask_ends():
        for c in tiles2:
            block(z1b, c, 0, True)
            block(z1b, c, nr // 2, False)

    gain0 = gain_ref[0]

    def rise(c, m, count):
        x, y, w = (wide[c, m + k : m + k + count, :] for k in (3, 4, 5))
        even, odd = pl.ds(2 * m, count, stride=2), pl.ds(2 * m + 1, count, stride=2)
        out0[c, even, :] = gain0 * q0[c, even, :] + (0.125 * (x + w) + 0.75 * y)
        out0[c, odd, :] = gain0 * q0[c, odd, :] + 0.5 * (y + w)

    def upward(parts):
        z = jnp.concatenate([jnp.concatenate([z1b[c, p, :] for c in tiles2], axis=1) for p in parts], axis=0)
        z = right(z, table("e1")) + jnp.concatenate([y1[p, :] for p in parts], axis=0)
        return right(z, table("e0"))

    with jax.named_scope("factor"):
        shape = (stack, 256)
        at_row = level_of(shape, 0, tops[1:])
        at_col = level_of(shape, 1, lane_cuts)
        gains = [gain_ref[level] - gain_ref[level - 1] for level in (3, 4, 5)] + [-gain_ref[5]]
        value = jnp.where(
            at_row == 0, gains[0], jnp.where(at_row == 1, gains[1], jnp.where(at_row == 2, gains[2], gains[3]))
        )
        factor[...] = jnp.where(at_row == at_col, value, 0.0)

    with jax.named_scope("base"):
        await_tables("e1", "e0")
        for c in tiles2:
            z2b[c] = y2[:, c * LANES : (c + 1) * LANES]
            grow_rows(z2b.at[c], z1b.at[c], 0, nr // 4 + 8)
        mask_ends()
        base = upward((slice(0, size1),))
        for c in own_range:
            wide[c] = base[:, c * LANES : (c + 1) * LANES]
        for c in own_range:
            for m in range(0, nr // 2, 32):
                rise(c, m, 32)

    with jax.named_scope("w_edges"):
        await_edges(lambda d: d[0] != 0)
        await_tables("ec0", "r012", "er", "second")
    packed_lanes = jnp.logical_and(lane8 % (LANES // 2) >= MIDDLE[0], lane8 % (LANES // 2) <= MIDDLE[-1])
    with jax.named_scope("edges"):
        for rp, at1, at2, firsts in ((1, 0, 0, tops), (2, nr // 2, nr // 4, bottoms)):
            for cp in range(1 + ns):

                def add():
                    got = edge_r.at[rp - 1, cp]
                    tail = unpack(got[OWN_TILES - 1]) if cp == 0 else None
                    if cp == 0:
                        adds1 = [unpack(got[0]), unpack(got[1]), [jnp.where(lane8 < 8, y, 0.0) for y in tail]]
                        adds2 = [
                            unpack(got[2]),
                            [jnp.where(lane8 < 8, pltpu.roll(y, LANES - 8, axis=1), 0.0) for y in tail],
                        ]
                        for x, at, adds in ((x1, at1, adds1), (x2, at2, adds2)):
                            for c, more in enumerate(adds):
                                for a in range(2):
                                    x[a, c, at : at + 8, :] = x[a, c, at : at + 8, :] + more[a]
                        deep = [unpack(got[3]), tail]
                    else:
                        y = got[1]
                        both = ((x1, at1, into1[cp], y), (x2, at2, into2[cp], pltpu.roll(y, LANES - 8, axis=1)))
                        for x, at, into, part_ in both:
                            for a, more in enumerate(unpack_lanes(jnp.where(packed_lanes, part_, 0.0))):
                                x[a, into, at : at + 8, :] = x[a, into, at : at + 8, :] + more
                        deep = [unpack(got[0]), unpack(y)]
                    deep[1] = [jnp.where(lane8 < 32, pltpu.roll(y, LANES - 16, axis=1), 0.0) for y in deep[1]]
                    for c in range(2):
                        for a, more in enumerate(deep[c]):
                            for f in firsts:
                                g[a, c, f : f + 8, :] = g[a, c, f : f + 8, :] + more

                given(comes(rp, cp), add)
        for x, y, at, gain in ((x1, y1, nr // 2, gain1), (x2, y2, nr // 4, gain2)):
            q_rows(x, y, slice(0, 8), gain)
            q_rows(x, y, slice(at, at + 8), gain)
    with jax.named_scope("fix"):
        for c in tiles2:
            for at in (0, nr // 4):
                z2b[c, at : at + 8, :] = y2[at : at + 8, c * LANES : (c + 1) * LANES]
                grow_rows(z2b.at[c], z1b.at[c], at, 8)
        mask_ends()
        parts = (slice(0, 16), slice(nr // 2, nr // 2 + 16))
        base = upward(parts)
        for c in own_range:
            for i, p in enumerate(parts):
                wide[c, p, :] = base[16 * i : 16 * i + 16, c * LANES : (c + 1) * LANES]
            rise(c, 0, 8)
            rise(c, nr // 2 - 8, 8)

    with jax.named_scope("deep"):
        n, d = (jnp.concatenate([g[a, 0], g[a, 1]], axis=1) for a in range(2))
        x = jnp.where(d > 0, factor[...] * (n / d), 0.0)
        high, low = split(x)
        er = [table("er", k) for k in (0, 1)]
        x = dot(er[0], high) + dot(er[0], low) + dot(er[1], high)
        high, low = split(x)
        x = dot(high, table("ec0")) + dot(low, table("ec0")) + dot(high, table("ec0", 1))

    with jax.named_scope("w_top"):
        everything = pltpu.make_async_copy(slots, slots, precv)
        everything.wait()
        pltpu.make_async_copy(slots, slots, psend).wait()
    with jax.named_scope("top"):
        total = part[...] + jnp.sum(slots[...], axis=0)
        top_sum = jnp.sum(jnp.where(lane1 < LANES // 2, total, 0.0), axis=1, keepdims=True)
        top_weight = jnp.sum(jnp.where(lane1 < LANES // 2, 0.0, total), axis=1, keepdims=True)
        top_line = (top_sum / top_weight) * table("line", 0, (1, 2))
        ones = table("second")
        x = x + jnp.concatenate(
            [ones * top_line[:, c * LANES : (c + 1) * LANES] for c in own_range], axis=1
        )
        high, low = split(x)
        x = jnp.concatenate([high, high, low], axis=0)
    with jax.named_scope("out"):
        for r in range(0, nr, 128):
            y = dot(table("r012", 0, (r, r + 128)), x)
            for c in own_range:
                out_ref[r : r + 128, c * LANES : (c + 1) * LANES] = (
                    out0[c, r : r + 128, :] + y[:, c * LANES : (c + 1) * LANES]
                )


def local(mesh_shape, heights, scene_ids, scene_offset, scene_weight, band_gain):
    nx, ny, nz = mesh_shape
    nr, nc = heights.shape
    ns = 1 if nx == 2 else 2
    made = tables(nr, nc, nx, ny * nz)
    given, places = merge(made)
    sizes = (nr, nc, nx, ny, nz, ns)
    ext = (nr + 2 * HALO, nc)
    tiles = nc // LANES
    own_tiles = tiles
    m3 = nr // 8 + 8
    size1, size2, stack = nr // 2 + 16, nr // 4 + 16, nr // 8 + nr // 16 + nr // 32 + nr // 64 + 40
    tiles1, tiles2 = nc // 2 // LANES + 1, nc // 4 // LANES + 1
    beside = size1 + size2 + 4 * stack
    peers = nx * ny * nz - 1
    messages = 3 * (1 + ns) - 1
    hbm = pl.BlockSpec(memory_space=pltpu.HBM)
    return pl.pallas_call(
        functools.partial(kernel, sizes, places),
        out_shape=pltpu.VMEM((nr, nc), F32),
        in_specs=[hbm] * (5 + len(given)),
        out_specs=pl.BlockSpec(memory_space=pltpu.VMEM),
        scratch_shapes=[pltpu.VMEM(x.shape[1:], x.dtype) for x in given]
        + [
            pltpu.SMEM(scene_offset.shape, F32),
            pltpu.SMEM(scene_weight.shape, F32),
            pltpu.SMEM(band_gain.shape, F32),
            pltpu.VMEM(ext, F32),
            pltpu.VMEM(ext, jnp.int32),
            pltpu.VMEM((own_tiles, nr, LANES), F32),
        ]
        + [pltpu.VMEM((tiles, nr + 3 * HALO, LANES), F32)] * 2
        + [pltpu.VMEM((own_tiles, nr, LANES), F32)]
        + [pltpu.VMEM((tiles, nr // 2 + 32, LANES), F32)] * 2
        + [pltpu.VMEM((tiles, nr // 4 + 24, LANES), F32)] * 2
        + [pltpu.VMEM((own_tiles, m3, LANES), F32)] * 2
        + [
            pltpu.VMEM((2, tiles1, size1, LANES), F32),
            pltpu.VMEM((2, tiles2, size2, LANES), F32),
            pltpu.VMEM((2, 2, stack, LANES), F32),
            pltpu.VMEM((stack, 256), F32),
            pltpu.VMEM((size1, tiles1 * LANES), F32),
            pltpu.VMEM((size2, tiles2 * LANES), F32),
            pltpu.VMEM((ns, beside, LANES), F32),
            pltpu.VMEM((ns, beside, LANES), F32),
            pltpu.VMEM((2, 1 + ns, OWN_TILES, 8, LANES), F32),
            pltpu.VMEM((2, 1 + ns, OWN_TILES, 8, LANES), F32),
            pltpu.VMEM((tiles2, nr // 4 + 16, LANES), F32),
            pltpu.VMEM((tiles2, nr // 2 + 16, LANES), F32),
            pltpu.VMEM((own_tiles, nr // 2 + 16, LANES), F32),
            pltpu.VMEM((1, LANES), F32),
            pltpu.VMEM((peers, 1, LANES), F32),
            pltpu.SemaphoreType.DMA((CHUNKS + 3,)),
            pltpu.SemaphoreType.DMA((len(given),)),
            pltpu.SemaphoreType.DMA((messages,)),
            pltpu.SemaphoreType.DMA((messages,)),
            pltpu.SemaphoreType.DMA(()),
            pltpu.SemaphoreType.DMA(()),
        ],
        compiler_params=pltpu.CompilerParams(collective_id=0, has_side_effects=True),
    )(scene_offset, scene_weight, band_gain, heights, scene_ids, *given)


def solution(mesh):
    placed = (P(("gy", "gz"), "gx"), P(("gy", "gz"), "gx"), P(), P(), P())
    shape = tuple(mesh.shape[name] for name in ("gx", "gy", "gz"))
    return jax.shard_map(
        functools.partial(local, shape), mesh=mesh, in_specs=placed,
        out_specs=P(("gy", "gz"), "gx"), check_vma=False,
    )
```

```python
import functools

import jax
import jax.numpy as jnp
import numpy as np
from jax import lax
from jax.experimental import pallas as pl
from jax.experimental.pallas import tpu as pltpu
from jax.sharding import PartitionSpec as P

F32, BF16 = jnp.float32, jnp.bfloat16
FAR = 1 << 20
HALO = 16
LANES = 128
LEVELS = 6
MIDDLE = (3, 4, 5)


def reach(count, levels):
    weights = np.ones(count >> levels, np.float64)
    for _ in range(levels):
        fine = np.zeros(2 * weights.size + 4, np.float64)
        for tap, value in zip(range(-2, 3), (0.0625, 0.25, 0.375, 0.25, 0.0625)):
            fine[2 + tap : 2 + tap + 2 * weights.size : 2] += value * weights
        weights = fine[2:-2]
    return weights


class Axis:
    def __init__(self, n, at, count):
        self.n, self.at, self.count = n, at, count

    def inside(self, index, level):
        place = index + self.at * (self.n >> level)
        return (place >= 0) & (place < self.count * (self.n >> level))

    def shrink(self, fine, coarse, level):
        far = np.abs(fine[:, None] - 2 * coarse[None, :])
        value = np.select([far == 0, far == 1, far == 2], [0.375, 0.25, 0.0625], 0.0)
        return value * self.inside(coarse, level)[None, :]

    def grow(self, coarse, fine, level):
        far = np.abs(2 * coarse[:, None] - fine[None, :])
        value = np.select([far == 0, far == 1, far == 2], [0.75, 0.5, 0.125], 0.0)
        return value * self.inside(fine, level)[None, :]

    def window(self, level, edge):
        return np.arange(-edge, (self.n >> level) + edge)

    def deep(self, lanes, shift=0):
        out = [x + shift * (self.n >> level) for level, x in zip((3, 4, 5, 6), self.out())]
        w4, w5 = self.window(4, 30), self.window(5, 14)
        to4 = self.shrink(lanes, w4, 4)
        to5 = to4 @ self.shrink(w4, w5, 5)
        same = (lanes[:, None] == out[0][None, :]) * self.inside(out[0], 3)[None, :]
        parts = [
            same * 1.0,
            self.shrink(lanes, out[1], 4),
            to4 @ self.shrink(w4, out[2], 5),
            to5 @ self.shrink(w5, out[3], 6),
        ]
        return np.concatenate(parts, axis=1) * self.inside(lanes, 3)[:, None]

    def out(self):
        low = -4
        return [low + np.arange(size) for size in self.sizes()]

    def sizes(self):
        return [self.n // 8 + 8, self.n // 16 + 8, self.n // 32 + 8, self.n // 64 + 16]

    def back(self):
        o3, o4, o5, o6 = self.out()
        w4, w5 = self.window(4, 4), self.window(5, 4)
        from4 = self.grow(w4, o3, 3)
        from5 = self.grow(w5, w4, 4) @ from4
        parts = [
            np.eye(o3.size) * self.inside(o3, 3)[None, :],
            self.grow(o4, o3, 3),
            self.grow(o5, w4, 4) @ from4,
            self.grow(o6, w5, 5) @ from5,
        ]
        return np.concatenate(parts, axis=0)

    def sums(self, level, place):
        weights = reach(self.count * (self.n >> level), LEVELS - level)
        place = place + self.at * (self.n >> level)
        return np.where((place >= 0) & (place < weights.size), weights[np.clip(place, 0, weights.size - 1)], 0.0)

    def ones(self, level):
        x = self.inside(self.window(6, 4), 6) * 1.0
        for k in range(5, level - 1, -1):
            x = x @ self.grow(self.window(k + 1, 4), self.window(k, 4), k)
        return x


def pad(x, shape):
    return np.pad(x, [(0, size - have) for size, have in zip(shape, x.shape)])


def halves(x):
    high = x.astype(np.float32).astype(jnp.bfloat16)
    low = (x - high.astype(np.float64)).astype(np.float32).astype(jnp.bfloat16)
    return high, low


def spaced(n):
    size = -(-(n + 8) // LANES) * LANES
    return np.concatenate([np.arange(-4, n + 4), np.full(size - n - 8, FAR)])


def col_tables(n, at, count):
    ax = Axis(n, at, count)
    shifts = [1 if at == 0 else -1] if count == 2 else [1, -1]
    lane = np.arange(LANES)
    own = np.arange(n)
    out1, out2 = spaced(n // 2), spaced(n // 4)
    w1, w2 = ax.window(1, 16), ax.window(2, 8)
    middle = np.isin(lane, MIDDLE)[None, :]
    s1, s2 = [], []
    for d in shifts:
        near = n - LANES + lane if d > 0 else lane
        over1, over2 = (lane - 4 + (n >> level if d > 0 else 0) for level in (1, 2))
        s1.append(ax.shrink(near, over1, 1) * middle)
        s2.append(ax.shrink(near, w1, 1) @ ax.shrink(w1, over2, 2) * middle)
    s1, s2 = (np.stack([np.stack([x, np.roll(x, LANES // 2, 1)]) for x in y]) for y in (s1, s2))
    o3 = ax.out()[0]
    to2 = ax.shrink(own, w1, 1)
    c03 = to2 @ ax.shrink(w1, w2, 2) @ ax.shrink(w2, o3, 3)
    c03 = np.concatenate([pad(x.astype(np.float64), (n, LANES)) for x in halves(c03)], axis=1)
    three = np.concatenate([o3, np.full(LANES - o3.size, FAR)])
    call = []
    for d in [0] + shifts:
        call.append([pad(x.astype(np.float64), (LANES, 256)) for x in halves(ax.deep(three, d))])
    high, low = (np.concatenate([x[k] for x in call], axis=1) for k in range(2))
    call = np.concatenate([high, high, low], axis=0)
    back = ax.back()
    to0 = ax.grow(w2, w1, 1) @ ax.grow(w1, own, 0)
    ec0 = np.stack([pad(x.astype(np.float64), (256, n)) for x in halves(back @ ax.grow(o3, w2, 2) @ to0)])
    return dict(
        c1=ax.shrink(own, out1, 1), c2=to2 @ ax.shrink(w1, out2, 2), s1=s1, s2=s2, c03=c03, call=call,
        ec0=ec0, e0=np.concatenate([ax.grow(out2, out1, 1) @ ax.grow(out1, own, 0), ax.grow(out1, own, 0)], axis=0),
    ), dict(line=np.stack([ax.sums(0, own), ax.ones(0)[4:-4]]))


def row_tables(n, at, count):
    ax = Axis(n, at, count)
    o3 = ax.out()[0]
    deep = ax.deep(o3).T
    high, low = (x.astype(np.float64) for x in halves(deep))
    size6 = ax.sizes()[3]
    rall = np.concatenate([high, low[-size6:]], axis=0)
    rall = pad(rall, (-(-rall.shape[0] // 16) * 16, -(-o3.size // 16) * 16))
    rall = np.concatenate([rall, rall], axis=1)
    back = ax.back()
    deep_rows = -(-o3.size // 16) * 16
    er = np.stack([pad(x.astype(np.float64), (deep_rows, x.shape[1])) for x in halves(back.T)])
    first = np.repeat(ax.sums(3, o3)[:, None], LANES, 1)
    w1, w2 = ax.window(1, 8), ax.window(2, 8)
    r012 = (ax.grow(o3, w2, 2) @ ax.grow(w2, w1, 1) @ ax.grow(w1, np.arange(n), 0)).T
    high, low = (pad(x.astype(np.float64), (n, deep_rows)) for x in halves(r012))
    r012 = np.concatenate([high, low, high], axis=1)
    second = np.repeat(pad(ax.ones(3), (deep_rows,))[:, None], LANES, 1)
    return dict(rall=rall, er=er, r012=r012), dict(first=first, second=second)


def tables(nr, nc, nx, blocks):
    def places(count):
        return (0, 1) if count == 2 else (0, 1, count - 1)

    cols = [col_tables(nc, at, nx) for at in places(nx)]
    rows = [row_tables(nr, at, blocks) for at in places(blocks)]

    def cast(x):
        return jnp.asarray(np.asarray(x, np.float32)).astype(BF16)

    def keep(x):
        return jnp.asarray(np.asarray(x, np.float32))

    out = {}
    for some in (cols, rows):
        for k in some[0][0]:
            out[k] = cast(np.stack([x[0][k] for x in some]))
        for k in some[0][1]:
            out[k] = keep(np.stack([x[1][k] for x in some]))
    return out


def merge(made):
    arrays, places = [], {}
    for at, group in enumerate(COLS + ROWS):
        lanes = max(made[name].shape[-1] for name in group)
        parts, start = [], 0
        for name in group:
            x = made[name]
            rows, width = x.shape[-2:]
            x = x.reshape(x.shape[0], -1, rows, width)
            tall = -(-rows // 16) * 16 if len(group) > 1 else rows
            x = jnp.pad(x, ((0, 0), (0, 0), (0, tall - rows), (0, lanes - width)))
            places[name] = (at, start, tall, rows, width)
            start += x.shape[1] * tall
            parts.append(x.reshape(x.shape[0], -1, lanes))
        arrays.append(jnp.concatenate(parts, axis=1))
    return arrays, places


def split(x):
    high = x.astype(BF16)
    return high, (x - high.astype(F32)).astype(BF16)


def dot(a, b):
    return jnp.dot(a, b, preferred_element_type=F32)


def right(x, c):
    high, low = split(x)
    return dot(high, c) + dot(low, c)


COLS = (("c03", "c2"), ("call", "e0"), ("c1",), ("s1", "s2"), ("ec0",), ("line",))
ROWS = (("rall", "er", "r012"), ("first", "second"))
OWN_TILES, SIDE_TILES = 5, 2
CHUNKS = 8


def kernel(
    sizes, places, off_hbm, wgt_hbm, gain_hbm, h_ref, s_ref, *rest
):
    nr, nc, nx, ny, nz, ns = sizes
    count = len(COLS) + len(ROWS)
    tables_hbm, rest = rest[:count], rest[count:]
    out_ref, rest = rest[0], rest[1:]
    tab, rest = rest[:count], rest[count:]
    (
        off_ref, wgt_ref, gain_ref, h_buf, s_buf, q0, num, den, out0, n1, d1, n2, d2, n3, d3,
        x1, x2, g, factor, y1, y2, side_s, side_r, edge_s, edge_r, z2b, z1b, wide, part, slots,
        own_sem, tab_sem, send0, recv0, psend, precv,
    ) = rest
    cx, cy, cz = lax.axis_index("gx"), lax.axis_index("gy"), lax.axis_index("gz")
    row = cy * nz + cz
    blocks = ny * nz
    own_tiles = nc // LANES
    t3 = nr // 8
    m3 = t3 + 8

    def kind(at, count):
        return at if count == 2 else jnp.where(at == 0, 0, jnp.where(at == count - 1, 2, 1))

    ct, rt = kind(cx, nx), kind(row, blocks)

    loads = []
    step = nr // CHUNKS
    for k in range(CHUNKS):
        rows = pl.ds(k * step, step)
        for a, (src, dst) in enumerate(((h_ref, h_buf), (s_ref, s_buf))):
            loads.append(
                pltpu.make_async_copy(
                    src.at[rows, :],
                    dst.at[pl.ds(HALO + k * step, step), pl.ds(0, nc)],
                    own_sem.at[k],
                )
            )
    small = [
        pltpu.make_async_copy(src, dst, own_sem.at[CHUNKS + a])
        for a, (src, dst) in enumerate(((off_hbm, off_ref), (wgt_hbm, wgt_ref), (gain_hbm, gain_ref)))
    ]
    fetch = [
        pltpu.make_async_copy(src.at[ct if i < len(COLS) else rt], tab[i], tab_sem.at[i])
        for i, src in enumerate(tables_hbm)
    ]
    ready = set()

    def await_tables(*names):
        for name in names:
            if places[name][0] not in ready:
                ready.add(places[name][0])
                fetch[places[name][0]].wait()

    def table(name, k=0, rows=None):
        at, start, tall, height, width = places[name]
        first, last = rows or (0, height)
        return tab[at][start + k * tall + first : start + k * tall + last, :width]

    for copy in loads[:2] + small + loads[2:]:
        copy.start()

    up, down = row > 0, row < blocks - 1
    send_row, recv_row = {0: None, 1: down, 2: up}, {0: None, 1: up, 2: down}
    if ns == 1:
        send_col, recv_col = {0: None, 1: None}, {0: None, 1: None}
        to_col = {0: cx, 1: 1 - cx}
        near_tile = {1: (1 - cx) * (own_tiles - 1)}
        into1, into2 = {1: (1 - cx) * (x1.shape[1] - 1)}, {1: (1 - cx) * (x2.shape[1] - 1)}
    else:
        send_col = {0: None, 1: cx < nx - 1, 2: cx > 0}
        recv_col = {0: None, 1: cx > 0, 2: cx < nx - 1}
        to_col = {0: cx, 1: cx + 1, 2: cx - 1}
        near_tile = {1: own_tiles - 1, 2: 0}
        into1, into2 = {1: 0, 2: x1.shape[1] - 1}, {1: 0, 2: x2.shape[1] - 1}
    kinds = [(rp, cp) for rp in (0, 1, 2) for cp in range(1 + ns) if rp or cp]

    def device(rp, cp):
        target = row + {0: 0, 1: 1, 2: -1}[rp]
        return {"gx": to_col[cp], "gy": target // nz, "gz": target % nz}

    def also(a, b):
        return b if a is None else a if b is None else jnp.logical_and(a, b)

    def sends(rp, cp):
        return also(send_row[rp], send_col[cp])

    def comes(rp, cp):
        return also(recv_row[rp], recv_col[cp])

    def given(flag, body):
        if flag is None:
            body()
        else:
            pl.when(flag)(body)

    everyone = nx * blocks
    me = row * nx + cx

    def peer(s):
        other = (me + s) % everyone
        line = other // nx
        return {"gx": other % nx, "gy": line // nz, "gz": line % nz}

    def places_of(at, count):
        return [jnp.where(at + d < count, at + d, at + d - count) for d in range(count)]

    def others(body):
        if everyone <= 64:
            xs, ys, zs = places_of(cx, nx), places_of(cy, ny), places_of(cz, nz)
            for s in range(1, everyone):
                line = s // nx
                body(s, {"gx": xs[s % nx], "gy": ys[line // nz], "gz": zs[line % nz]})
        else:
            def step_(s, carry):
                body(s, peer(s))
                return carry

            lax.fori_loop(1, everyone, step_, 0)

    barrier = pltpu.get_barrier_semaphore()
    others(lambda s, who: pl.semaphore_signal(barrier, inc=1, device_id=who))

    for copy in fetch:
        copy.start()

    zero = jnp.zeros((HALO, LANES), F32)
    for x in (num, den):
        for c in range(own_tiles):
            x[c, 0:HALO, :] = zero
            x[c, nr + HALO : nr + 2 * HALO, :] = zero
            x[c, nr + 2 * HALO :, :] = zero
    zero = jnp.zeros((8, LANES), F32)
    for x in (n1, d1, n2, d2):
        for c in range(own_tiles):
            x[c, 0:8, :] = zero
            x[c, x.shape[1] - 8 :, :] = zero

    for rp, cp in kinds:
        if rp and comes(rp, cp) is not None:
            @pl.when(jnp.logical_not(comes(rp, cp)))
            def _():
                edge_r[rp - 1, cp] = jnp.zeros((OWN_TILES, 8, LANES), F32)

    def edge(i):
        rp, cp = kinds[i]
        if rp == 0:
            src, dst = side_s.at[cp - 1], side_r.at[cp - 1]
        else:
            place = pl.ds(0, OWN_TILES) if cp == 0 else pl.ds(0, SIDE_TILES)
            src, dst = edge_s.at[rp - 1, cp, place], edge_r.at[rp - 1, cp, place]
        return pltpu.make_async_remote_copy(
            src_ref=src, dst_ref=dst, send_sem=send0.at[i], recv_sem=recv0.at[i], device_id=device(rp, cp)
        )

    lane8 = lax.broadcasted_iota(jnp.int32, (8, LANES), 1)
    line8 = lax.broadcasted_iota(jnp.int32, (8, LANES), 0)

    def spread(table):
        line = jnp.zeros((8, LANES), F32)
        for i in range(table.shape[0]):
            line = jnp.where(lane8 == i, table[i], line)
        return line

    for copy in small:
        copy.wait()
    wgt_row = spread(wgt_ref)

    def tree(ids, table):
        values = [table[i] for i in range(table.shape[0])]
        bit = 1
        while len(values) > 1:
            mask = (ids & bit) != 0
            values = [jnp.where(mask, values[i + 1], values[i]) for i in range(0, len(values), 2)]
            bit *= 2
        return values[0]

    def level0(base, count, c):
        rows = pl.ds(base, count)
        ids = s_buf[rows, c * LANES : (c + 1) * LANES]
        weight = jnp.concatenate(
            [jnp.take_along_axis(wgt_row, ids[r : r + 8], axis=1) for r in range(0, count, 8)], axis=0
        )
        moved = h_buf[rows, c * LANES : (c + 1) * LANES] + tree(ids, off_ref)
        num[c, rows, :] = weight * moved
        den[c, rows, :] = weight
        return moved

    def summary(s, who):
        return pltpu.make_async_remote_copy(
            src_ref=part,
            dst_ref=slots.at[s - 1],
            send_sem=psend,
            recv_sem=precv,
            device_id=who,
        )

    def send_edges(wanted):
        for i, d in enumerate(kinds):
            if wanted(d):
                given(sends(*d), lambda: edge(i).start())

    lane1 = lax.broadcasted_iota(jnp.int32, (1, LANES), 1)

    def meet():
        with jax.named_scope("meet"):
            pl.semaphore_wait(barrier, everyone - 1)

        others(lambda s, who: summary(s, who).start())

    def taps(src, c, start, count):
        x = [src[c, pl.ds(start + a, count, stride=2), :] for a in range(-2, 3)]
        return 0.375 * x[2] + (0.25 * (x[1] + x[3]) + 0.0625 * (x[0] + x[4]))

    def hold(x, c, p, first):
        if first:
            ok = jnp.logical_or(line8 >= 4, up)
        else:
            ok = jnp.logical_or(line8 < 4, down)
        x[c, p : p + 8, :] = jnp.where(ok, x[c, p : p + 8, :], 0.0)

    last1, last2 = nr // 2 + 8, nr // 4 + 8

    def rows1(src, dst, c, p, count):
        dst[c, p : p + count, :] = taps(src, c, 2 * p - 8, count)

    def rows2(src, dst, c, p, count):
        dst[c, p : p + count, :] = taps(src, c, 2 * p - 12, count)

    pairs = ((num, n1, n2, n3), (den, d1, d2, d3))
    part1, part2 = step // 2, nr // 8

    def group1(k):
        count = part1 if k < CHUNKS - 1 else part1 + 16
        for src, one, _, _ in pairs:
            for c in range(own_tiles):
                rows1(src, one, c, 8 + k * part1, count)
                if k == 0:
                    hold(one, c, 8, True)
                if k == CHUNKS - 1:
                    hold(one, c, last1, False)

    def group2(k):
        for _, one, two, _ in pairs:
            for c in range(own_tiles):
                rows2(one, two, c, 8 + k * part2, part2 + 8 * k)
                hold(two, c, last2 if k else 8, not k)

    with jax.named_scope("level0"):
        for k in range(CHUNKS):
            both = pl.ds(0, 2 * step)
            pltpu.make_async_copy(h_ref.at[both, :], h_buf.at[both, pl.ds(0, nc)], own_sem.at[k]).wait()
            for c in range(own_tiles):
                q0[c, k * step : (k + 1) * step, :] = level0(HALO + k * step, step, c)
            if k:
                group1(k - 1)
            if k == CHUNKS - 1:
                group2(0)

    with jax.named_scope("rowpyr"):
        group1(CHUNKS - 1)
        group2(1)
        for _, _, two, three in pairs:
            for c in range(own_tiles):
                three[c] = taps(two, c, 4, m3)

    with jax.named_scope("sums"):
        await_tables("line", "first")
        flat = []
        for x in (n3, d3):
            y = sum(x[c] * table("line", 0, (0, 1))[:, c * LANES : (c + 1) * LANES] for c in range(own_tiles))
            y = jnp.sum(y * table("first"), axis=0, keepdims=True)
            flat.append(y + pltpu.roll(y, LANES // 2, axis=1))
        part[...] = jnp.where(lane1 < LANES // 2, flat[0], flat[1])

    early_half = jnp.logical_and(cz > 0, cz < nz // 2) if nz > 1 else None
    first_plane = cz == 0
    if early_half is None:
        meet()
    else:
        pl.when(cz >= nz // 2)(meet)
    def wide_of(x, rows, tiles):
        return jnp.concatenate([x[c, rows, :] for c in tiles], axis=1)

    own_range = range(own_tiles)
    size1, size2 = x1.shape[2], x2.shape[2]
    s3, s4, s5, s6 = (nr // 8 + 8, nr // 16 + 8, nr // 32 + 8, nr // 64 + 16)
    stack = s3 + s4 + s5 + s6
    tops = (0, s3, s3 + s4, s3 + s4 + s5)
    bottoms = tuple(top + (nr >> level) for top, level in zip(tops, (3, 4, 5, 6)))

    def level_of(shape, dim, cuts):
        index = lax.broadcasted_iota(jnp.int32, shape, dim)
        return sum((index >= cut).astype(jnp.int32) for cut in cuts)

    c3, c4, c5 = nc // 8 + 8, nc // 16 + 8, nc // 32 + 8
    lane_cuts = (c3, c3 + c4, c3 + c4 + c5)
    middle = jnp.logical_and(line8 >= MIDDLE[0], line8 <= MIDDLE[-1])

    def pack(n, d):
        return jnp.where(middle, n, pltpu.roll(d, 4, axis=0))

    def unpack(x):
        return [jnp.where(middle, x, 0.0), jnp.where(middle, pltpu.roll(x, 4, axis=0), 0.0)]

    def unpack_lanes(x):
        low = lax.broadcasted_iota(jnp.int32, x.shape, 1) < LANES // 2
        return jnp.where(low, x, 0.0), jnp.where(low, pltpu.roll(x, LANES // 2, axis=1), 0.0)

    with jax.named_scope("p3"):
        await_tables("c03", "rall", "call")
        x = jnp.concatenate([wide_of(n3, slice(None), own_range), wide_of(d3, slice(None), own_range)], axis=0)
        x = right(x, table("c03"))
        x = x[:, :LANES] + x[:, LANES:]
        high, low = split(jnp.concatenate([x[:m3], x[m3:]], axis=1))
        gap = jnp.zeros((-m3 % 16, 2 * LANES), BF16)
        x = dot(table("rall"), jnp.concatenate([high, gap, low, gap], axis=0))
        x = jnp.concatenate([x[: stack - s6], x[stack - s6 : stack] + x[stack : stack + s6]], axis=0)
        def across(y):
            y = jnp.concatenate([y[:, :LANES], y[:, LANES:]], axis=0)
            high, low = split(y)
            return high, dot(jnp.concatenate([high, low], axis=1), table("call", 0, (0, 2 * LANES)))

        rows_all = x
        high, y = across(jnp.concatenate([x[f : f + 8] for firsts in (bottoms, tops) for f in firsts], axis=0))
        deep_ends = y + dot(high, table("call", 0, (2 * LANES, 3 * LANES)))

    base_g = size1 + size2

    def own_lines(x1_, x2_, g_):
        last = x1_[2] + pltpu.roll(x2_[1], 8, axis=1) + pltpu.roll(g_[1], 16, axis=1)
        return [x1_[0], x1_[1], x2_[0], g_[0], last]

    def ends(x, c, last):
        return jnp.concatenate([x[c, 8:16, :], x[c, last : last + 8, :]], axis=0)

    with jax.named_scope("edge_own"):
        await_tables("s1", "s2", "c1", "c2")

        def own_ends(n, d, last, name):
            y = jnp.concatenate(
                [jnp.concatenate([ends(x, c, last) for c in own_range], axis=1) for x in (n, d)], axis=0
            )
            return right(y, table(name))

        own1, own2 = own_ends(n1, d1, last1, "c1"), own_ends(n2, d2, last2, "c2")

    with jax.named_scope("edge_side"):
        side_ends = []
        for k in range(1, 1 + ns):
            pair = []
            for n, d, last, name in ((n1, d1, last1, "s1"), (n2, d2, last2, "s2")):
                y = right(ends(n, near_tile[k], last), table(name, 2 * (k - 1)))
                pair.append(y + right(ends(d, near_tile[k], last), table(name, 2 * (k - 1) + 1)))
            side_ends.append(pair)

    def tile(x, at, c):
        return x[at : at + 8, c * LANES : (c + 1) * LANES]

    with jax.named_scope("g_pack"):
        for k in range(1 + ns):
            for rp in (1, 2):
                deep = []
                for a in range(2):
                    lines = []
                    for c in range(2):
                        index = lane8 + c * LANES
                        first = a * 64 + (rp - 1) * 32
                        lane = k * 256 + c * LANES
                        b = [deep_ends[first + 8 * l : first + 8 * l + 8, lane : lane + LANES] for l in range(4)]
                        lines.append(
                            jnp.where(
                                index < lane_cuts[0], b[0],
                                jnp.where(index < lane_cuts[1], b[1], jnp.where(index < lane_cuts[2], b[2], b[3])),
                            )
                        )
                    deep.append(lines)
                at = 8 * (2 - rp)
                if k == 0:
                    packed = [
                        own_lines(
                            [tile(own1, 16 * a + at, c) for c in range(3)],
                            [tile(own2, 16 * a + at, c) for c in range(2)],
                            deep[a],
                        )
                        for a in range(2)
                    ]
                    for t in range(OWN_TILES):
                        edge_s[rp - 1, 0, t] = pack(packed[0][t], packed[1][t])
                else:
                    lines = [y[at : at + 8] for y in side_ends[k - 1]]
                    edge_s[rp - 1, k, 0] = pack(deep[0][0], deep[1][0])
                    edge_s[rp - 1, k, 1] = (
                        lines[0] + pltpu.roll(lines[1], 8, axis=1)
                        + pltpu.roll(pack(deep[0][1], deep[1][1]), 16, axis=1)
                    )

    if early_half is not None:
        pl.when(early_half)(meet)

    with jax.named_scope("send"):
        if early_half is None:
            send_edges(lambda d: d[0] != 0)
        else:
            pl.when(jnp.logical_not(first_plane))(lambda: send_edges(lambda d: d[0] != 0))

    body1, body2 = slice(8, 8 + size1), slice(8, 8 + size2)

    with jax.named_scope("g"):
        high, y = across(rows_all)
        tail = stack - 32
        more = [dot(high[a * stack + tail : (a + 1) * stack], table("call", 0, (2 * LANES, 3 * LANES))) for a in range(2)]
        for a in range(2):
            for c in range(2):
                for k in range(1 + ns):
                    lanes_ = slice(k * 256 + c * LANES, k * 256 + (c + 1) * LANES)
                    upper = y[a * stack : a * stack + tail, lanes_]
                    lower = y[a * stack + tail : (a + 1) * stack, lanes_] + more[a][:, lanes_]
                    if k == 0:
                        g[a, c, :tail] = upper
                        g[a, c, tail:] = lower
                    else:
                        first = base_g + (2 * a + c) * stack
                        side_s[k - 1, first : first + tail, :] = upper
                        side_s[k - 1, first + tail : first + stack, :] = lower

    with jax.named_scope("x_side"):
        for k in range(1, 1 + ns):
            for base, n, d, body, name in ((0, n1, d1, body1, "s1"), (size1, n2, d2, body2, "s2")):
                y = right(n[near_tile[k], body, :], table(name, 2 * (k - 1) + 0))
                y = y + right(d[near_tile[k], body, :], table(name, 2 * (k - 1) + 1))
                side_s[k - 1, base : base + y.shape[0], :] = y
        if early_half is None:
            send_edges(lambda d: d[0] == 0)
        else:
            pl.when(jnp.logical_not(first_plane))(lambda: send_edges(lambda d: d[0] == 0))

    with jax.named_scope("x_own"):
        for n, d, body, name, dst in ((n1, d1, body1, "c1", x1), (n2, d2, body2, "c2", x2)):
            for a, y in enumerate((n, d)):
                y = right(wide_of(y, body, own_range), table(name))
                for c in range(dst.shape[1]):
                    dst[a, c] = y[:, c * LANES : (c + 1) * LANES]

    if early_half is not None:

        @pl.when(first_plane)
        def _():
            meet()
            send_edges(lambda d: True)

    def ratio(n, d):
        return jnp.where(d > 0, n / d, 0.0)

    def await_edges(wanted):
        for i, d in enumerate(kinds):
            if wanted(d):
                given(sends(*d), lambda: edge(i).wait_send())
                given(comes(*d), lambda: edge(i).wait_recv())

    def q_rows(x, y, rows, gain):
        for c in range(x.shape[1]):
            y[rows, c * LANES : (c + 1) * LANES] = gain * ratio(x[0, c, rows, :], x[1, c, rows, :])

    gain1, gain2 = gain_ref[1] - gain_ref[0], gain_ref[2] - gain_ref[1]

    with jax.named_scope("w_side"):
        await_edges(lambda d: d[0] == 0)
    with jax.named_scope("add_side"):
        for k in range(1, 1 + ns):
            def add():
                for base, size, x, into in ((0, size1, x1, into1[k]), (size1, size2, x2, into2[k])):
                    more = unpack_lanes(side_r[k - 1, base : base + size, :])
                    for a in range(2):
                        x[a, into] = x[a, into] + more[a]
                for a in range(2):
                    for c in range(2):
                        base = base_g + (2 * a + c) * stack
                        g[a, c] = g[a, c] + side_r[k - 1, base : base + stack, :]

            given(recv_col[k], add)
    with jax.named_scope("q"):
        q_rows(x1, y1, slice(0, size1), gain1)
        q_rows(x2, y2, slice(0, size2), gain2)

    def grow_rows(src, dst, first, count):
        x, y, w = (src[first + k : first + k + count, :] for k in (1, 2, 3))
        dst[pl.ds(2 * first, count, stride=2), :] = 0.125 * (x + w) + 0.75 * y
        dst[pl.ds(2 * first + 1, count, stride=2), :] = 0.5 * (y + w)

    def block(x, c, p, first):
        ok = jnp.logical_or(line8 >= 4, up) if first else jnp.logical_or(line8 < 4, down)
        x[c, p : p + 8, :] = jnp.where(ok, x[c, p : p + 8, :], 0.0)

    tiles2 = range(x2.shape[1])

    def mask_ends():
        for c in tiles2:
            block(z1b, c, 0, True)
            block(z1b, c, nr // 2, False)

    gain0 = gain_ref[0]

    def rise(c, m, count):
        x, y, w = (wide[c, m + k : m + k + count, :] for k in (3, 4, 5))
        even, odd = pl.ds(2 * m, count, stride=2), pl.ds(2 * m + 1, count, stride=2)
        out0[c, even, :] = gain0 * q0[c, even, :] + (0.125 * (x + w) + 0.75 * y)
        out0[c, odd, :] = gain0 * q0[c, odd, :] + 0.5 * (y + w)

    def upward(parts):
        z = [jnp.concatenate([z1b[c, p, :] for p in parts], axis=0) for c in tiles2]
        z.append(jnp.concatenate([y1[p, :] for p in parts], axis=0))
        return right(jnp.concatenate(z, axis=1), table("e0"))

    with jax.named_scope("factor"):
        shape = (stack, 256)
        at_row = level_of(shape, 0, tops[1:])
        at_col = level_of(shape, 1, lane_cuts)
        gains = [gain_ref[level] - gain_ref[level - 1] for level in (3, 4, 5)] + [-gain_ref[5]]
        value = jnp.where(
            at_row == 0, gains[0], jnp.where(at_row == 1, gains[1], jnp.where(at_row == 2, gains[2], gains[3]))
        )
        factor[...] = jnp.where(at_row == at_col, value, 0.0)

    with jax.named_scope("base"):
        await_tables("e0")
        for c in tiles2:
            z2b[c] = y2[:, c * LANES : (c + 1) * LANES]
            grow_rows(z2b.at[c], z1b.at[c], 0, nr // 4 + 8)
        mask_ends()
        base = upward((slice(0, size1),))
        for c in own_range:
            wide[c] = base[:, c * LANES : (c + 1) * LANES]
        for c in own_range:
            for m in range(0, nr // 2, 32):
                rise(c, m, 32)

    with jax.named_scope("w_edges"):
        await_edges(lambda d: d[0] != 0)
        await_tables("ec0", "r012", "er", "second")
    packed_lanes = jnp.logical_and(lane8 % (LANES // 2) >= MIDDLE[0], lane8 % (LANES // 2) <= MIDDLE[-1])
    with jax.named_scope("edges"):
        for rp, at1, at2, firsts in ((1, 0, 0, tops), (2, nr // 2, nr // 4, bottoms)):
            def moved_to(y, by, ok):
                return [jnp.where(ok, pltpu.roll(z, LANES - by, axis=1), 0.0) for z in y]

            got = edge_r.at[rp - 1, 0]
            tail = unpack(got[OWN_TILES - 1])
            adds1 = [unpack(got[0]), unpack(got[1]), [jnp.where(lane8 < 8, y, 0.0) for y in tail]]
            adds2 = [unpack(got[2]), moved_to(tail, 8, lane8 < 8)]
            deep = [unpack(got[3]), moved_to(tail, 16, lane8 < 32)]
            for cp in range(1, 1 + ns):
                y = edge_r[rp - 1, cp, 1]
                for a, more in enumerate(unpack(edge_r[rp - 1, cp, 0])):
                    deep[0][a] = deep[0][a] + more
                for a, more in enumerate(moved_to(unpack(y), 16, lane8 < 32)):
                    deep[1][a] = deep[1][a] + more
            for x, at, adds in ((x1, at1, adds1), (x2, at2, adds2)):
                for c, more in enumerate(adds):
                    for a in range(2):
                        x[a, c, at : at + 8, :] = x[a, c, at : at + 8, :] + more[a]
            for cp in range(1, 1 + ns):
                y = edge_r[rp - 1, cp, 1]
                for x, at, into, z in ((x1, at1, into1[cp], y), (x2, at2, into2[cp], pltpu.roll(y, LANES - 8, axis=1))):
                    for a, more in enumerate(unpack_lanes(jnp.where(packed_lanes, z, 0.0))):
                        x[a, into, at : at + 8, :] = x[a, into, at : at + 8, :] + more
            for c in range(2):
                for a in range(2):
                    for f in firsts:
                        g[a, c, f : f + 8, :] = g[a, c, f : f + 8, :] + deep[c][a]
        for x, y, at, gain in ((x1, y1, nr // 2, gain1), (x2, y2, nr // 4, gain2)):
            q_rows(x, y, slice(0, 8), gain)
            q_rows(x, y, slice(at, at + 8), gain)
    with jax.named_scope("fix"):
        for c in tiles2:
            for at in (0, nr // 4):
                z2b[c, at : at + 8, :] = y2[at : at + 8, c * LANES : (c + 1) * LANES]
                grow_rows(z2b.at[c], z1b.at[c], at, 8)
        mask_ends()
        parts = (slice(0, 16), slice(nr // 2, nr // 2 + 16))
        base = upward(parts)
        for c in own_range:
            for i, p in enumerate(parts):
                wide[c, p, :] = base[16 * i : 16 * i + 16, c * LANES : (c + 1) * LANES]
            rise(c, 0, 8)
            rise(c, nr // 2 - 8, 8)

    with jax.named_scope("deep"):
        n, d = (jnp.concatenate([g[a, 0], g[a, 1]], axis=1) for a in range(2))
        x = jnp.where(d > 0, factor[...] * (n / d), 0.0)
        high, low = split(x)
        er = [table("er", k) for k in (0, 1)]
        x = dot(er[0], high) + dot(er[0], low) + dot(er[1], high)
        high, low = split(x)
        x = dot(high, table("ec0")) + dot(low, table("ec0")) + dot(high, table("ec0", 1))

    with jax.named_scope("w_top"):
        everything = pltpu.make_async_copy(slots, slots, precv)
        everything.wait()
        pltpu.make_async_copy(slots, slots, psend).wait()
    with jax.named_scope("top"):
        total = part[...] + jnp.sum(slots[...], axis=0)
        top_sum = jnp.sum(jnp.where(lane1 < LANES // 2, total, 0.0), axis=1, keepdims=True)
        top_weight = jnp.sum(jnp.where(lane1 < LANES // 2, 0.0, total), axis=1, keepdims=True)
        top_line = (top_sum / top_weight) * table("line", 0, (1, 2))
        ones = table("second")
        x = x + jnp.concatenate(
            [ones * top_line[:, c * LANES : (c + 1) * LANES] for c in own_range], axis=1
        )
        high, low = split(x)
        x = jnp.concatenate([high, high, low], axis=0)
    with jax.named_scope("out"):
        for r in range(0, nr, 128):
            y = dot(table("r012", 0, (r, r + 128)), x)
            for c in own_range:
                out_ref[r : r + 128, c * LANES : (c + 1) * LANES] = (
                    out0[c, r : r + 128, :] + y[:, c * LANES : (c + 1) * LANES]
                )


def local(mesh_shape, heights, scene_ids, scene_offset, scene_weight, band_gain):
    nx, ny, nz = mesh_shape
    nr, nc = heights.shape
    ns = 1 if nx == 2 else 2
    made = tables(nr, nc, nx, ny * nz)
    given, places = merge(made)
    sizes = (nr, nc, nx, ny, nz, ns)
    ext = (nr + 2 * HALO, nc)
    tiles = nc // LANES
    own_tiles = tiles
    m3 = nr // 8 + 8
    size1, size2, stack = nr // 2 + 16, nr // 4 + 16, nr // 8 + nr // 16 + nr // 32 + nr // 64 + 40
    tiles1, tiles2 = nc // 2 // LANES + 1, nc // 4 // LANES + 1
    beside = size1 + size2 + 4 * stack
    peers = nx * ny * nz - 1
    messages = 3 * (1 + ns) - 1
    hbm = pl.BlockSpec(memory_space=pltpu.HBM)
    return pl.pallas_call(
        functools.partial(kernel, sizes, places),
        out_shape=pltpu.VMEM((nr, nc), F32),
        in_specs=[hbm] * (5 + len(given)),
        out_specs=pl.BlockSpec(memory_space=pltpu.VMEM),
        scratch_shapes=[pltpu.VMEM(x.shape[1:], x.dtype) for x in given]
        + [
            pltpu.SMEM(scene_offset.shape, F32),
            pltpu.SMEM(scene_weight.shape, F32),
            pltpu.SMEM(band_gain.shape, F32),
            pltpu.VMEM(ext, F32),
            pltpu.VMEM(ext, jnp.int32),
            pltpu.VMEM((own_tiles, nr, LANES), F32),
        ]
        + [pltpu.VMEM((tiles, nr + 3 * HALO, LANES), F32)] * 2
        + [pltpu.VMEM((own_tiles, nr, LANES), F32)]
        + [pltpu.VMEM((tiles, nr // 2 + 32, LANES), F32)] * 2
        + [pltpu.VMEM((tiles, nr // 4 + 24, LANES), F32)] * 2
        + [pltpu.VMEM((own_tiles, m3, LANES), F32)] * 2
        + [
            pltpu.VMEM((2, tiles1, size1, LANES), F32),
            pltpu.VMEM((2, tiles2, size2, LANES), F32),
            pltpu.VMEM((2, 2, stack, LANES), F32),
            pltpu.VMEM((stack, 256), F32),
            pltpu.VMEM((size1, tiles1 * LANES), F32),
            pltpu.VMEM((size2, tiles2 * LANES), F32),
            pltpu.VMEM((ns, beside, LANES), F32),
            pltpu.VMEM((ns, beside, LANES), F32),
            pltpu.VMEM((2, 1 + ns, OWN_TILES, 8, LANES), F32),
            pltpu.VMEM((2, 1 + ns, OWN_TILES, 8, LANES), F32),
            pltpu.VMEM((tiles2, nr // 4 + 16, LANES), F32),
            pltpu.VMEM((tiles2, nr // 2 + 16, LANES), F32),
            pltpu.VMEM((own_tiles, nr // 2 + 16, LANES), F32),
            pltpu.VMEM((1, LANES), F32),
            pltpu.VMEM((peers, 1, LANES), F32),
            pltpu.SemaphoreType.DMA((CHUNKS + 3,)),
            pltpu.SemaphoreType.DMA((len(given),)),
            pltpu.SemaphoreType.DMA((messages,)),
            pltpu.SemaphoreType.DMA((messages,)),
            pltpu.SemaphoreType.DMA(()),
            pltpu.SemaphoreType.DMA(()),
        ],
        compiler_params=pltpu.CompilerParams(collective_id=0, has_side_effects=True),
    )(scene_offset, scene_weight, band_gain, heights, scene_ids, *given)


def solution(mesh):
    placed = (P(("gy", "gz"), "gx"), P(("gy", "gz"), "gx"), P(), P(), P())
    shape = tuple(mesh.shape[name] for name in ("gx", "gy", "gz"))
    return jax.shard_map(
        functools.partial(local, shape), mesh=mesh, in_specs=placed,
        out_specs=P(("gy", "gz"), "gx"), check_vma=False,
    )
```

```python
import functools

import jax
import jax.numpy as jnp
import numpy as np
from jax import lax
from jax.experimental import pallas as pl
from jax.experimental.pallas import tpu as pltpu
from jax.sharding import PartitionSpec as P

F32, BF16 = jnp.float32, jnp.bfloat16
FAR = 1 << 20
HALO = 16
LANES = 128
LEVELS = 6
MIDDLE = (3, 4, 5)


def reach(count, levels):
    weights = np.ones(count >> levels, np.float64)
    for _ in range(levels):
        fine = np.zeros(2 * weights.size + 4, np.float64)
        for tap, value in zip(range(-2, 3), (0.0625, 0.25, 0.375, 0.25, 0.0625)):
            fine[2 + tap : 2 + tap + 2 * weights.size : 2] += value * weights
        weights = fine[2:-2]
    return weights


class Axis:
    def __init__(self, n, at, count):
        self.n, self.at, self.count = n, at, count

    def inside(self, index, level):
        place = index + self.at * (self.n >> level)
        return (place >= 0) & (place < self.count * (self.n >> level))

    def shrink(self, fine, coarse, level):
        far = np.abs(fine[:, None] - 2 * coarse[None, :])
        value = np.select([far == 0, far == 1, far == 2], [0.375, 0.25, 0.0625], 0.0)
        return value * self.inside(coarse, level)[None, :]

    def grow(self, coarse, fine, level):
        far = np.abs(2 * coarse[:, None] - fine[None, :])
        value = np.select([far == 0, far == 1, far == 2], [0.75, 0.5, 0.125], 0.0)
        return value * self.inside(fine, level)[None, :]

    def window(self, level, edge):
        return np.arange(-edge, (self.n >> level) + edge)

    def deep(self, lanes, shift=0):
        out = [x + shift * (self.n >> level) for level, x in zip((3, 4, 5, 6), self.out())]
        w4, w5 = self.window(4, 30), self.window(5, 14)
        to4 = self.shrink(lanes, w4, 4)
        to5 = to4 @ self.shrink(w4, w5, 5)
        same = (lanes[:, None] == out[0][None, :]) * self.inside(out[0], 3)[None, :]
        parts = [
            same * 1.0,
            self.shrink(lanes, out[1], 4),
            to4 @ self.shrink(w4, out[2], 5),
            to5 @ self.shrink(w5, out[3], 6),
        ]
        return np.concatenate(parts, axis=1) * self.inside(lanes, 3)[:, None]

    def out(self):
        low = -4
        return [low + np.arange(size) for size in self.sizes()]

    def sizes(self):
        return [self.n // 8 + 8, self.n // 16 + 8, self.n // 32 + 8, self.n // 64 + 16]

    def back(self):
        o3, o4, o5, o6 = self.out()
        w4, w5 = self.window(4, 4), self.window(5, 4)
        from4 = self.grow(w4, o3, 3)
        from5 = self.grow(w5, w4, 4) @ from4
        parts = [
            np.eye(o3.size) * self.inside(o3, 3)[None, :],
            self.grow(o4, o3, 3),
            self.grow(o5, w4, 4) @ from4,
            self.grow(o6, w5, 5) @ from5,
        ]
        return np.concatenate(parts, axis=0)

    def sums(self, level, place):
        weights = reach(self.count * (self.n >> level), LEVELS - level)
        place = place + self.at * (self.n >> level)
        return np.where((place >= 0) & (place < weights.size), weights[np.clip(place, 0, weights.size - 1)], 0.0)

    def ones(self, level):
        x = self.inside(self.window(6, 4), 6) * 1.0
        for k in range(5, level - 1, -1):
            x = x @ self.grow(self.window(k + 1, 4), self.window(k, 4), k)
        return x


def pad(x, shape):
    return np.pad(x, [(0, size - have) for size, have in zip(shape, x.shape)])


def halves(x):
    high = x.astype(np.float32).astype(jnp.bfloat16)
    low = (x - high.astype(np.float64)).astype(np.float32).astype(jnp.bfloat16)
    return high, low


def spaced(n):
    size = -(-(n + 8) // LANES) * LANES
    return np.concatenate([np.arange(-4, n + 4), np.full(size - n - 8, FAR)])


def col_tables(n, at, count):
    ax = Axis(n, at, count)
    shifts = [1 if at == 0 else -1] if count == 2 else [1, -1]
    lane = np.arange(LANES)
    own = np.arange(n)
    out1, out2 = spaced(n // 2), spaced(n // 4)
    w1, w2 = ax.window(1, 16), ax.window(2, 8)
    middle = np.isin(lane, MIDDLE)[None, :]
    s1, s2 = [], []
    for d in shifts:
        near = n - LANES + lane if d > 0 else lane
        over1, over2 = (lane - 4 + (n >> level if d > 0 else 0) for level in (1, 2))
        s1.append(ax.shrink(near, over1, 1) * middle)
        s2.append(ax.shrink(near, w1, 1) @ ax.shrink(w1, over2, 2) * middle)
    s1, s2 = (np.stack([np.stack([x, np.roll(x, LANES // 2, 1)]) for x in y]) for y in (s1, s2))
    o3 = ax.out()[0]
    to2 = ax.shrink(own, w1, 1)
    c03 = to2 @ ax.shrink(w1, w2, 2) @ ax.shrink(w2, o3, 3)
    c03 = np.concatenate([pad(x.astype(np.float64), (n, LANES)) for x in halves(c03)], axis=1)
    three = np.concatenate([o3, np.full(LANES - o3.size, FAR)])
    call = []
    for d in [0] + shifts:
        call.append([pad(x.astype(np.float64), (LANES, 256)) for x in halves(ax.deep(three, d))])
    high, low = (np.concatenate([x[k] for x in call], axis=1) for k in range(2))
    call = np.concatenate([high, high, low], axis=0)
    back = ax.back()
    to0 = ax.grow(w2, w1, 1) @ ax.grow(w1, own, 0)
    from1, from2 = ax.grow(out1, own, 0), ax.grow(out2, out1, 1) @ ax.grow(out1, own, 0)
    m1, m2 = n // 2, n // 4
    e0 = np.concatenate([from2[:m2], from1[:m1], from1[m1 : m1 + 8], from2[m2 : m2 + 8]], axis=0)
    e0 = pad(e0, (m1 + m2 + LANES, n))
    ec0 = np.stack([pad(x.astype(np.float64), (256, n)) for x in halves(back @ ax.grow(o3, w2, 2) @ to0)])
    return dict(
        c1=ax.shrink(own, out1, 1), c2=to2 @ ax.shrink(w1, out2, 2), s1=s1, s2=s2, c03=c03, call=call,
        ec0=ec0, e0=e0,
    ), dict(line=np.stack([ax.sums(0, own), ax.ones(0)[4:-4]]))


def row_tables(n, at, count):
    ax = Axis(n, at, count)
    o3 = ax.out()[0]
    deep = ax.deep(o3).T
    high, low = (x.astype(np.float64) for x in halves(deep))
    size6 = ax.sizes()[3]
    rall = np.concatenate([high, low[-size6:]], axis=0)
    rall = pad(rall, (-(-rall.shape[0] // 16) * 16, -(-o3.size // 16) * 16))
    rall = np.concatenate([rall, rall], axis=1)
    back = ax.back()
    deep_rows = -(-o3.size // 16) * 16
    er = np.stack([pad(x.astype(np.float64), (deep_rows, x.shape[1])) for x in halves(back.T)])
    first = np.repeat(ax.sums(3, o3)[:, None], LANES, 1)
    w1, w2 = ax.window(1, 8), ax.window(2, 8)
    r012 = (ax.grow(o3, w2, 2) @ ax.grow(w2, w1, 1) @ ax.grow(w1, np.arange(n), 0)).T
    high, low = (pad(x.astype(np.float64), (n, deep_rows)) for x in halves(r012))
    r012 = np.concatenate([high, low, high], axis=1)
    second = np.repeat(pad(ax.ones(3), (deep_rows,))[:, None], LANES, 1)
    return dict(rall=rall, er=er, r012=r012), dict(first=first, second=second)


def tables(nr, nc, nx, blocks):
    def places(count):
        return (0, 1) if count == 2 else (0, 1, count - 1)

    cols = [col_tables(nc, at, nx) for at in places(nx)]
    rows = [row_tables(nr, at, blocks) for at in places(blocks)]

    def cast(x):
        return jnp.asarray(np.asarray(x, np.float32)).astype(BF16)

    def keep(x):
        return jnp.asarray(np.asarray(x, np.float32))

    out = {}
    for some in (cols, rows):
        for k in some[0][0]:
            out[k] = cast(np.stack([x[0][k] for x in some]))
        for k in some[0][1]:
            out[k] = keep(np.stack([x[1][k] for x in some]))
    return out


def merge(made):
    arrays, places = [], {}
    for at, group in enumerate(COLS + ROWS):
        lanes = max(made[name].shape[-1] for name in group)
        parts, start = [], 0
        for name in group:
            x = made[name]
            rows, width = x.shape[-2:]
            x = x.reshape(x.shape[0], -1, rows, width)
            tall = -(-rows // 16) * 16 if len(group) > 1 else rows
            x = jnp.pad(x, ((0, 0), (0, 0), (0, tall - rows), (0, lanes - width)))
            places[name] = (at, start, tall, rows, width)
            start += x.shape[1] * tall
            parts.append(x.reshape(x.shape[0], -1, lanes))
        arrays.append(jnp.concatenate(parts, axis=1))
    return arrays, places


def split(x):
    high = x.astype(BF16)
    return high, (x - high.astype(F32)).astype(BF16)


def dot(a, b):
    return jnp.dot(a, b, preferred_element_type=F32)


def right(x, c):
    high, low = split(x)
    return dot(high, c) + dot(low, c)


COLS = (("c03", "c2"), ("call", "e0"), ("c1",), ("s1", "s2"), ("ec0",), ("line",))
ROWS = (("rall", "er"), ("first", "second"), ("r012",))
OWN_TILES, SIDE_TILES = 5, 2
CHUNKS = 4
PIECES = 4


def kernel(
    sizes, places, off_hbm, wgt_hbm, gain_hbm, h_ref, s_ref, *rest
):
    nr, nc, nx, ny, nz, ns = sizes
    count = len(COLS) + len(ROWS)
    tables_hbm, rest = rest[:count], rest[count:]
    out0, us_ref, r012_ref, rest = *rest[:3], rest[3:]
    tab, rest = (*rest[: count - 1], r012_ref), rest[count - 1 :]
    (
        off_ref, wgt_ref, gain_ref, h_buf, s_buf, q0, num, den, n1, d1, n2, d2, n3, d3,
        x1, x2, g, factor, y1, y2, side_s, side_r, edge_s, edge_r, z2b, z1b, wide, part, slots,
        own_sem, tab_sem, send0, recv0, psend, precv,
    ) = rest
    cx, cy, cz = lax.axis_index("gx"), lax.axis_index("gy"), lax.axis_index("gz")
    row = cy * nz + cz
    blocks = ny * nz
    own_tiles = nc // LANES
    t3 = nr // 8
    m3 = t3 + 8

    def kind(at, count):
        return at if count == 2 else jnp.where(at == 0, 0, jnp.where(at == count - 1, 2, 1))

    ct, rt = kind(cx, nx), kind(row, blocks)

    loads = []
    step = nr // CHUNKS
    for k in range(CHUNKS):
        rows = pl.ds(k * step, step)
        for a, (src, dst) in enumerate(((h_ref, h_buf), (s_ref, s_buf))):
            loads.append(
                pltpu.make_async_copy(
                    src.at[rows, :],
                    dst.at[pl.ds(HALO + k * step, step), pl.ds(0, nc)],
                    own_sem.at[k],
                )
            )
    small = [
        pltpu.make_async_copy(src, dst, own_sem.at[CHUNKS + a])
        for a, (src, dst) in enumerate(((off_hbm, off_ref), (wgt_hbm, wgt_ref), (gain_hbm, gain_ref)))
    ]
    fetch = [
        pltpu.make_async_copy(src.at[ct if i < len(COLS) else rt], tab[i], tab_sem.at[i])
        for i, src in enumerate(tables_hbm)
    ]
    ready = set()

    def await_tables(*names):
        for name in names:
            if places[name][0] not in ready:
                ready.add(places[name][0])
                fetch[places[name][0]].wait()

    def table(name, k=0, rows=None):
        at, start, tall, height, width = places[name]
        first, last = rows or (0, height)
        return tab[at][start + k * tall + first : start + k * tall + last, :width]

    for copy in loads[:2] + small + loads[2:]:
        copy.start()

    up, down = row > 0, row < blocks - 1
    send_row, recv_row = {0: None, 1: down, 2: up}, {0: None, 1: up, 2: down}
    if ns == 1:
        send_col, recv_col = {0: None, 1: None}, {0: None, 1: None}
        to_col = {0: cx, 1: 1 - cx}
        near_tile = {1: (1 - cx) * (own_tiles - 1)}
        into1, into2 = {1: (1 - cx) * (x1.shape[1] - 1)}, {1: (1 - cx) * (x2.shape[1] - 1)}
    else:
        send_col = {0: None, 1: cx < nx - 1, 2: cx > 0}
        recv_col = {0: None, 1: cx > 0, 2: cx < nx - 1}
        to_col = {0: cx, 1: cx + 1, 2: cx - 1}
        near_tile = {1: own_tiles - 1, 2: 0}
        into1, into2 = {1: 0, 2: x1.shape[1] - 1}, {1: 0, 2: x2.shape[1] - 1}
    kinds = [(rp, cp) for rp in (0, 1, 2) for cp in range(1 + ns) if rp or cp]

    def device(rp, cp):
        target = row + {0: 0, 1: 1, 2: -1}[rp]
        return {"gx": to_col[cp], "gy": target // nz, "gz": target % nz}

    def also(a, b):
        return b if a is None else a if b is None else jnp.logical_and(a, b)

    def sends(rp, cp):
        return also(send_row[rp], send_col[cp])

    def comes(rp, cp):
        return also(recv_row[rp], recv_col[cp])

    def given(flag, body):
        if flag is None:
            body()
        else:
            pl.when(flag)(body)

    everyone = nx * blocks
    me = row * nx + cx

    def peer(s):
        other = (me + s) % everyone
        line = other // nx
        return {"gx": other % nx, "gy": line // nz, "gz": line % nz}

    def places_of(at, count):
        return [jnp.where(at + d < count, at + d, at + d - count) for d in range(count)]

    def others(body):
        if everyone <= 64:
            xs, ys, zs = places_of(cx, nx), places_of(cy, ny), places_of(cz, nz)
            for s in range(1, everyone):
                line = s // nx
                body(s, {"gx": xs[s % nx], "gy": ys[line // nz], "gz": zs[line % nz]})
        else:
            def step_(s, carry):
                body(s, peer(s))
                return carry

            lax.fori_loop(1, everyone, step_, 0)

    barrier = pltpu.get_barrier_semaphore()
    others(lambda s, who: pl.semaphore_signal(barrier, inc=1, device_id=who))

    for copy in fetch:
        copy.start()

    zero = jnp.zeros((HALO, LANES), F32)
    for x in (num, den):
        for c in range(own_tiles):
            x[c, 0:HALO, :] = zero
            x[c, nr + HALO : nr + 2 * HALO, :] = zero
            x[c, nr + 2 * HALO :, :] = zero
    zero = jnp.zeros((8, LANES), F32)
    for x in (n1, d1, n2, d2):
        for c in range(own_tiles):
            x[c, 0:8, :] = zero
            x[c, x.shape[1] - 8 :, :] = zero

    for rp, cp in kinds:
        if rp and comes(rp, cp) is not None:
            @pl.when(jnp.logical_not(comes(rp, cp)))
            def _():
                edge_r[rp - 1, cp] = jnp.zeros((OWN_TILES, 8, LANES), F32)

    def edge(i):
        rp, cp = kinds[i]
        if rp == 0:
            src, dst = side_s.at[cp - 1], side_r.at[cp - 1]
        else:
            place = pl.ds(0, OWN_TILES) if cp == 0 else pl.ds(0, SIDE_TILES)
            src, dst = edge_s.at[rp - 1, cp, place], edge_r.at[rp - 1, cp, place]
        return pltpu.make_async_remote_copy(
            src_ref=src, dst_ref=dst, send_sem=send0.at[i], recv_sem=recv0.at[i], device_id=device(rp, cp)
        )

    lane8 = lax.broadcasted_iota(jnp.int32, (8, LANES), 1)
    line8 = lax.broadcasted_iota(jnp.int32, (8, LANES), 0)

    def spread(table):
        line = jnp.zeros((8, LANES), F32)
        for i in range(table.shape[0]):
            line = jnp.where(lane8 == i, table[i], line)
        return line

    for copy in small:
        copy.wait()
    wgt_row = spread(wgt_ref)

    def tree(ids, table):
        values = [table[i] for i in range(table.shape[0])]
        bit = 1
        while len(values) > 1:
            mask = (ids & bit) != 0
            values = [jnp.where(mask, values[i + 1], values[i]) for i in range(0, len(values), 2)]
            bit *= 2
        return values[0]

    def level0(base, count, c):
        rows = pl.ds(base, count)
        ids = s_buf[rows, c * LANES : (c + 1) * LANES]
        weight = jnp.concatenate(
            [jnp.take_along_axis(wgt_row, ids[r : r + 8], axis=1) for r in range(0, count, 8)], axis=0
        )
        moved = h_buf[rows, c * LANES : (c + 1) * LANES] + tree(ids, off_ref)
        num[c, rows, :] = weight * moved
        den[c, rows, :] = weight
        return moved

    def summary(s, who):
        return pltpu.make_async_remote_copy(
            src_ref=part,
            dst_ref=slots.at[s - 1],
            send_sem=psend,
            recv_sem=precv,
            device_id=who,
        )

    def send_edges(wanted):
        for i, d in enumerate(kinds):
            if wanted(d):
                given(sends(*d), lambda: edge(i).start())

    lane1 = lax.broadcasted_iota(jnp.int32, (1, LANES), 1)

    def meet():
        with jax.named_scope("meet"):
            pl.semaphore_wait(barrier, everyone - 1)

        others(lambda s, who: summary(s, who).start())

    def taps(src, c, start, count):
        x = [src[c, pl.ds(start + a, count, stride=2), :] for a in range(-2, 3)]
        return 0.375 * x[2] + (0.25 * (x[1] + x[3]) + 0.0625 * (x[0] + x[4]))

    def hold(x, c, p, first):
        if first:
            ok = jnp.logical_or(line8 >= 4, up)
        else:
            ok = jnp.logical_or(line8 < 4, down)
        x[c, p : p + 8, :] = jnp.where(ok, x[c, p : p + 8, :], 0.0)

    last1, last2 = nr // 2 + 8, nr // 4 + 8

    def rows1(src, dst, c, p, count):
        dst[c, p : p + count, :] = taps(src, c, 2 * p - 8, count)

    def rows2(src, dst, c, p, count):
        dst[c, p : p + count, :] = taps(src, c, 2 * p - 12, count)

    pairs = ((num, n1, n2, n3), (den, d1, d2, d3))
    part1, part2 = step // 2, nr // 8

    def group1(k):
        count = part1 if k < CHUNKS - 1 else part1 + 16
        for src, one, _, _ in pairs:
            for c in range(own_tiles):
                rows1(src, one, c, 8 + k * part1, count)
                if k == 0:
                    hold(one, c, 8, True)
                if k == CHUNKS - 1:
                    hold(one, c, last1, False)

    def group2(k):
        for _, one, two, _ in pairs:
            for c in range(own_tiles):
                rows2(one, two, c, 8 + k * part2, part2 + 8 * k)
                hold(two, c, last2 if k else 8, not k)

    with jax.named_scope("level0"):
        for k in range(CHUNKS):
            both = pl.ds(0, 2 * step)
            pltpu.make_async_copy(h_ref.at[both, :], h_buf.at[both, pl.ds(0, nc)], own_sem.at[k]).wait()
            for c in range(own_tiles):
                q0[c, k * step : (k + 1) * step, :] = level0(HALO + k * step, step, c)
            if k:
                group1(k - 1)
            if k == CHUNKS - 1:
                group2(0)

    with jax.named_scope("rowpyr"):
        group1(CHUNKS - 1)
        group2(1)
        for _, _, two, three in pairs:
            for c in range(own_tiles):
                three[c] = taps(two, c, 4, m3)

    with jax.named_scope("sums"):
        await_tables("line", "first")
        flat = []
        for x in (n3, d3):
            y = sum(x[c] * table("line", 0, (0, 1))[:, c * LANES : (c + 1) * LANES] for c in range(own_tiles))
            y = jnp.sum(y * table("first"), axis=0, keepdims=True)
            flat.append(y + pltpu.roll(y, LANES // 2, axis=1))
        part[...] = jnp.where(lane1 < LANES // 2, flat[0], flat[1])

    early_half = jnp.logical_and(cz > 0, cz < nz // 2) if nz > 1 else None
    first_plane = cz == 0
    if early_half is None:
        meet()
    else:
        pl.when(cz >= nz // 2)(meet)
    def wide_of(x, rows, tiles):
        return jnp.concatenate([x[c, rows, :] for c in tiles], axis=1)

    own_range = range(own_tiles)
    size1, size2 = x1.shape[2], x2.shape[2]
    s3, s4, s5, s6 = (nr // 8 + 8, nr // 16 + 8, nr // 32 + 8, nr // 64 + 16)
    stack = s3 + s4 + s5 + s6
    tops = (0, s3, s3 + s4, s3 + s4 + s5)
    bottoms = tuple(top + (nr >> level) for top, level in zip(tops, (3, 4, 5, 6)))

    def level_of(shape, dim, cuts):
        index = lax.broadcasted_iota(jnp.int32, shape, dim)
        return sum((index >= cut).astype(jnp.int32) for cut in cuts)

    c3, c4, c5 = nc // 8 + 8, nc // 16 + 8, nc // 32 + 8
    lane_cuts = (c3, c3 + c4, c3 + c4 + c5)
    middle = jnp.logical_and(line8 >= MIDDLE[0], line8 <= MIDDLE[-1])

    def pack(n, d):
        return jnp.where(middle, n, pltpu.roll(d, 4, axis=0))

    def unpack(x):
        return [jnp.where(middle, x, 0.0), jnp.where(middle, pltpu.roll(x, 4, axis=0), 0.0)]

    def unpack_lanes(x):
        low = lax.broadcasted_iota(jnp.int32, x.shape, 1) < LANES // 2
        return jnp.where(low, x, 0.0), jnp.where(low, pltpu.roll(x, LANES // 2, axis=1), 0.0)

    with jax.named_scope("p3"):
        await_tables("c03", "rall", "call")
        x = jnp.concatenate([wide_of(n3, slice(None), own_range), wide_of(d3, slice(None), own_range)], axis=0)
        x = right(x, table("c03"))
        x = x[:, :LANES] + x[:, LANES:]
        high, low = split(jnp.concatenate([x[:m3], x[m3:]], axis=1))
        gap = jnp.zeros((-m3 % 16, 2 * LANES), BF16)
        x = dot(table("rall"), jnp.concatenate([high, gap, low, gap], axis=0))
        x = jnp.concatenate([x[: stack - s6], x[stack - s6 : stack] + x[stack : stack + s6]], axis=0)
        def across(y):
            y = jnp.concatenate([y[:, :LANES], y[:, LANES:]], axis=0)
            high, low = split(y)
            return high, dot(jnp.concatenate([high, low], axis=1), table("call", 0, (0, 2 * LANES)))

        rows_all = x
        high, y = across(jnp.concatenate([x[f : f + 8] for firsts in (bottoms, tops) for f in firsts], axis=0))
        deep_ends = y + dot(high, table("call", 0, (2 * LANES, 3 * LANES)))

    base_g = size1 + size2

    def own_lines(x1_, x2_, g_):
        last = x1_[2] + pltpu.roll(x2_[1], 8, axis=1) + pltpu.roll(g_[1], 16, axis=1)
        return [x1_[0], x1_[1], x2_[0], g_[0], last]

    def ends(x, c, last):
        return jnp.concatenate([x[c, 8:16, :], x[c, last : last + 8, :]], axis=0)

    with jax.named_scope("edge_own"):
        await_tables("s1", "s2", "c1", "c2")

        def own_ends(n, d, last, name):
            y = jnp.concatenate(
                [jnp.concatenate([ends(x, c, last) for c in own_range], axis=1) for x in (n, d)], axis=0
            )
            return right(y, table(name))

        own1, own2 = own_ends(n1, d1, last1, "c1"), own_ends(n2, d2, last2, "c2")

    with jax.named_scope("edge_side"):
        side_ends = []
        for k in range(1, 1 + ns):
            pair = []
            for n, d, last, name in ((n1, d1, last1, "s1"), (n2, d2, last2, "s2")):
                y = right(ends(n, near_tile[k], last), table(name, 2 * (k - 1)))
                pair.append(y + right(ends(d, near_tile[k], last), table(name, 2 * (k - 1) + 1)))
            side_ends.append(pair)

    def tile(x, at, c):
        return x[at : at + 8, c * LANES : (c + 1) * LANES]

    with jax.named_scope("g_pack"):
        for k in range(1 + ns):
            for rp in (1, 2):
                deep = []
                for a in range(2):
                    lines = []
                    for c in range(2):
                        index = lane8 + c * LANES
                        first = a * 64 + (rp - 1) * 32
                        lane = k * 256 + c * LANES
                        b = [deep_ends[first + 8 * l : first + 8 * l + 8, lane : lane + LANES] for l in range(4)]
                        lines.append(
                            jnp.where(
                                index < lane_cuts[0], b[0],
                                jnp.where(index < lane_cuts[1], b[1], jnp.where(index < lane_cuts[2], b[2], b[3])),
                            )
                        )
                    deep.append(lines)
                at = 8 * (2 - rp)
                if k == 0:
                    packed = [
                        own_lines(
                            [tile(own1, 16 * a + at, c) for c in range(3)],
                            [tile(own2, 16 * a + at, c) for c in range(2)],
                            deep[a],
                        )
                        for a in range(2)
                    ]
                    for t in range(OWN_TILES):
                        edge_s[rp - 1, 0, t] = pack(packed[0][t], packed[1][t])
                else:
                    lines = [y[at : at + 8] for y in side_ends[k - 1]]
                    edge_s[rp - 1, k, 0] = pack(deep[0][0], deep[1][0])
                    edge_s[rp - 1, k, 1] = (
                        lines[0] + pltpu.roll(lines[1], 8, axis=1)
                        + pltpu.roll(pack(deep[0][1], deep[1][1]), 16, axis=1)
                    )

    if early_half is not None:
        pl.when(early_half)(meet)

    with jax.named_scope("send"):
        if early_half is None:
            send_edges(lambda d: d[0] != 0)
        else:
            pl.when(jnp.logical_not(first_plane))(lambda: send_edges(lambda d: d[0] != 0))

    body1, body2 = slice(8, 8 + size1), slice(8, 8 + size2)

    with jax.named_scope("g"):
        high, y = across(rows_all)
        tail = stack - 32
        more = [dot(high[a * stack + tail : (a + 1) * stack], table("call", 0, (2 * LANES, 3 * LANES))) for a in range(2)]
        for a in range(2):
            for c in range(2):
                for k in range(1 + ns):
                    lanes_ = slice(k * 256 + c * LANES, k * 256 + (c + 1) * LANES)
                    upper = y[a * stack : a * stack + tail, lanes_]
                    lower = y[a * stack + tail : (a + 1) * stack, lanes_] + more[a][:, lanes_]
                    if k == 0:
                        g[a, c, :tail] = upper
                        g[a, c, tail:] = lower
                    else:
                        first = base_g + (2 * a + c) * stack
                        side_s[k - 1, first : first + tail, :] = upper
                        side_s[k - 1, first + tail : first + stack, :] = lower

    with jax.named_scope("x_side"):
        for k in range(1, 1 + ns):
            for base, n, d, body, name in ((0, n1, d1, body1, "s1"), (size1, n2, d2, body2, "s2")):
                y = right(n[near_tile[k], body, :], table(name, 2 * (k - 1) + 0))
                y = y + right(d[near_tile[k], body, :], table(name, 2 * (k - 1) + 1))
                side_s[k - 1, base : base + y.shape[0], :] = y
        if early_half is None:
            send_edges(lambda d: d[0] == 0)
        else:
            pl.when(jnp.logical_not(first_plane))(lambda: send_edges(lambda d: d[0] == 0))

    with jax.named_scope("x_own"):
        for n, d, body, name, dst in ((n1, d1, body1, "c1", x1), (n2, d2, body2, "c2", x2)):
            for a, y in enumerate((n, d)):
                y = right(wide_of(y, body, own_range), table(name))
                for c in range(dst.shape[1]):
                    dst[a, c] = y[:, c * LANES : (c + 1) * LANES]

    if early_half is not None:

        @pl.when(first_plane)
        def _():
            meet()
            send_edges(lambda d: True)

    def ratio(n, d):
        return jnp.where(d > 0, n / d, 0.0)

    def await_edges(wanted):
        for i, d in enumerate(kinds):
            if wanted(d):
                given(sends(*d), lambda: edge(i).wait_send())
                given(comes(*d), lambda: edge(i).wait_recv())

    def q_rows(x, y, rows, gain):
        for c in range(x.shape[1]):
            y[rows, c * LANES : (c + 1) * LANES] = gain * ratio(x[0, c, rows, :], x[1, c, rows, :])

    gain1, gain2 = gain_ref[1] - gain_ref[0], gain_ref[2] - gain_ref[1]

    with jax.named_scope("w_side"):
        await_edges(lambda d: d[0] == 0)
    with jax.named_scope("add_side"):
        for k in range(1, 1 + ns):
            def add():
                for base, size, x, into in ((0, size1, x1, into1[k]), (size1, size2, x2, into2[k])):
                    more = unpack_lanes(side_r[k - 1, base : base + size, :])
                    for a in range(2):
                        x[a, into] = x[a, into] + more[a]
                for a in range(2):
                    for c in range(2):
                        base = base_g + (2 * a + c) * stack
                        g[a, c] = g[a, c] + side_r[k - 1, base : base + stack, :]

            given(recv_col[k], add)
    with jax.named_scope("q"):
        q_rows(x1, y1, slice(0, size1), gain1)
        q_rows(x2, y2, slice(0, size2), gain2)

    def grow_rows(src, dst, first, count):
        x, y, w = (src[first + k : first + k + count, :] for k in (1, 2, 3))
        dst[pl.ds(2 * first, count, stride=2), :] = 0.125 * (x + w) + 0.75 * y
        dst[pl.ds(2 * first + 1, count, stride=2), :] = 0.5 * (y + w)

    def block(x, c, p, first):
        ok = jnp.logical_or(line8 >= 4, up) if first else jnp.logical_or(line8 < 4, down)
        x[c, p : p + 8, :] = jnp.where(ok, x[c, p : p + 8, :], 0.0)

    tiles2 = range(x2.shape[1])

    def mask_ends():
        for c in tiles2:
            block(z1b, c, 0, True)
            block(z1b, c, nr // 2, False)

    gain0 = gain_ref[0]

    def rise(c, m, count):
        x, y, w = (wide[c, m + k : m + k + count, :] for k in (3, 4, 5))
        even, odd = pl.ds(2 * m, count, stride=2), pl.ds(2 * m + 1, count, stride=2)
        out0[c, even, :] = gain0 * q0[c, even, :] + (0.125 * (x + w) + 0.75 * y)
        out0[c, odd, :] = gain0 * q0[c, odd, :] + 0.5 * (y + w)

    def upward(parts):
        z = [jnp.concatenate([z1b[c, p, :] for p in parts], axis=0) for c in tiles2]
        z += [
            jnp.concatenate([y1[p, c * LANES : (c + 1) * LANES] for p in parts], axis=0)
            for c in range(x1.shape[1])
        ]
        first, second = (lax.broadcasted_iota(jnp.int32, z[0].shape, 1) < k for k in (8, 16))
        t2 = len(tiles2) - 1
        ends = jnp.where(first, z[-1], jnp.where(second, pltpu.roll(z[t2], 8, axis=1), 0.0))
        z = z[:t2] + z[t2 + 1 : -1] + [ends]
        return right(jnp.concatenate(z, axis=1), table("e0"))

    with jax.named_scope("factor"):
        shape = (stack, 256)
        at_row = level_of(shape, 0, tops[1:])
        at_col = level_of(shape, 1, lane_cuts)
        gains = [gain_ref[level] - gain_ref[level - 1] for level in (3, 4, 5)] + [-gain_ref[5]]
        value = jnp.where(
            at_row == 0, gains[0], jnp.where(at_row == 1, gains[1], jnp.where(at_row == 2, gains[2], gains[3]))
        )
        factor[...] = jnp.where(at_row == at_col, value, 0.0)

    with jax.named_scope("base"):
        await_tables("e0")
        for c in tiles2:
            z2b[c] = y2[:, c * LANES : (c + 1) * LANES]
            grow_rows(z2b.at[c], z1b.at[c], 0, nr // 4 + 8)
        mask_ends()
        base = upward((slice(0, size1),))
        for c in own_range:
            wide[c] = base[:, c * LANES : (c + 1) * LANES]
        for c in own_range:
            for m in range(0, nr // 2, 32):
                rise(c, m, 32)

    with jax.named_scope("w_edges"):
        await_edges(lambda d: d[0] != 0)
        await_tables("ec0", "r012", "er", "second")
    packed_lanes = jnp.logical_and(lane8 % (LANES // 2) >= MIDDLE[0], lane8 % (LANES // 2) <= MIDDLE[-1])
    with jax.named_scope("edges"):
        for rp, at1, at2, firsts in ((1, 0, 0, tops), (2, nr // 2, nr // 4, bottoms)):
            def moved_to(y, by, ok):
                return [jnp.where(ok, pltpu.roll(z, LANES - by, axis=1), 0.0) for z in y]

            got = edge_r.at[rp - 1, 0]
            tail = unpack(got[OWN_TILES - 1])
            adds1 = [unpack(got[0]), unpack(got[1]), [jnp.where(lane8 < 8, y, 0.0) for y in tail]]
            adds2 = [unpack(got[2]), moved_to(tail, 8, lane8 < 8)]
            deep = [unpack(got[3]), moved_to(tail, 16, lane8 < 32)]
            for cp in range(1, 1 + ns):
                y = edge_r[rp - 1, cp, 1]
                for a, more in enumerate(unpack(edge_r[rp - 1, cp, 0])):
                    deep[0][a] = deep[0][a] + more
                for a, more in enumerate(moved_to(unpack(y), 16, lane8 < 32)):
                    deep[1][a] = deep[1][a] + more
            for x, at, adds in ((x1, at1, adds1), (x2, at2, adds2)):
                for c, more in enumerate(adds):
                    for a in range(2):
                        x[a, c, at : at + 8, :] = x[a, c, at : at + 8, :] + more[a]
            for cp in range(1, 1 + ns):
                y = edge_r[rp - 1, cp, 1]
                for x, at, into, z in ((x1, at1, into1[cp], y), (x2, at2, into2[cp], pltpu.roll(y, LANES - 8, axis=1))):
                    for a, more in enumerate(unpack_lanes(jnp.where(packed_lanes, z, 0.0))):
                        x[a, into, at : at + 8, :] = x[a, into, at : at + 8, :] + more
            for c in range(2):
                for a in range(2):
                    for f in firsts:
                        g[a, c, f : f + 8, :] = g[a, c, f : f + 8, :] + deep[c][a]
        for x, y, at, gain in ((x1, y1, nr // 2, gain1), (x2, y2, nr // 4, gain2)):
            q_rows(x, y, slice(0, 8), gain)
            q_rows(x, y, slice(at, at + 8), gain)
    with jax.named_scope("fix"):
        for c in tiles2:
            for at in (0, nr // 4):
                z2b[c, at : at + 8, :] = y2[at : at + 8, c * LANES : (c + 1) * LANES]
                grow_rows(z2b.at[c], z1b.at[c], at, 8)
        mask_ends()
        parts = (slice(0, 16), slice(nr // 2, nr // 2 + 16))
        base = upward(parts)
        for c in own_range:
            for i, p in enumerate(parts):
                wide[c, p, :] = base[16 * i : 16 * i + 16, c * LANES : (c + 1) * LANES]
            rise(c, 0, 8)
            rise(c, nr // 2 - 8, 8)

    with jax.named_scope("deep"):
        n, d = (jnp.concatenate([g[a, 0], g[a, 1]], axis=1) for a in range(2))
        x = jnp.where(d > 0, factor[...] * (n / d), 0.0)
        high, low = split(x)
        er = [table("er", k) for k in (0, 1)]
        x = dot(er[0], high) + dot(er[0], low) + dot(er[1], high)
        high, low = split(x)
        x = dot(high, table("ec0")) + dot(low, table("ec0")) + dot(high, table("ec0", 1))

    with jax.named_scope("w_top"):
        everything = pltpu.make_async_copy(slots, slots, precv)
        everything.wait()
        pltpu.make_async_copy(slots, slots, psend).wait()
    with jax.named_scope("top"):
        total = part[...] + jnp.sum(slots[...], axis=0)
        top_sum = jnp.sum(jnp.where(lane1 < LANES // 2, total, 0.0), axis=1, keepdims=True)
        top_weight = jnp.sum(jnp.where(lane1 < LANES // 2, 0.0, total), axis=1, keepdims=True)
        top_line = (top_sum / top_weight) * table("line", 0, (1, 2))
        ones = table("second")
        x = x + jnp.concatenate(
            [ones * top_line[:, c * LANES : (c + 1) * LANES] for c in own_range], axis=1
        )
        high, low = split(x)
        us_ref[...] = jnp.concatenate([high, high, low], axis=0)


def last(base_ref, us_ref, rows_ref, out_ref, buf, sem):
    nr, nc = buf.shape
    step = nr // sem.shape[0]
    writes = []
    for k in range(sem.shape[0]):
        here = slice(k * step, (k + 1) * step)
        y = dot(rows_ref[here, :], us_ref[...])
        for c in range(base_ref.shape[0]):
            cols = slice(c * LANES, (c + 1) * LANES)
            buf[here, cols] = base_ref[c, here, :] + y[:, cols]
        writes.append(pltpu.make_async_copy(buf.at[here, :], out_ref.at[here, :], sem.at[k]))
        writes[-1].start()
    for write in writes:
        write.wait()


def local(mesh_shape, heights, scene_ids, scene_offset, scene_weight, band_gain):
    nx, ny, nz = mesh_shape
    nr, nc = heights.shape
    ns = 1 if nx == 2 else 2
    made = tables(nr, nc, nx, ny * nz)
    given, places = merge(made)
    sizes = (nr, nc, nx, ny, nz, ns)
    ext = (nr + 2 * HALO, nc)
    tiles = nc // LANES
    own_tiles = tiles
    m3 = nr // 8 + 8
    size1, size2, stack = nr // 2 + 16, nr // 4 + 16, nr // 8 + nr // 16 + nr // 32 + nr // 64 + 40
    tiles1, tiles2 = nc // 2 // LANES + 1, nc // 4 // LANES + 1
    beside = size1 + size2 + 4 * stack
    peers = nx * ny * nz - 1
    messages = 3 * (1 + ns) - 1
    hbm = pl.BlockSpec(memory_space=pltpu.HBM)
    deep_rows = made["r012"].shape[-1]
    vmem = pl.BlockSpec(memory_space=pltpu.VMEM)
    kept = pl.pallas_call(
        functools.partial(kernel, sizes, places),
        out_shape=(
            pltpu.VMEM((own_tiles, nr, LANES), F32),
            pltpu.VMEM((deep_rows, nc), BF16),
            pltpu.VMEM((nr, deep_rows), BF16),
        ),
        in_specs=[hbm] * (5 + len(given)),
        out_specs=(vmem, vmem, vmem),
        scratch_shapes=[pltpu.VMEM(x.shape[1:], x.dtype) for x in given[:-1]]
        + [
            pltpu.SMEM(scene_offset.shape, F32),
            pltpu.SMEM(scene_weight.shape, F32),
            pltpu.SMEM(band_gain.shape, F32),
            pltpu.VMEM(ext, F32),
            pltpu.VMEM(ext, jnp.int32),
            pltpu.VMEM((own_tiles, nr, LANES), F32),
        ]
        + [pltpu.VMEM((tiles, nr + 3 * HALO, LANES), F32)] * 2
        + [pltpu.VMEM((tiles, nr // 2 + 32, LANES), F32)] * 2
        + [pltpu.VMEM((tiles, nr // 4 + 24, LANES), F32)] * 2
        + [pltpu.VMEM((own_tiles, m3, LANES), F32)] * 2
        + [
            pltpu.VMEM((2, tiles1, size1, LANES), F32),
            pltpu.VMEM((2, tiles2, size2, LANES), F32),
            pltpu.VMEM((2, 2, stack, LANES), F32),
            pltpu.VMEM((stack, 256), F32),
            pltpu.VMEM((size1, tiles1 * LANES), F32),
            pltpu.VMEM((size2, tiles2 * LANES), F32),
            pltpu.VMEM((ns, beside, LANES), F32),
            pltpu.VMEM((ns, beside, LANES), F32),
            pltpu.VMEM((2, 1 + ns, OWN_TILES, 8, LANES), F32),
            pltpu.VMEM((2, 1 + ns, OWN_TILES, 8, LANES), F32),
            pltpu.VMEM((tiles2, nr // 4 + 16, LANES), F32),
            pltpu.VMEM((tiles2, nr // 2 + 16, LANES), F32),
            pltpu.VMEM((own_tiles, nr // 2 + 16, LANES), F32),
            pltpu.VMEM((1, LANES), F32),
            pltpu.VMEM((peers, 1, LANES), F32),
            pltpu.SemaphoreType.DMA((CHUNKS + 3,)),
            pltpu.SemaphoreType.DMA((len(given),)),
            pltpu.SemaphoreType.DMA((messages,)),
            pltpu.SemaphoreType.DMA((messages,)),
            pltpu.SemaphoreType.DMA(()),
            pltpu.SemaphoreType.DMA(()),
        ],
        compiler_params=pltpu.CompilerParams(collective_id=0, has_side_effects=True),
    )(scene_offset, scene_weight, band_gain, heights, scene_ids, *given)
    return pl.pallas_call(
        last,
        out_shape=jax.ShapeDtypeStruct((nr, nc), F32),
        in_specs=[vmem] * 3,
        out_specs=pl.BlockSpec(memory_space=pltpu.HBM),
        scratch_shapes=[pltpu.VMEM((nr, nc), F32), pltpu.SemaphoreType.DMA((PIECES,))],
        compiler_params=pltpu.CompilerParams(vmem_limit_bytes=16 * 1024 * 1024),
    )(*kept)


def solution(mesh):
    placed = (P(("gy", "gz"), "gx"), P(("gy", "gz"), "gx"), P(), P(), P())
    shape = tuple(mesh.shape[name] for name in ("gx", "gy", "gz"))
    return jax.shard_map(
        functools.partial(local, shape), mesh=mesh, in_specs=placed,
        out_specs=P(("gy", "gz"), "gx"), check_vma=False,
    )
```

```python
import functools

import jax
import jax.numpy as jnp
import numpy as np
from jax import lax
from jax.experimental import pallas as pl
from jax.experimental.pallas import tpu as pltpu
from jax.sharding import PartitionSpec as P

F32, BF16 = jnp.float32, jnp.bfloat16
FAR = 1 << 20
HALO = 16
LANES = 128
LEVELS = 6
MIDDLE = (3, 4, 5)


def reach(count, levels):
    weights = np.ones(count >> levels, np.float64)
    for _ in range(levels):
        fine = np.zeros(2 * weights.size + 4, np.float64)
        for tap, value in zip(range(-2, 3), (0.0625, 0.25, 0.375, 0.25, 0.0625)):
            fine[2 + tap : 2 + tap + 2 * weights.size : 2] += value * weights
        weights = fine[2:-2]
    return weights


class Axis:
    def __init__(self, n, at, count):
        self.n, self.at, self.count = n, at, count

    def inside(self, index, level):
        place = index + self.at * (self.n >> level)
        return (place >= 0) & (place < self.count * (self.n >> level))

    def shrink(self, fine, coarse, level):
        far = np.abs(fine[:, None] - 2 * coarse[None, :])
        value = np.select([far == 0, far == 1, far == 2], [0.375, 0.25, 0.0625], 0.0)
        return value * self.inside(coarse, level)[None, :]

    def grow(self, coarse, fine, level):
        far = np.abs(2 * coarse[:, None] - fine[None, :])
        value = np.select([far == 0, far == 1, far == 2], [0.75, 0.5, 0.125], 0.0)
        return value * self.inside(fine, level)[None, :]

    def window(self, level, edge):
        return np.arange(-edge, (self.n >> level) + edge)

    def deep(self, lanes, shift=0):
        out = [x + shift * (self.n >> level) for level, x in zip((3, 4, 5, 6), self.out())]
        w4, w5 = self.window(4, 30), self.window(5, 14)
        to4 = self.shrink(lanes, w4, 4)
        to5 = to4 @ self.shrink(w4, w5, 5)
        same = (lanes[:, None] == out[0][None, :]) * self.inside(out[0], 3)[None, :]
        parts = [
            same * 1.0,
            self.shrink(lanes, out[1], 4),
            to4 @ self.shrink(w4, out[2], 5),
            to5 @ self.shrink(w5, out[3], 6),
        ]
        return np.concatenate(parts, axis=1) * self.inside(lanes, 3)[:, None]

    def out(self):
        low = -4
        return [low + np.arange(size) for size in self.sizes()]

    def sizes(self):
        return [self.n // 8 + 8, self.n // 16 + 8, self.n // 32 + 8, self.n // 64 + 16]

    def back(self):
        o3, o4, o5, o6 = self.out()
        w4, w5 = self.window(4, 4), self.window(5, 4)
        from4 = self.grow(w4, o3, 3)
        from5 = self.grow(w5, w4, 4) @ from4
        parts = [
            np.eye(o3.size) * self.inside(o3, 3)[None, :],
            self.grow(o4, o3, 3),
            self.grow(o5, w4, 4) @ from4,
            self.grow(o6, w5, 5) @ from5,
        ]
        return np.concatenate(parts, axis=0)

    def sums(self, level, place):
        weights = reach(self.count * (self.n >> level), LEVELS - level)
        place = place + self.at * (self.n >> level)
        return np.where((place >= 0) & (place < weights.size), weights[np.clip(place, 0, weights.size - 1)], 0.0)

    def ones(self, level):
        x = self.inside(self.window(6, 4), 6) * 1.0
        for k in range(5, level - 1, -1):
            x = x @ self.grow(self.window(k + 1, 4), self.window(k, 4), k)
        return x


def pad(x, shape):
    return np.pad(x, [(0, size - have) for size, have in zip(shape, x.shape)])


def halves(x):
    high = x.astype(np.float32).astype(jnp.bfloat16)
    low = (x - high.astype(np.float64)).astype(np.float32).astype(jnp.bfloat16)
    return high, low


def spaced(n):
    size = -(-(n + 8) // LANES) * LANES
    return np.concatenate([np.arange(-4, n + 4), np.full(size - n - 8, FAR)])


def col_tables(n, at, count):
    ax = Axis(n, at, count)
    shifts = [1 if at == 0 else -1] if count == 2 else [1, -1]
    lane = np.arange(LANES)
    own = np.arange(n)
    out1, out2 = spaced(n // 2), spaced(n // 4)
    w1, w2 = ax.window(1, 16), ax.window(2, 8)
    middle = np.isin(lane, MIDDLE)[None, :]
    s1, s2 = [], []
    for d in shifts:
        near = n - LANES + lane if d > 0 else lane
        over1, over2 = (lane - 4 + (n >> level if d > 0 else 0) for level in (1, 2))
        s1.append(ax.shrink(near, over1, 1) * middle)
        s2.append(ax.shrink(near, w1, 1) @ ax.shrink(w1, over2, 2) * middle)
    s1, s2 = (np.stack([np.stack([x, np.roll(x, LANES // 2, 1)]) for x in y]) for y in (s1, s2))
    o3 = ax.out()[0]
    to2 = ax.shrink(own, w1, 1)
    c03 = to2 @ ax.shrink(w1, w2, 2) @ ax.shrink(w2, o3, 3)
    c03 = np.concatenate([pad(x.astype(np.float64), (n, LANES)) for x in halves(c03)], axis=1)
    three = np.concatenate([o3, np.full(LANES - o3.size, FAR)])
    call = []
    for d in [0] + shifts:
        call.append([pad(x.astype(np.float64), (LANES, 256)) for x in halves(ax.deep(three, d))])
    high, low = (np.concatenate([x[k] for x in call], axis=1) for k in range(2))
    call = np.concatenate([high, high, low], axis=0)
    back = ax.back()
    to0 = ax.grow(w2, w1, 1) @ ax.grow(w1, own, 0)
    from1, from2 = ax.grow(out1, own, 0), ax.grow(out2, out1, 1) @ ax.grow(out1, own, 0)
    m1, m2 = n // 2, n // 4
    e0 = np.concatenate([from2[:m2], from1[:m1], from1[m1 : m1 + 8], from2[m2 : m2 + 8]], axis=0)
    e0 = pad(e0, (m1 + m2 + LANES, n))
    ec0 = np.stack([pad(x.astype(np.float64), (256, n)) for x in halves(back @ ax.grow(o3, w2, 2) @ to0)])
    return dict(
        c1=ax.shrink(own, out1, 1), c2=to2 @ ax.shrink(w1, out2, 2), s1=s1, s2=s2, c03=c03, call=call,
        ec0=ec0, e0=e0,
    ), dict(line=np.stack([ax.sums(0, own), ax.ones(0)[4:-4]]))


def row_tables(n, at, count):
    ax = Axis(n, at, count)
    o3 = ax.out()[0]
    deep = ax.deep(o3).T
    high, low = (x.astype(np.float64) for x in halves(deep))
    size6 = ax.sizes()[3]
    rall = np.concatenate([high, low[-size6:]], axis=0)
    rall = pad(rall, (-(-rall.shape[0] // 16) * 16, -(-o3.size // 16) * 16))
    rall = np.concatenate([rall, rall], axis=1)
    back = ax.back()
    deep_rows = -(-o3.size // 16) * 16
    er = np.stack([pad(x.astype(np.float64), (deep_rows, x.shape[1])) for x in halves(back.T)])
    first = np.repeat(ax.sums(3, o3)[:, None], LANES, 1)
    w1, w2 = ax.window(1, 8), ax.window(2, 8)
    r012 = (ax.grow(o3, w2, 2) @ ax.grow(w2, w1, 1) @ ax.grow(w1, np.arange(n), 0)).T
    high, low = (pad(x.astype(np.float64), (n, deep_rows)) for x in halves(r012))
    r012 = np.concatenate([high, low, high], axis=1)
    second = np.repeat(pad(ax.ones(3), (deep_rows,))[:, None], LANES, 1)
    return dict(rall=rall, er=er, r012=r012), dict(first=first, second=second)


def tables(nr, nc, nx, blocks):
    def places(count):
        return (0, 1) if count == 2 else (0, 1, count - 1)

    cols = [col_tables(nc, at, nx) for at in places(nx)]
    rows = [row_tables(nr, at, blocks) for at in places(blocks)]

    def cast(x):
        return jnp.asarray(np.asarray(x, np.float32)).astype(BF16)

    def keep(x):
        return jnp.asarray(np.asarray(x, np.float32))

    out = {}
    for some in (cols, rows):
        for k in some[0][0]:
            out[k] = cast(np.stack([x[0][k] for x in some]))
        for k in some[0][1]:
            out[k] = keep(np.stack([x[1][k] for x in some]))
    return out


def merge(made):
    arrays, places = [], {}
    for at, group in enumerate(COLS + ROWS):
        lanes = max(made[name].shape[-1] for name in group)
        parts, start = [], 0
        for name in group:
            x = made[name]
            rows, width = x.shape[-2:]
            x = x.reshape(x.shape[0], -1, rows, width)
            tall = -(-rows // 16) * 16 if len(group) > 1 else rows
            x = jnp.pad(x, ((0, 0), (0, 0), (0, tall - rows), (0, lanes - width)))
            places[name] = (at, start, tall, rows, width)
            start += x.shape[1] * tall
            parts.append(x.reshape(x.shape[0], -1, lanes))
        arrays.append(jnp.concatenate(parts, axis=1))
    return arrays, places


def split(x):
    high = x.astype(BF16)
    return high, (x - high.astype(F32)).astype(BF16)


def dot(a, b):
    return jnp.dot(a, b, preferred_element_type=F32)


def right(x, c):
    high, low = split(x)
    return dot(high, c) + dot(low, c)


COLS = (("c03", "c2"), ("call", "e0", "ec0"), ("c1",), ("s1", "s2"), ("line",))
ROWS = (("rall", "er"), ("first", "second"), ("r012",))
OWN_TILES, SIDE_TILES = 5, 2
CHUNKS = 4
PIECES = 4


def kernel(
    sizes, places, off_hbm, wgt_hbm, gain_hbm, h_ref, s_ref, *rest
):
    nr, nc, nx, ny, nz, ns = sizes
    count = len(COLS) + len(ROWS)
    tables_hbm, rest = rest[:count], rest[count:]
    out0, us_ref, r012_ref, rest = *rest[:3], rest[3:]
    tab, rest = (*rest[: count - 1], r012_ref), rest[count - 1 :]
    (
        off_ref, wgt_ref, gain_ref, h_buf, s_buf, q0, num, den, n1, d1, n2, d2, n3, d3,
        x1, x2, g, factor, y1, y2, side_s, side_r, edge_s, edge_r, z2b, z1b, wide, part, slots,
        own_sem, tab_sem, send0, recv0, psend, precv,
    ) = rest
    cx, cy, cz = lax.axis_index("gx"), lax.axis_index("gy"), lax.axis_index("gz")
    row = cy * nz + cz
    blocks = ny * nz
    own_tiles = nc // LANES
    t3 = nr // 8
    m3 = t3 + 8

    def kind(at, count):
        return at if count == 2 else jnp.where(at == 0, 0, jnp.where(at == count - 1, 2, 1))

    ct, rt = kind(cx, nx), kind(row, blocks)

    loads = []
    step = nr // CHUNKS
    for k in range(CHUNKS):
        rows = pl.ds(k * step, step)
        for a, (src, dst) in enumerate(((h_ref, h_buf), (s_ref, s_buf))):
            loads.append(
                pltpu.make_async_copy(
                    src.at[rows, :],
                    dst.at[pl.ds(HALO + k * step, step), pl.ds(0, nc)],
                    own_sem.at[k],
                )
            )
    small = [
        pltpu.make_async_copy(src, dst, own_sem.at[CHUNKS + a])
        for a, (src, dst) in enumerate(((off_hbm, off_ref), (wgt_hbm, wgt_ref), (gain_hbm, gain_ref)))
    ]
    fetch = [
        pltpu.make_async_copy(src.at[ct if i < len(COLS) else rt], tab[i], tab_sem.at[i])
        for i, src in enumerate(tables_hbm)
    ]
    ready = set()

    def await_tables(*names):
        for name in names:
            if places[name][0] not in ready:
                ready.add(places[name][0])
                fetch[places[name][0]].wait()

    def table(name, k=0, rows=None):
        at, start, tall, height, width = places[name]
        first, last = rows or (0, height)
        return tab[at][start + k * tall + first : start + k * tall + last, :width]

    for copy in loads[:2] + small + loads[2:]:
        copy.start()

    up, down = row > 0, row < blocks - 1
    send_row, recv_row = {0: None, 1: down, 2: up}, {0: None, 1: up, 2: down}
    if ns == 1:
        send_col, recv_col = {0: None, 1: None}, {0: None, 1: None}
        to_col = {0: cx, 1: 1 - cx}
        near_tile = {1: (1 - cx) * (own_tiles - 1)}
        into1, into2 = {1: (1 - cx) * (x1.shape[1] - 1)}, {1: (1 - cx) * (x2.shape[1] - 1)}
    else:
        send_col = {0: None, 1: cx < nx - 1, 2: cx > 0}
        recv_col = {0: None, 1: cx > 0, 2: cx < nx - 1}
        to_col = {0: cx, 1: cx + 1, 2: cx - 1}
        near_tile = {1: own_tiles - 1, 2: 0}
        into1, into2 = {1: 0, 2: x1.shape[1] - 1}, {1: 0, 2: x2.shape[1] - 1}
    kinds = [(rp, cp) for rp in (0, 1, 2) for cp in range(1 + ns) if rp or cp]

    def device(rp, cp):
        target = row + {0: 0, 1: 1, 2: -1}[rp]
        return {"gx": to_col[cp], "gy": target // nz, "gz": target % nz}

    def also(a, b):
        return b if a is None else a if b is None else jnp.logical_and(a, b)

    def sends(rp, cp):
        return also(send_row[rp], send_col[cp])

    def comes(rp, cp):
        return also(recv_row[rp], recv_col[cp])

    def given(flag, body):
        if flag is None:
            body()
        else:
            pl.when(flag)(body)

    everyone = nx * blocks
    me = row * nx + cx

    def peer(s):
        other = (me + s) % everyone
        line = other // nx
        return {"gx": other % nx, "gy": line // nz, "gz": line % nz}

    def places_of(at, count):
        return [jnp.where(at + d < count, at + d, at + d - count) for d in range(count)]

    def others(body):
        if everyone <= 64:
            xs, ys, zs = places_of(cx, nx), places_of(cy, ny), places_of(cz, nz)
            for s in range(1, everyone):
                line = s // nx
                body(s, {"gx": xs[s % nx], "gy": ys[line // nz], "gz": zs[line % nz]})
        else:
            def step_(s, carry):
                body(s, peer(s))
                return carry

            lax.fori_loop(1, everyone, step_, 0)

    barrier = pltpu.get_barrier_semaphore()
    others(lambda s, who: pl.semaphore_signal(barrier, inc=1, device_id=who))

    for copy in fetch:
        copy.start()

    zero = jnp.zeros((HALO, LANES), F32)
    for x in (num, den):
        for c in range(own_tiles):
            x[c, 0:HALO, :] = zero
            x[c, nr + HALO : nr + 2 * HALO, :] = zero
            x[c, nr + 2 * HALO :, :] = zero
    zero = jnp.zeros((8, LANES), F32)
    for x in (n1, d1, n2, d2):
        for c in range(own_tiles):
            x[c, 0:8, :] = zero
            x[c, x.shape[1] - 8 :, :] = zero

    for rp, cp in kinds:
        if rp and comes(rp, cp) is not None:
            @pl.when(jnp.logical_not(comes(rp, cp)))
            def _():
                edge_r[rp - 1, cp] = jnp.zeros((OWN_TILES, 8, LANES), F32)

    def edge(i):
        rp, cp = kinds[i]
        if rp == 0:
            src, dst = side_s.at[cp - 1], side_r.at[cp - 1]
        else:
            place = pl.ds(0, OWN_TILES) if cp == 0 else pl.ds(0, SIDE_TILES)
            src, dst = edge_s.at[rp - 1, cp, place], edge_r.at[rp - 1, cp, place]
        return pltpu.make_async_remote_copy(
            src_ref=src, dst_ref=dst, send_sem=send0.at[i], recv_sem=recv0.at[i], device_id=device(rp, cp)
        )

    lane8 = lax.broadcasted_iota(jnp.int32, (8, LANES), 1)
    line8 = lax.broadcasted_iota(jnp.int32, (8, LANES), 0)

    def spread(table):
        line = jnp.zeros((8, LANES), F32)
        for i in range(table.shape[0]):
            line = jnp.where(lane8 == i, table[i], line)
        return line

    for copy in small:
        copy.wait()
    wgt_row = spread(wgt_ref)

    def tree(ids, table):
        values = [table[i] for i in range(table.shape[0])]
        bit = 1
        while len(values) > 1:
            mask = (ids & bit) != 0
            values = [jnp.where(mask, values[i + 1], values[i]) for i in range(0, len(values), 2)]
            bit *= 2
        return values[0]

    def level0(base, count, c):
        rows = pl.ds(base, count)
        ids = s_buf[rows, c * LANES : (c + 1) * LANES]
        weight = jnp.concatenate(
            [jnp.take_along_axis(wgt_row, ids[r : r + 8], axis=1) for r in range(0, count, 8)], axis=0
        )
        moved = h_buf[rows, c * LANES : (c + 1) * LANES] + tree(ids, off_ref)
        num[c, rows, :] = weight * moved
        den[c, rows, :] = weight
        return moved

    def summary(s, who):
        return pltpu.make_async_remote_copy(
            src_ref=part,
            dst_ref=slots.at[s - 1],
            send_sem=psend,
            recv_sem=precv,
            device_id=who,
        )

    def send_edges(wanted):
        for i, d in enumerate(kinds):
            if wanted(d):
                given(sends(*d), lambda: edge(i).start())

    lane1 = lax.broadcasted_iota(jnp.int32, (1, LANES), 1)

    def meet():
        with jax.named_scope("meet"):
            pl.semaphore_wait(barrier, everyone - 1)

        others(lambda s, who: summary(s, who).start())

    def taps(src, c, start, count):
        x = [src[c, pl.ds(start + a, count, stride=2), :] for a in range(-2, 3)]
        return 6.0 * x[2] + (4.0 * (x[1] + x[3]) + (x[0] + x[4]))

    def hold(x, c, p, first):
        if first:
            ok = jnp.logical_or(line8 >= 4, up)
        else:
            ok = jnp.logical_or(line8 < 4, down)
        x[c, p : p + 8, :] = jnp.where(ok, x[c, p : p + 8, :], 0.0)

    last1, last2 = nr // 2 + 8, nr // 4 + 8

    def rows1(src, dst, c, p, count):
        dst[c, p : p + count, :] = taps(src, c, 2 * p - 8, count)

    def rows2(src, dst, c, p, count):
        dst[c, p : p + count, :] = taps(src, c, 2 * p - 12, count)

    pairs = ((num, n1, n2, n3), (den, d1, d2, d3))
    part1, part2 = step // 2, nr // 8

    def group1(k):
        count = part1 if k < CHUNKS - 1 else part1 + 16
        for src, one, _, _ in pairs:
            for c in range(own_tiles):
                rows1(src, one, c, 8 + k * part1, count)
                if k == 0:
                    hold(one, c, 8, True)
                if k == CHUNKS - 1:
                    hold(one, c, last1, False)

    def group2(k):
        for _, one, two, _ in pairs:
            for c in range(own_tiles):
                rows2(one, two, c, 8 + k * part2, part2 + 8 * k)
                hold(two, c, last2 if k else 8, not k)

    with jax.named_scope("level0"):
        for k in range(CHUNKS):
            both = pl.ds(0, 2 * step)
            pltpu.make_async_copy(h_ref.at[both, :], h_buf.at[both, pl.ds(0, nc)], own_sem.at[k]).wait()
            for c in range(own_tiles):
                q0[c, k * step : (k + 1) * step, :] = level0(HALO + k * step, step, c)
            if k:
                group1(k - 1)
            if k == CHUNKS - 1:
                group2(0)

    with jax.named_scope("rowpyr"):
        group1(CHUNKS - 1)
        group2(1)
        for _, _, two, three in pairs:
            for c in range(own_tiles):
                three[c] = taps(two, c, 4, m3)

    with jax.named_scope("sums"):
        await_tables("line", "first")
        flat = []
        for x in (n3, d3):
            y = sum(x[c] * table("line", 0, (0, 1))[:, c * LANES : (c + 1) * LANES] for c in range(own_tiles))
            y = jnp.sum(y * table("first"), axis=0, keepdims=True)
            flat.append(y + pltpu.roll(y, LANES // 2, axis=1))
        part[...] = jnp.where(lane1 < LANES // 2, flat[0], flat[1])

    early_half = jnp.logical_and(cz > 0, cz < nz // 2) if nz > 1 else None
    first_plane = cz == 0
    if early_half is None:
        meet()
    else:
        pl.when(cz >= nz // 2)(meet)
    def wide_of(x, rows, tiles):
        return jnp.concatenate([x[c, rows, :] for c in tiles], axis=1)

    own_range = range(own_tiles)
    size1, size2 = x1.shape[2], x2.shape[2]
    s3, s4, s5, s6 = (nr // 8 + 8, nr // 16 + 8, nr // 32 + 8, nr // 64 + 16)
    stack = s3 + s4 + s5 + s6
    tops = (0, s3, s3 + s4, s3 + s4 + s5)
    bottoms = tuple(top + (nr >> level) for top, level in zip(tops, (3, 4, 5, 6)))

    def level_of(shape, dim, cuts):
        index = lax.broadcasted_iota(jnp.int32, shape, dim)
        return sum((index >= cut).astype(jnp.int32) for cut in cuts)

    c3, c4, c5 = nc // 8 + 8, nc // 16 + 8, nc // 32 + 8
    lane_cuts = (c3, c3 + c4, c3 + c4 + c5)
    middle = jnp.logical_and(line8 >= MIDDLE[0], line8 <= MIDDLE[-1])

    def pack(n, d):
        return jnp.where(middle, n, pltpu.roll(d, 4, axis=0))

    def unpack(x):
        return [jnp.where(middle, x, 0.0), jnp.where(middle, pltpu.roll(x, 4, axis=0), 0.0)]

    def unpack_lanes(x):
        low = lax.broadcasted_iota(jnp.int32, x.shape, 1) < LANES // 2
        return jnp.where(low, x, 0.0), jnp.where(low, pltpu.roll(x, LANES // 2, axis=1), 0.0)

    with jax.named_scope("p3"):
        await_tables("c03", "rall", "call")
        x = jnp.concatenate([wide_of(n3, slice(None), own_range), wide_of(d3, slice(None), own_range)], axis=0)
        x = right(x, table("c03"))
        x = x[:, :LANES] + x[:, LANES:]
        high, low = split(jnp.concatenate([x[:m3], x[m3:]], axis=1))
        gap = jnp.zeros((-m3 % 16, 2 * LANES), BF16)
        x = dot(table("rall"), jnp.concatenate([high, gap, low, gap], axis=0))
        x = jnp.concatenate([x[: stack - s6], x[stack - s6 : stack] + x[stack : stack + s6]], axis=0)
        def across(y):
            y = jnp.concatenate([y[:, :LANES], y[:, LANES:]], axis=0)
            high, low = split(y)
            return high, dot(jnp.concatenate([high, low], axis=1), table("call", 0, (0, 2 * LANES)))

        rows_all = x
        high, y = across(jnp.concatenate([x[f : f + 8] for firsts in (bottoms, tops) for f in firsts], axis=0))
        deep_ends = y + dot(high, table("call", 0, (2 * LANES, 3 * LANES)))

    base_g = size1 + size2

    def own_lines(x1_, x2_, g_):
        last = x1_[2] + pltpu.roll(x2_[1], 8, axis=1) + pltpu.roll(g_[1], 16, axis=1)
        return [x1_[0], x1_[1], x2_[0], g_[0], last]

    def ends(x, c, last):
        return jnp.concatenate([x[c, 8:16, :], x[c, last : last + 8, :]], axis=0)

    def filtered(y, name):
        m, cut_ = table(name), (table(name).shape[1] // LANES - 1) * LANES
        return jnp.concatenate([right(y, m[:, :cut_]), right(y[:, nc // 2 :], m[nc // 2 :, cut_:])], axis=1)

    with jax.named_scope("edge_own"):
        await_tables("s1", "s2", "c1", "c2")

        def own_ends(n, d, last, name):
            y = jnp.concatenate(
                [jnp.concatenate([ends(x, c, last) for c in own_range], axis=1) for x in (n, d)], axis=0
            )
            return filtered(y, name) if name == "c1" else right(y, table(name))

        own1, own2 = own_ends(n1, d1, last1, "c1"), own_ends(n2, d2, last2, "c2")

    with jax.named_scope("edge_side"):
        side_ends = []
        for k in range(1, 1 + ns):
            pair = []
            for n, d, last, name in ((n1, d1, last1, "s1"), (n2, d2, last2, "s2")):
                y = right(ends(n, near_tile[k], last), table(name, 2 * (k - 1)))
                pair.append(y + right(ends(d, near_tile[k], last), table(name, 2 * (k - 1) + 1)))
            side_ends.append(pair)

    def tile(x, at, c):
        return x[at : at + 8, c * LANES : (c + 1) * LANES]

    with jax.named_scope("g_pack"):
        for k in range(1 + ns):
            for rp in (1, 2):
                deep = []
                for a in range(2):
                    lines = []
                    for c in range(2):
                        index = lane8 + c * LANES
                        first = a * 64 + (rp - 1) * 32
                        lane = k * 256 + c * LANES
                        b = [deep_ends[first + 8 * l : first + 8 * l + 8, lane : lane + LANES] for l in range(4)]
                        lines.append(
                            jnp.where(
                                index < lane_cuts[0], b[0],
                                jnp.where(index < lane_cuts[1], b[1], jnp.where(index < lane_cuts[2], b[2], b[3])),
                            )
                        )
                    deep.append(lines)
                at = 8 * (2 - rp)
                if k == 0:
                    packed = [
                        own_lines(
                            [tile(own1, 16 * a + at, c) for c in range(3)],
                            [tile(own2, 16 * a + at, c) for c in range(2)],
                            deep[a],
                        )
                        for a in range(2)
                    ]
                    for t in range(OWN_TILES):
                        edge_s[rp - 1, 0, t] = pack(packed[0][t], packed[1][t])
                else:
                    lines = [y[at : at + 8] for y in side_ends[k - 1]]
                    edge_s[rp - 1, k, 0] = pack(deep[0][0], deep[1][0])
                    edge_s[rp - 1, k, 1] = (
                        lines[0] + pltpu.roll(lines[1], 8, axis=1)
                        + pltpu.roll(pack(deep[0][1], deep[1][1]), 16, axis=1)
                    )

    if early_half is not None:
        pl.when(early_half)(meet)

    with jax.named_scope("send"):
        if early_half is None:
            send_edges(lambda d: d[0] != 0)
        else:
            pl.when(jnp.logical_not(first_plane))(lambda: send_edges(lambda d: d[0] != 0))

    body1, body2 = slice(8, 8 + size1), slice(8, 8 + size2)

    with jax.named_scope("g"):
        high, y = across(rows_all)
        tail = stack - 32
        more = [dot(high[a * stack + tail : (a + 1) * stack], table("call", 0, (2 * LANES, 3 * LANES))) for a in range(2)]
        for a in range(2):
            for c in range(2):
                for k in range(1 + ns):
                    lanes_ = slice(k * 256 + c * LANES, k * 256 + (c + 1) * LANES)
                    upper = y[a * stack : a * stack + tail, lanes_]
                    lower = y[a * stack + tail : (a + 1) * stack, lanes_] + more[a][:, lanes_]
                    if k == 0:
                        g[a, c, :tail] = upper
                        g[a, c, tail:] = lower
                    else:
                        first = base_g + (2 * a + c) * stack
                        side_s[k - 1, first : first + tail, :] = upper
                        side_s[k - 1, first + tail : first + stack, :] = lower

    with jax.named_scope("x_side"):
        for k in range(1, 1 + ns):
            for base, n, d, body, name in ((0, n1, d1, body1, "s1"), (size1, n2, d2, body2, "s2")):
                y = right(n[near_tile[k], body, :], table(name, 2 * (k - 1) + 0))
                y = y + right(d[near_tile[k], body, :], table(name, 2 * (k - 1) + 1))
                side_s[k - 1, base : base + y.shape[0], :] = y
        if early_half is None:
            send_edges(lambda d: d[0] == 0)
        else:
            pl.when(jnp.logical_not(first_plane))(lambda: send_edges(lambda d: d[0] == 0))

    with jax.named_scope("x_own"):
        for n, d, body, name, dst in ((n1, d1, body1, "c1", x1), (n2, d2, body2, "c2", x2)):
            for a, y in enumerate((n, d)):
                y = wide_of(y, body, own_range)
                y = filtered(y, name) if name == "c1" else right(y, table(name))
                for c in range(dst.shape[1]):
                    dst[a, c] = y[:, c * LANES : (c + 1) * LANES]

    if early_half is not None:

        @pl.when(first_plane)
        def _():
            meet()
            send_edges(lambda d: True)

    def ratio(n, d):
        return jnp.where(d > 0, n / d, 0.0)

    def await_edges(wanted):
        for i, d in enumerate(kinds):
            if wanted(d):
                given(sends(*d), lambda: edge(i).wait_send())
                given(comes(*d), lambda: edge(i).wait_recv())

    def q_rows(x, y, rows, gain):
        for c in range(x.shape[1]):
            y[rows, c * LANES : (c + 1) * LANES] = gain * ratio(x[0, c, rows, :], x[1, c, rows, :])

    gain1, gain2 = gain_ref[1] - gain_ref[0], gain_ref[2] - gain_ref[1]

    with jax.named_scope("w_side"):
        await_edges(lambda d: d[0] == 0)
    with jax.named_scope("add_side"):
        for k in range(1, 1 + ns):
            def add():
                for base, size, x, into in ((0, size1, x1, into1[k]), (size1, size2, x2, into2[k])):
                    more = unpack_lanes(side_r[k - 1, base : base + size, :])
                    for a in range(2):
                        x[a, into] = x[a, into] + more[a]
                for a in range(2):
                    for c in range(2):
                        base = base_g + (2 * a + c) * stack
                        g[a, c] = g[a, c] + side_r[k - 1, base : base + stack, :]

            given(recv_col[k], add)
    with jax.named_scope("q"):
        q_rows(x1, y1, slice(0, size1), gain1)
        q_rows(x2, y2, slice(0, size2), gain2)

    def grow_rows(src, dst, first, count):
        x, y, w = (src[first + k : first + k + count, :] for k in (1, 2, 3))
        dst[pl.ds(2 * first, count, stride=2), :] = 0.125 * (x + w) + 0.75 * y
        dst[pl.ds(2 * first + 1, count, stride=2), :] = 0.5 * (y + w)

    def block(x, c, p, first):
        ok = jnp.logical_or(line8 >= 4, up) if first else jnp.logical_or(line8 < 4, down)
        x[c, p : p + 8, :] = jnp.where(ok, x[c, p : p + 8, :], 0.0)

    tiles2 = range(x2.shape[1])

    def mask_ends():
        for c in tiles2:
            block(z1b, c, 0, True)
            block(z1b, c, nr // 2, False)

    gain0 = gain_ref[0]

    def rise(c, m, count):
        x, y, w = (wide[c, m + k : m + k + count, :] for k in (3, 4, 5))
        even, odd = pl.ds(2 * m, count, stride=2), pl.ds(2 * m + 1, count, stride=2)
        out0[c, even, :] = gain0 * q0[c, even, :] + (0.125 * (x + w) + 0.75 * y)
        out0[c, odd, :] = gain0 * q0[c, odd, :] + 0.5 * (y + w)

    def upward(parts):
        z = [jnp.concatenate([z1b[c, p, :] for p in parts], axis=0) for c in tiles2]
        z += [
            jnp.concatenate([y1[p, c * LANES : (c + 1) * LANES] for p in parts], axis=0)
            for c in range(x1.shape[1])
        ]
        first, second = (lax.broadcasted_iota(jnp.int32, z[0].shape, 1) < k for k in (8, 16))
        t2 = len(tiles2) - 1
        ends = jnp.where(first, z[-1], jnp.where(second, pltpu.roll(z[t2], 8, axis=1), 0.0))
        z = z[:t2] + z[t2 + 1 : -1] + [ends]
        return right(jnp.concatenate(z, axis=1), table("e0"))

    with jax.named_scope("factor"):
        shape = (stack, 256)
        at_row = level_of(shape, 0, tops[1:])
        at_col = level_of(shape, 1, lane_cuts)
        gains = [gain_ref[level] - gain_ref[level - 1] for level in (3, 4, 5)] + [-gain_ref[5]]
        value = jnp.where(
            at_row == 0, gains[0], jnp.where(at_row == 1, gains[1], jnp.where(at_row == 2, gains[2], gains[3]))
        )
        factor[...] = jnp.where(at_row == at_col, value, 0.0)

    with jax.named_scope("base"):
        await_tables("e0")
        for c in tiles2:
            z2b[c] = y2[:, c * LANES : (c + 1) * LANES]
            grow_rows(z2b.at[c], z1b.at[c], 0, nr // 4 + 8)
        mask_ends()
        base = upward((slice(0, size1),))
        for c in own_range:
            wide[c] = base[:, c * LANES : (c + 1) * LANES]
        for c in own_range:
            for m in range(0, nr // 2, 32):
                rise(c, m, 32)

    with jax.named_scope("w_edges"):
        await_edges(lambda d: d[0] != 0)
        await_tables("ec0", "r012", "er", "second")
    packed_lanes = jnp.logical_and(lane8 % (LANES // 2) >= MIDDLE[0], lane8 % (LANES // 2) <= MIDDLE[-1])
    with jax.named_scope("edges"):
        for rp, at1, at2, firsts in ((1, 0, 0, tops), (2, nr // 2, nr // 4, bottoms)):
            def moved_to(y, by, ok):
                return [jnp.where(ok, pltpu.roll(z, LANES - by, axis=1), 0.0) for z in y]

            got = edge_r.at[rp - 1, 0]
            tail = unpack(got[OWN_TILES - 1])
            adds1 = [unpack(got[0]), unpack(got[1]), [jnp.where(lane8 < 8, y, 0.0) for y in tail]]
            adds2 = [unpack(got[2]), moved_to(tail, 8, lane8 < 8)]
            deep = [unpack(got[3]), moved_to(tail, 16, lane8 < 32)]
            for cp in range(1, 1 + ns):
                y = edge_r[rp - 1, cp, 1]
                for a, more in enumerate(unpack(edge_r[rp - 1, cp, 0])):
                    deep[0][a] = deep[0][a] + more
                for a, more in enumerate(moved_to(unpack(y), 16, lane8 < 32)):
                    deep[1][a] = deep[1][a] + more
            for x, at, adds in ((x1, at1, adds1), (x2, at2, adds2)):
                for c, more in enumerate(adds):
                    for a in range(2):
                        x[a, c, at : at + 8, :] = x[a, c, at : at + 8, :] + more[a]
            for cp in range(1, 1 + ns):
                y = edge_r[rp - 1, cp, 1]
                for x, at, into, z in ((x1, at1, into1[cp], y), (x2, at2, into2[cp], pltpu.roll(y, LANES - 8, axis=1))):
                    for a, more in enumerate(unpack_lanes(jnp.where(packed_lanes, z, 0.0))):
                        x[a, into, at : at + 8, :] = x[a, into, at : at + 8, :] + more
            for c in range(2):
                for a in range(2):
                    for f in firsts:
                        g[a, c, f : f + 8, :] = g[a, c, f : f + 8, :] + deep[c][a]
        for x, y, at, gain in ((x1, y1, nr // 2, gain1), (x2, y2, nr // 4, gain2)):
            q_rows(x, y, slice(0, 8), gain)
            q_rows(x, y, slice(at, at + 8), gain)
    with jax.named_scope("fix"):
        for c in tiles2:
            for at in (0, nr // 4):
                z2b[c, at : at + 8, :] = y2[at : at + 8, c * LANES : (c + 1) * LANES]
                grow_rows(z2b.at[c], z1b.at[c], at, 8)
        mask_ends()
        parts = (slice(0, 16), slice(nr // 2, nr // 2 + 16))
        base = upward(parts)
        for c in own_range:
            for i, p in enumerate(parts):
                wide[c, p, :] = base[16 * i : 16 * i + 16, c * LANES : (c + 1) * LANES]
            rise(c, 0, 8)
            rise(c, nr // 2 - 8, 8)

    with jax.named_scope("deep"):
        n, d = (jnp.concatenate([g[a, 0], g[a, 1]], axis=1) for a in range(2))
        x = jnp.where(d > 0, factor[...] * (n / d), 0.0)
        high, low = split(x)
        er = [table("er", k) for k in (0, 1)]
        x = dot(er[0], high) + dot(er[0], low) + dot(er[1], high)
        high, low = split(x)
        x = dot(high, table("ec0")) + dot(low, table("ec0")) + dot(high, table("ec0", 1))

    with jax.named_scope("w_top"):
        everything = pltpu.make_async_copy(slots, slots, precv)
        everything.wait()
        pltpu.make_async_copy(slots, slots, psend).wait()
    with jax.named_scope("top"):
        total = part[...] + jnp.sum(slots[...], axis=0)
        top_sum = jnp.sum(jnp.where(lane1 < LANES // 2, total, 0.0), axis=1, keepdims=True)
        top_weight = jnp.sum(jnp.where(lane1 < LANES // 2, 0.0, total), axis=1, keepdims=True)
        top_line = (top_sum / top_weight) * table("line", 0, (1, 2))
        ones = table("second")
        x = x + jnp.concatenate(
            [ones * top_line[:, c * LANES : (c + 1) * LANES] for c in own_range], axis=1
        )
        high, low = split(x)
        us_ref[...] = jnp.concatenate([high, high, low], axis=0)


def last(base_ref, us_ref, rows_ref, out_ref, buf, sem):
    nr, nc = buf.shape
    step = nr // sem.shape[0]
    writes = []
    for k in range(sem.shape[0]):
        here = slice(k * step, (k + 1) * step)
        y = dot(rows_ref[here, :], us_ref[...])
        for c in range(base_ref.shape[0]):
            cols = slice(c * LANES, (c + 1) * LANES)
            buf[here, cols] = base_ref[c, here, :] + y[:, cols]
        writes.append(pltpu.make_async_copy(buf.at[here, :], out_ref.at[here, :], sem.at[k]))
        writes[-1].start()
    for write in writes:
        write.wait()


def local(mesh_shape, heights, scene_ids, scene_offset, scene_weight, band_gain):
    nx, ny, nz = mesh_shape
    nr, nc = heights.shape
    ns = 1 if nx == 2 else 2
    made = tables(nr, nc, nx, ny * nz)
    given, places = merge(made)
    sizes = (nr, nc, nx, ny, nz, ns)
    ext = (nr + 2 * HALO, nc)
    tiles = nc // LANES
    own_tiles = tiles
    m3 = nr // 8 + 8
    size1, size2, stack = nr // 2 + 16, nr // 4 + 16, nr // 8 + nr // 16 + nr // 32 + nr // 64 + 40
    tiles1, tiles2 = nc // 2 // LANES + 1, nc // 4 // LANES + 1
    beside = size1 + size2 + 4 * stack
    peers = nx * ny * nz - 1
    messages = 3 * (1 + ns) - 1
    hbm = pl.BlockSpec(memory_space=pltpu.HBM)
    deep_rows = made["r012"].shape[-1]
    vmem = pl.BlockSpec(memory_space=pltpu.VMEM)
    kept = pl.pallas_call(
        functools.partial(kernel, sizes, places),
        out_shape=(
            pltpu.VMEM((own_tiles, nr, LANES), F32),
            pltpu.VMEM((deep_rows, nc), BF16),
            pltpu.VMEM((nr, deep_rows), BF16),
        ),
        in_specs=[hbm] * (5 + len(given)),
        out_specs=(vmem, vmem, vmem),
        scratch_shapes=[pltpu.VMEM(x.shape[1:], x.dtype) for x in given[:-1]]
        + [
            pltpu.SMEM(scene_offset.shape, F32),
            pltpu.SMEM(scene_weight.shape, F32),
            pltpu.SMEM(band_gain.shape, F32),
            pltpu.VMEM(ext, F32),
            pltpu.VMEM(ext, jnp.int32),
            pltpu.VMEM((own_tiles, nr, LANES), F32),
        ]
        + [pltpu.VMEM((tiles, nr + 3 * HALO, LANES), F32)] * 2
        + [pltpu.VMEM((tiles, nr // 2 + 32, LANES), F32)] * 2
        + [pltpu.VMEM((tiles, nr // 4 + 24, LANES), F32)] * 2
        + [pltpu.VMEM((own_tiles, m3, LANES), F32)] * 2
        + [
            pltpu.VMEM((2, tiles1, size1, LANES), F32),
            pltpu.VMEM((2, tiles2, size2, LANES), F32),
            pltpu.VMEM((2, 2, stack, LANES), F32),
            pltpu.VMEM((stack, 256), F32),
            pltpu.VMEM((size1, tiles1 * LANES), F32),
            pltpu.VMEM((size2, tiles2 * LANES), F32),
            pltpu.VMEM((ns, beside, LANES), F32),
            pltpu.VMEM((ns, beside, LANES), F32),
            pltpu.VMEM((2, 1 + ns, OWN_TILES, 8, LANES), F32),
            pltpu.VMEM((2, 1 + ns, OWN_TILES, 8, LANES), F32),
            pltpu.VMEM((tiles2, nr // 4 + 16, LANES), F32),
            pltpu.VMEM((tiles2, nr // 2 + 16, LANES), F32),
            pltpu.VMEM((own_tiles, nr // 2 + 16, LANES), F32),
            pltpu.VMEM((1, LANES), F32),
            pltpu.VMEM((peers, 1, LANES), F32),
            pltpu.SemaphoreType.DMA((CHUNKS + 3,)),
            pltpu.SemaphoreType.DMA((len(given),)),
            pltpu.SemaphoreType.DMA((messages,)),
            pltpu.SemaphoreType.DMA((messages,)),
            pltpu.SemaphoreType.DMA(()),
            pltpu.SemaphoreType.DMA(()),
        ],
        compiler_params=pltpu.CompilerParams(collective_id=0, has_side_effects=True),
    )(scene_offset, scene_weight, band_gain, heights, scene_ids, *given)
    return pl.pallas_call(
        last,
        out_shape=jax.ShapeDtypeStruct((nr, nc), F32),
        in_specs=[vmem] * 3,
        out_specs=pl.BlockSpec(memory_space=pltpu.HBM),
        scratch_shapes=[pltpu.VMEM((nr, nc), F32), pltpu.SemaphoreType.DMA((PIECES,))],
        compiler_params=pltpu.CompilerParams(vmem_limit_bytes=16 * 1024 * 1024),
    )(*kept)


def solution(mesh):
    placed = (P(("gy", "gz"), "gx"), P(("gy", "gz"), "gx"), P(), P(), P())
    shape = tuple(mesh.shape[name] for name in ("gx", "gy", "gz"))
    return jax.shard_map(
        functools.partial(local, shape), mesh=mesh, in_specs=placed,
        out_specs=P(("gy", "gz"), "gx"), check_vma=False,
    )
```

```python
import functools

import jax
import jax.numpy as jnp
import numpy as np
from jax import lax
from jax.experimental import pallas as pl
from jax.experimental.pallas import tpu as pltpu
from jax.sharding import PartitionSpec as P

F32, BF16 = jnp.float32, jnp.bfloat16
FAR = 1 << 20
HALO = 16
LANES = 128
LEVELS = 6
MIDDLE = (3, 4, 5)


def reach(count, levels):
    weights = np.ones(count >> levels, np.float64)
    for _ in range(levels):
        fine = np.zeros(2 * weights.size + 4, np.float64)
        for tap, value in zip(range(-2, 3), (0.0625, 0.25, 0.375, 0.25, 0.0625)):
            fine[2 + tap : 2 + tap + 2 * weights.size : 2] += value * weights
        weights = fine[2:-2]
    return weights


class Axis:
    def __init__(self, n, at, count):
        self.n, self.at, self.count = n, at, count

    def inside(self, index, level):
        place = index + self.at * (self.n >> level)
        return (place >= 0) & (place < self.count * (self.n >> level))

    def shrink(self, fine, coarse, level):
        far = np.abs(fine[:, None] - 2 * coarse[None, :])
        value = np.select([far == 0, far == 1, far == 2], [0.375, 0.25, 0.0625], 0.0)
        return value * self.inside(coarse, level)[None, :]

    def grow(self, coarse, fine, level):
        far = np.abs(2 * coarse[:, None] - fine[None, :])
        value = np.select([far == 0, far == 1, far == 2], [0.75, 0.5, 0.125], 0.0)
        return value * self.inside(fine, level)[None, :]

    def window(self, level, edge):
        return np.arange(-edge, (self.n >> level) + edge)

    def deep(self, lanes, shift=0):
        out = [x + shift * (self.n >> level) for level, x in zip((3, 4, 5, 6), self.out())]
        w4, w5 = self.window(4, 30), self.window(5, 14)
        to4 = self.shrink(lanes, w4, 4)
        to5 = to4 @ self.shrink(w4, w5, 5)
        same = (lanes[:, None] == out[0][None, :]) * self.inside(out[0], 3)[None, :]
        parts = [
            same * 1.0,
            self.shrink(lanes, out[1], 4),
            to4 @ self.shrink(w4, out[2], 5),
            to5 @ self.shrink(w5, out[3], 6),
        ]
        return np.concatenate(parts, axis=1) * self.inside(lanes, 3)[:, None]

    def out(self):
        low = -4
        return [low + np.arange(size) for size in self.sizes()]

    def sizes(self):
        return [self.n // 8 + 8, self.n // 16 + 8, self.n // 32 + 8, self.n // 64 + 16]

    def back(self):
        o3, o4, o5, o6 = self.out()
        w4, w5 = self.window(4, 4), self.window(5, 4)
        from4 = self.grow(w4, o3, 3)
        from5 = self.grow(w5, w4, 4) @ from4
        parts = [
            np.eye(o3.size) * self.inside(o3, 3)[None, :],
            self.grow(o4, o3, 3),
            self.grow(o5, w4, 4) @ from4,
            self.grow(o6, w5, 5) @ from5,
        ]
        return np.concatenate(parts, axis=0)

    def sums(self, level, place):
        weights = reach(self.count * (self.n >> level), LEVELS - level)
        place = place + self.at * (self.n >> level)
        return np.where((place >= 0) & (place < weights.size), weights[np.clip(place, 0, weights.size - 1)], 0.0)

    def ones(self, level):
        x = self.inside(self.window(6, 4), 6) * 1.0
        for k in range(5, level - 1, -1):
            x = x @ self.grow(self.window(k + 1, 4), self.window(k, 4), k)
        return x


def pad(x, shape):
    return np.pad(x, [(0, size - have) for size, have in zip(shape, x.shape)])


def halves(x):
    high = x.astype(np.float32).astype(jnp.bfloat16)
    low = (x - high.astype(np.float64)).astype(np.float32).astype(jnp.bfloat16)
    return high, low


def spaced(n):
    size = -(-(n + 8) // LANES) * LANES
    return np.concatenate([np.arange(-4, n + 4), np.full(size - n - 8, FAR)])


def col_tables(n, at, count):
    ax = Axis(n, at, count)
    shifts = [1 if at == 0 else -1] if count == 2 else [1, -1]
    lane = np.arange(LANES)
    own = np.arange(n)
    out1, out2 = spaced(n // 2), spaced(n // 4)
    w1, w2 = ax.window(1, 16), ax.window(2, 8)
    middle = np.isin(lane, MIDDLE)[None, :]
    s1, s2 = [], []
    for d in shifts:
        near = n - LANES + lane if d > 0 else lane
        over1, over2 = (lane - 4 + (n >> level if d > 0 else 0) for level in (1, 2))
        s1.append(ax.shrink(near, over1, 1) * middle)
        s2.append(ax.shrink(near, w1, 1) @ ax.shrink(w1, over2, 2) * middle)
    s1, s2 = (np.stack([np.stack([x, np.roll(x, LANES // 2, 1)]) for x in y]) for y in (s1, s2))
    o3 = ax.out()[0]
    to2 = ax.shrink(own, w1, 1)
    c03 = to2 @ ax.shrink(w1, w2, 2) @ ax.shrink(w2, o3, 3)
    c03 = np.concatenate([pad(x.astype(np.float64), (n, LANES)) for x in halves(c03)], axis=1)
    three = np.concatenate([o3, np.full(LANES - o3.size, FAR)])
    call = []
    for d in [0] + shifts:
        call.append([pad(x.astype(np.float64), (LANES, 256)) for x in halves(ax.deep(three, d))])
    high, low = (np.concatenate([x[k] for x in call], axis=1) for k in range(2))
    call = np.concatenate([high, high, low], axis=0)
    back = ax.back()
    to0 = ax.grow(w2, w1, 1) @ ax.grow(w1, own, 0)
    from1, from2 = ax.grow(out1, own, 0), ax.grow(out2, out1, 1) @ ax.grow(out1, own, 0)
    m1, m2 = n // 2, n // 4
    e0 = np.concatenate([from2[:m2], from1[:m1], from1[m1 : m1 + 8], from2[m2 : m2 + 8]], axis=0)
    e0 = pad(e0, (m1 + m2 + LANES, n))
    ec0 = np.stack([pad(x.astype(np.float64), (256, n)) for x in halves(back @ ax.grow(o3, w2, 2) @ to0)])
    return dict(
        c1=ax.shrink(own, out1, 1), c2=to2 @ ax.shrink(w1, out2, 2), s1=s1, s2=s2, c03=c03, call=call,
        ec0=ec0, e0=e0,
    ), dict(line=np.stack([ax.sums(0, own), ax.ones(0)[4:-4]]))


def row_tables(n, at, count):
    ax = Axis(n, at, count)
    o3 = ax.out()[0]
    deep = ax.deep(o3).T
    high, low = (x.astype(np.float64) for x in halves(deep))
    size6 = ax.sizes()[3]
    rall = np.concatenate([high, low[-size6:]], axis=0)
    rall = pad(rall, (-(-rall.shape[0] // 16) * 16, -(-o3.size // 16) * 16))
    rall = np.concatenate([rall, rall], axis=1)
    back = ax.back()
    deep_rows = -(-o3.size // 16) * 16
    er = np.stack([pad(x.astype(np.float64), (deep_rows, x.shape[1])) for x in halves(back.T)])
    first = np.repeat(ax.sums(3, o3)[:, None], LANES, 1)
    w1, w2 = ax.window(1, 8), ax.window(2, 8)
    r012 = (ax.grow(o3, w2, 2) @ ax.grow(w2, w1, 1) @ ax.grow(w1, np.arange(n), 0)).T
    high, low = (pad(x.astype(np.float64), (n, deep_rows)) for x in halves(r012))
    r012 = np.concatenate([high, low, high], axis=1)
    second = np.repeat(pad(ax.ones(3), (deep_rows,))[:, None], LANES, 1)
    return dict(rall=rall, er=er, r012=r012), dict(first=first, second=second)


def tables(nr, nc, nx, blocks):
    def places(count):
        return (0, 1) if count == 2 else (0, 1, count - 1)

    cols = [col_tables(nc, at, nx) for at in places(nx)]
    rows = [row_tables(nr, at, blocks) for at in places(blocks)]

    def cast(x):
        return jnp.asarray(np.asarray(x, np.float32)).astype(BF16)

    def keep(x):
        return jnp.asarray(np.asarray(x, np.float32))

    out = {}
    for some in (cols, rows):
        for k in some[0][0]:
            out[k] = cast(np.stack([x[0][k] for x in some]))
        for k in some[0][1]:
            out[k] = keep(np.stack([x[1][k] for x in some]))
    return out


def merge(made):
    arrays, places = [], {}
    for at, group in enumerate(COLS + ROWS):
        lanes = max(made[name].shape[-1] for name in group)
        parts, start = [], 0
        for name in group:
            x = made[name]
            rows, width = x.shape[-2:]
            x = x.reshape(x.shape[0], -1, rows, width)
            tall = -(-rows // 16) * 16 if len(group) > 1 else rows
            x = jnp.pad(x, ((0, 0), (0, 0), (0, tall - rows), (0, lanes - width)))
            places[name] = (at, start, tall, rows, width)
            start += x.shape[1] * tall
            parts.append(x.reshape(x.shape[0], -1, lanes))
        arrays.append(jnp.concatenate(parts, axis=1))
    return arrays, places


def split(x):
    high = x.astype(BF16)
    return high, (x - high.astype(F32)).astype(BF16)


def dot(a, b):
    return jnp.dot(a, b, preferred_element_type=F32)


def right(x, c):
    high, low = split(x)
    return dot(high, c) + dot(low, c)


COLS = (("c03", "c2"), ("call", "e0", "ec0"), ("c1",), ("s1", "s2"), ("line",))
ROWS = (("rall", "er"), ("first", "second"), ("r012",))
OWN_TILES, SIDE_TILES = 5, 2
CHUNKS = 4
PIECES = 8


def kernel(
    sizes, places, off_hbm, wgt_hbm, gain_hbm, h_ref, s_ref, *rest
):
    nr, nc, nx, ny, nz, ns = sizes
    count = len(COLS) + len(ROWS)
    tables_hbm, rest = rest[:count], rest[count:]
    out0, us_ref, r012_ref, rest = *rest[:3], rest[3:]
    tab, rest = (*rest[: count - 1], r012_ref), rest[count - 1 :]
    (
        off_ref, wgt_ref, gain_ref, h_buf, s_buf, q0, num, den, n1, d1, n2, d2, n3, d3,
        x1, x2, g, factor, y1, y2, side_s, side_r, edge_s, edge_r, z2b, z1b, wide, part, slots,
        own_sem, tab_sem, send0, recv0, psend, precv,
    ) = rest
    cx, cy, cz = lax.axis_index("gx"), lax.axis_index("gy"), lax.axis_index("gz")
    row = cy * nz + cz
    blocks = ny * nz
    own_tiles = nc // LANES
    t3 = nr // 8
    m3 = t3 + 8

    def kind(at, count):
        return at if count == 2 else jnp.where(at == 0, 0, jnp.where(at == count - 1, 2, 1))

    ct, rt = kind(cx, nx), kind(row, blocks)

    loads = []
    step = nr // CHUNKS
    for k in range(CHUNKS):
        rows = pl.ds(k * step, step)
        for a, (src, dst) in enumerate(((h_ref, h_buf), (s_ref, s_buf))):
            loads.append(
                pltpu.make_async_copy(
                    src.at[rows, :],
                    dst.at[pl.ds(HALO + k * step, step), pl.ds(0, nc)],
                    own_sem.at[k],
                )
            )
    small = [
        pltpu.make_async_copy(src, dst, own_sem.at[CHUNKS + a])
        for a, (src, dst) in enumerate(((off_hbm, off_ref), (wgt_hbm, wgt_ref), (gain_hbm, gain_ref)))
    ]
    fetch = [
        pltpu.make_async_copy(src.at[ct if i < len(COLS) else rt], tab[i], tab_sem.at[i])
        for i, src in enumerate(tables_hbm)
    ]
    ready = set()

    def await_tables(*names):
        for name in names:
            if places[name][0] not in ready:
                ready.add(places[name][0])
                fetch[places[name][0]].wait()

    def table(name, k=0, rows=None):
        at, start, tall, height, width = places[name]
        first, last = rows or (0, height)
        return tab[at][start + k * tall + first : start + k * tall + last, :width]

    for copy in loads[:2] + small + loads[2:]:
        copy.start()

    up, down = row > 0, row < blocks - 1
    send_row, recv_row = {0: None, 1: down, 2: up}, {0: None, 1: up, 2: down}
    if ns == 1:
        send_col, recv_col = {0: None, 1: None}, {0: None, 1: None}
        to_col = {0: cx, 1: 1 - cx}
        near_tile = {1: (1 - cx) * (own_tiles - 1)}
        into1, into2 = {1: (1 - cx) * (x1.shape[1] - 1)}, {1: (1 - cx) * (x2.shape[1] - 1)}
    else:
        send_col = {0: None, 1: cx < nx - 1, 2: cx > 0}
        recv_col = {0: None, 1: cx > 0, 2: cx < nx - 1}
        to_col = {0: cx, 1: cx + 1, 2: cx - 1}
        near_tile = {1: own_tiles - 1, 2: 0}
        into1, into2 = {1: 0, 2: x1.shape[1] - 1}, {1: 0, 2: x2.shape[1] - 1}
    kinds = [(rp, cp) for rp in (0, 1, 2) for cp in range(1 + ns) if rp or cp]

    def device(rp, cp):
        target = row + {0: 0, 1: 1, 2: -1}[rp]
        return {"gx": to_col[cp], "gy": target // nz, "gz": target % nz}

    def also(a, b):
        return b if a is None else a if b is None else jnp.logical_and(a, b)

    def sends(rp, cp):
        return also(send_row[rp], send_col[cp])

    def comes(rp, cp):
        return also(recv_row[rp], recv_col[cp])

    def given(flag, body):
        if flag is None:
            body()
        else:
            pl.when(flag)(body)

    everyone = nx * blocks
    me = row * nx + cx

    def peer(s):
        other = (me + s) % everyone
        line = other // nx
        return {"gx": other % nx, "gy": line // nz, "gz": line % nz}

    def places_of(at, count):
        return [jnp.where(at + d < count, at + d, at + d - count) for d in range(count)]

    def others(body):
        if everyone <= 64:
            xs, ys, zs = places_of(cx, nx), places_of(cy, ny), places_of(cz, nz)
            for s in range(1, everyone):
                line = s // nx
                body(s, {"gx": xs[s % nx], "gy": ys[line // nz], "gz": zs[line % nz]})
        else:
            def step_(s, carry):
                body(s, peer(s))
                return carry

            lax.fori_loop(1, everyone, step_, 0)

    barrier = pltpu.get_barrier_semaphore()
    others(lambda s, who: pl.semaphore_signal(barrier, inc=1, device_id=who))

    for copy in fetch:
        copy.start()

    zero = jnp.zeros((HALO, LANES), F32)
    for x in (num, den):
        for c in range(own_tiles):
            x[c, 0:HALO, :] = zero
            x[c, nr + HALO : nr + 2 * HALO, :] = zero
            x[c, nr + 2 * HALO :, :] = zero
    zero = jnp.zeros((8, LANES), F32)
    for x in (n1, d1, n2, d2):
        for c in range(own_tiles):
            x[c, 0:8, :] = zero
            x[c, x.shape[1] - 8 :, :] = zero

    for rp, cp in kinds:
        if rp and comes(rp, cp) is not None:
            @pl.when(jnp.logical_not(comes(rp, cp)))
            def _():
                edge_r[rp - 1, cp] = jnp.zeros((OWN_TILES, 8, LANES), F32)

    def edge(i):
        rp, cp = kinds[i]
        if rp == 0:
            src, dst = side_s.at[cp - 1], side_r.at[cp - 1]
        else:
            place = pl.ds(0, OWN_TILES) if cp == 0 else pl.ds(0, SIDE_TILES)
            src, dst = edge_s.at[rp - 1, cp, place], edge_r.at[rp - 1, cp, place]
        return pltpu.make_async_remote_copy(
            src_ref=src, dst_ref=dst, send_sem=send0.at[i], recv_sem=recv0.at[i], device_id=device(rp, cp)
        )

    lane8 = lax.broadcasted_iota(jnp.int32, (8, LANES), 1)
    line8 = lax.broadcasted_iota(jnp.int32, (8, LANES), 0)

    def spread(table):
        line = jnp.zeros((8, LANES), F32)
        for i in range(table.shape[0]):
            line = jnp.where(lane8 == i, table[i], line)
        return line

    for copy in small:
        copy.wait()
    wgt_row = spread(wgt_ref)

    def tree(ids, table):
        values = [table[i] for i in range(table.shape[0])]
        bit = 1
        while len(values) > 1:
            mask = (ids & bit) != 0
            values = [jnp.where(mask, values[i + 1], values[i]) for i in range(0, len(values), 2)]
            bit *= 2
        return values[0]

    def level0(base, count, c):
        rows = pl.ds(base, count)
        ids = s_buf[rows, c * LANES : (c + 1) * LANES]
        weight = jnp.concatenate(
            [jnp.take_along_axis(wgt_row, ids[r : r + 8], axis=1) for r in range(0, count, 8)], axis=0
        )
        moved = h_buf[rows, c * LANES : (c + 1) * LANES] + tree(ids, off_ref)
        num[c, rows, :] = weight * moved
        den[c, rows, :] = weight
        return moved

    def summary(s, who):
        return pltpu.make_async_remote_copy(
            src_ref=part,
            dst_ref=slots.at[s - 1],
            send_sem=psend,
            recv_sem=precv,
            device_id=who,
        )

    def send_edges(wanted):
        for i, d in enumerate(kinds):
            if wanted(d):
                given(sends(*d), lambda: edge(i).start())

    lane1 = lax.broadcasted_iota(jnp.int32, (1, LANES), 1)

    def meet():
        with jax.named_scope("meet"):
            pl.semaphore_wait(barrier, everyone - 1)

        others(lambda s, who: summary(s, who).start())

    def taps(src, c, start, count):
        x = [src[c, pl.ds(start + a, count, stride=2), :] for a in range(-2, 3)]
        return 6.0 * x[2] + (4.0 * (x[1] + x[3]) + (x[0] + x[4]))

    def hold(x, c, p, first):
        if first:
            ok = jnp.logical_or(line8 >= 4, up)
        else:
            ok = jnp.logical_or(line8 < 4, down)
        x[c, p : p + 8, :] = jnp.where(ok, x[c, p : p + 8, :], 0.0)

    last1, last2 = nr // 2 + 8, nr // 4 + 8

    def rows1(src, dst, c, p, count):
        dst[c, p : p + count, :] = taps(src, c, 2 * p - 8, count)

    def rows2(src, dst, c, p, count):
        dst[c, p : p + count, :] = taps(src, c, 2 * p - 12, count)

    pairs = ((num, n1, n2, n3), (den, d1, d2, d3))
    part1, part2 = step // 2, nr // 8

    def group1(k):
        count = part1 if k < CHUNKS - 1 else part1 + 16
        for src, one, _, _ in pairs:
            for c in range(own_tiles):
                rows1(src, one, c, 8 + k * part1, count)
                if k == 0:
                    hold(one, c, 8, True)
                if k == CHUNKS - 1:
                    hold(one, c, last1, False)

    def group2(k):
        for _, one, two, _ in pairs:
            for c in range(own_tiles):
                rows2(one, two, c, 8 + k * part2, part2 + 8 * k)
                hold(two, c, last2 if k else 8, not k)

    with jax.named_scope("level0"):
        for k in range(CHUNKS):
            both = pl.ds(0, 2 * step)
            pltpu.make_async_copy(h_ref.at[both, :], h_buf.at[both, pl.ds(0, nc)], own_sem.at[k]).wait()
            for c in range(own_tiles):
                q0[c, k * step : (k + 1) * step, :] = level0(HALO + k * step, step, c)
            if k:
                group1(k - 1)
            if k == CHUNKS - 1:
                group2(0)

    with jax.named_scope("rowpyr"):
        group1(CHUNKS - 1)
        group2(1)
        for _, _, two, three in pairs:
            for c in range(own_tiles):
                three[c] = taps(two, c, 4, m3)

    with jax.named_scope("sums"):
        await_tables("line", "first")
        flat = []
        for x in (n3, d3):
            y = sum(x[c] * table("line", 0, (0, 1))[:, c * LANES : (c + 1) * LANES] for c in range(own_tiles))
            y = jnp.sum(y * table("first"), axis=0, keepdims=True)
            flat.append(y + pltpu.roll(y, LANES // 2, axis=1))
        part[...] = jnp.where(lane1 < LANES // 2, flat[0], flat[1])

    early_half = jnp.logical_and(cz > 0, cz < nz // 2) if nz > 1 else None
    first_plane = cz == 0
    if early_half is None:
        meet()
    else:
        pl.when(cz >= nz // 2)(meet)
    def wide_of(x, rows, tiles):
        return jnp.concatenate([x[c, rows, :] for c in tiles], axis=1)

    own_range = range(own_tiles)
    size1, size2 = x1.shape[2], x2.shape[2]
    s3, s4, s5, s6 = (nr // 8 + 8, nr // 16 + 8, nr // 32 + 8, nr // 64 + 16)
    stack = s3 + s4 + s5 + s6
    tops = (0, s3, s3 + s4, s3 + s4 + s5)
    bottoms = tuple(top + (nr >> level) for top, level in zip(tops, (3, 4, 5, 6)))

    def level_of(shape, dim, cuts):
        index = lax.broadcasted_iota(jnp.int32, shape, dim)
        return sum((index >= cut).astype(jnp.int32) for cut in cuts)

    c3, c4, c5 = nc // 8 + 8, nc // 16 + 8, nc // 32 + 8
    lane_cuts = (c3, c3 + c4, c3 + c4 + c5)
    middle = jnp.logical_and(line8 >= MIDDLE[0], line8 <= MIDDLE[-1])

    def pack(n, d):
        return jnp.where(middle, n, pltpu.roll(d, 4, axis=0))

    def unpack(x):
        return [jnp.where(middle, x, 0.0), jnp.where(middle, pltpu.roll(x, 4, axis=0), 0.0)]

    def unpack_lanes(x):
        low = lax.broadcasted_iota(jnp.int32, x.shape, 1) < LANES // 2
        return jnp.where(low, x, 0.0), jnp.where(low, pltpu.roll(x, LANES // 2, axis=1), 0.0)

    with jax.named_scope("p3"):
        await_tables("c03", "rall", "call")
        x = jnp.concatenate([wide_of(n3, slice(None), own_range), wide_of(d3, slice(None), own_range)], axis=0)
        x = right(x, table("c03"))
        x = x[:, :LANES] + x[:, LANES:]
        high, low = split(jnp.concatenate([x[:m3], x[m3:]], axis=1))
        gap = jnp.zeros((-m3 % 16, 2 * LANES), BF16)
        x = dot(table("rall"), jnp.concatenate([high, gap, low, gap], axis=0))
        x = jnp.concatenate([x[: stack - s6], x[stack - s6 : stack] + x[stack : stack + s6]], axis=0)
        def across(y):
            y = jnp.concatenate([y[:, :LANES], y[:, LANES:]], axis=0)
            high, low = split(y)
            return high, dot(jnp.concatenate([high, low], axis=1), table("call", 0, (0, 2 * LANES)))

        rows_all = x
        high, y = across(jnp.concatenate([x[f : f + 8] for firsts in (bottoms, tops) for f in firsts], axis=0))
        deep_ends = y + dot(high, table("call", 0, (2 * LANES, 3 * LANES)))

    base_g = size1 + size2

    def own_lines(x1_, x2_, g_):
        last = x1_[2] + pltpu.roll(x2_[1], 8, axis=1) + pltpu.roll(g_[1], 16, axis=1)
        return [x1_[0], x1_[1], x2_[0], g_[0], last]

    def ends(x, c, last):
        return jnp.concatenate([x[c, 8:16, :], x[c, last : last + 8, :]], axis=0)

    def filtered(y, name):
        m, cut_ = table(name), (table(name).shape[1] // LANES - 1) * LANES
        return jnp.concatenate([right(y, m[:, :cut_]), right(y[:, nc // 2 :], m[nc // 2 :, cut_:])], axis=1)

    with jax.named_scope("edge_own"):
        await_tables("s1", "s2", "c1", "c2")

        def own_ends(n, d, last, name):
            y = jnp.concatenate(
                [jnp.concatenate([ends(x, c, last) for c in own_range], axis=1) for x in (n, d)], axis=0
            )
            return filtered(y, name) if name == "c1" else right(y, table(name))

        own1, own2 = own_ends(n1, d1, last1, "c1"), own_ends(n2, d2, last2, "c2")

    with jax.named_scope("edge_side"):
        side_ends = []
        for k in range(1, 1 + ns):
            pair = []
            for n, d, last, name in ((n1, d1, last1, "s1"), (n2, d2, last2, "s2")):
                y = right(ends(n, near_tile[k], last), table(name, 2 * (k - 1)))
                pair.append(y + right(ends(d, near_tile[k], last), table(name, 2 * (k - 1) + 1)))
            side_ends.append(pair)

    def tile(x, at, c):
        return x[at : at + 8, c * LANES : (c + 1) * LANES]

    with jax.named_scope("g_pack"):
        for k in range(1 + ns):
            for rp in (1, 2):
                deep = []
                for a in range(2):
                    lines = []
                    for c in range(2):
                        index = lane8 + c * LANES
                        first = a * 64 + (rp - 1) * 32
                        lane = k * 256 + c * LANES
                        b = [deep_ends[first + 8 * l : first + 8 * l + 8, lane : lane + LANES] for l in range(4)]
                        lines.append(
                            jnp.where(
                                index < lane_cuts[0], b[0],
                                jnp.where(index < lane_cuts[1], b[1], jnp.where(index < lane_cuts[2], b[2], b[3])),
                            )
                        )
                    deep.append(lines)
                at = 8 * (2 - rp)
                if k == 0:
                    packed = [
                        own_lines(
                            [tile(own1, 16 * a + at, c) for c in range(3)],
                            [tile(own2, 16 * a + at, c) for c in range(2)],
                            deep[a],
                        )
                        for a in range(2)
                    ]
                    for t in range(OWN_TILES):
                        edge_s[rp - 1, 0, t] = pack(packed[0][t], packed[1][t])
                else:
                    lines = [y[at : at + 8] for y in side_ends[k - 1]]
                    edge_s[rp - 1, k, 0] = pack(deep[0][0], deep[1][0])
                    edge_s[rp - 1, k, 1] = (
                        lines[0] + pltpu.roll(lines[1], 8, axis=1)
                        + pltpu.roll(pack(deep[0][1], deep[1][1]), 16, axis=1)
                    )

    if early_half is not None:
        pl.when(early_half)(meet)

    with jax.named_scope("send"):
        if early_half is None:
            send_edges(lambda d: d[0] != 0)
        else:
            pl.when(jnp.logical_not(first_plane))(lambda: send_edges(lambda d: d[0] != 0))

    body1, body2 = slice(8, 8 + size1), slice(8, 8 + size2)

    with jax.named_scope("g"):
        high, y = across(rows_all)
        tail = stack - 32
        more = [dot(high[a * stack + tail : (a + 1) * stack], table("call", 0, (2 * LANES, 3 * LANES))) for a in range(2)]
        for a in range(2):
            for c in range(2):
                for k in range(1 + ns):
                    lanes_ = slice(k * 256 + c * LANES, k * 256 + (c + 1) * LANES)
                    upper = y[a * stack : a * stack + tail, lanes_]
                    lower = y[a * stack + tail : (a + 1) * stack, lanes_] + more[a][:, lanes_]
                    if k == 0:
                        g[a, c, :tail] = upper
                        g[a, c, tail:] = lower
                    else:
                        first = base_g + (2 * a + c) * stack
                        side_s[k - 1, first : first + tail, :] = upper
                        side_s[k - 1, first + tail : first + stack, :] = lower

    with jax.named_scope("x_side"):
        for k in range(1, 1 + ns):
            for base, n, d, body, name in ((0, n1, d1, body1, "s1"), (size1, n2, d2, body2, "s2")):
                y = right(n[near_tile[k], body, :], table(name, 2 * (k - 1) + 0))
                y = y + right(d[near_tile[k], body, :], table(name, 2 * (k - 1) + 1))
                side_s[k - 1, base : base + y.shape[0], :] = y
        if early_half is None:
            send_edges(lambda d: d[0] == 0)
        else:
            pl.when(jnp.logical_not(first_plane))(lambda: send_edges(lambda d: d[0] == 0))

    with jax.named_scope("x_own"):
        for n, d, body, name, dst in ((n1, d1, body1, "c1", x1), (n2, d2, body2, "c2", x2)):
            for a, y in enumerate((n, d)):
                y = wide_of(y, body, own_range)
                y = filtered(y, name) if name == "c1" else right(y, table(name))
                for c in range(dst.shape[1]):
                    dst[a, c] = y[:, c * LANES : (c + 1) * LANES]

    if early_half is not None:

        @pl.when(first_plane)
        def _():
            meet()
            send_edges(lambda d: True)

    def ratio(n, d):
        return jnp.where(d > 0, n / d, 0.0)

    def await_edges(wanted):
        for i, d in enumerate(kinds):
            if wanted(d):
                given(sends(*d), lambda: edge(i).wait_send())
                given(comes(*d), lambda: edge(i).wait_recv())

    def q_rows(x, y, rows, gain):
        for c in range(x.shape[1]):
            y[rows, c * LANES : (c + 1) * LANES] = gain * ratio(x[0, c, rows, :], x[1, c, rows, :])

    gain1, gain2 = gain_ref[1] - gain_ref[0], gain_ref[2] - gain_ref[1]

    with jax.named_scope("w_side"):
        await_edges(lambda d: d[0] == 0)
    with jax.named_scope("add_side"):
        for k in range(1, 1 + ns):
            def add():
                for base, size, x, into in ((0, size1, x1, into1[k]), (size1, size2, x2, into2[k])):
                    more = unpack_lanes(side_r[k - 1, base : base + size, :])
                    for a in range(2):
                        x[a, into] = x[a, into] + more[a]
                for a in range(2):
                    for c in range(2):
                        base = base_g + (2 * a + c) * stack
                        g[a, c] = g[a, c] + side_r[k - 1, base : base + stack, :]

            given(recv_col[k], add)
    with jax.named_scope("q"):
        q_rows(x1, y1, slice(0, size1), gain1)
        q_rows(x2, y2, slice(0, size2), gain2)

    def grow_rows(src, dst, first, count):
        x, y, w = (src[first + k : first + k + count, :] for k in (1, 2, 3))
        dst[pl.ds(2 * first, count, stride=2), :] = 0.125 * (x + w) + 0.75 * y
        dst[pl.ds(2 * first + 1, count, stride=2), :] = 0.5 * (y + w)

    def block(x, c, p, first):
        ok = jnp.logical_or(line8 >= 4, up) if first else jnp.logical_or(line8 < 4, down)
        x[c, p : p + 8, :] = jnp.where(ok, x[c, p : p + 8, :], 0.0)

    tiles2 = range(x2.shape[1])

    def mask_ends():
        for c in tiles2:
            block(z1b, c, 0, True)
            block(z1b, c, nr // 2, False)

    gain0 = gain_ref[0]

    def rise(c, m, count):
        x, y, w = (wide[c, m + k : m + k + count, :] for k in (3, 4, 5))
        even, odd = pl.ds(2 * m, count, stride=2), pl.ds(2 * m + 1, count, stride=2)
        out0[c, even, :] = gain0 * q0[c, even, :] + (0.125 * (x + w) + 0.75 * y)
        out0[c, odd, :] = gain0 * q0[c, odd, :] + 0.5 * (y + w)

    def upward(parts):
        z = [jnp.concatenate([z1b[c, p, :] for p in parts], axis=0) for c in tiles2]
        z += [
            jnp.concatenate([y1[p, c * LANES : (c + 1) * LANES] for p in parts], axis=0)
            for c in range(x1.shape[1])
        ]
        first, second = (lax.broadcasted_iota(jnp.int32, z[0].shape, 1) < k for k in (8, 16))
        t2 = len(tiles2) - 1
        ends = jnp.where(first, z[-1], jnp.where(second, pltpu.roll(z[t2], 8, axis=1), 0.0))
        z = z[:t2] + z[t2 + 1 : -1] + [ends]
        return right(jnp.concatenate(z, axis=1), table("e0"))

    with jax.named_scope("factor"):
        shape = (stack, 256)
        at_row = level_of(shape, 0, tops[1:])
        at_col = level_of(shape, 1, lane_cuts)
        gains = [gain_ref[level] - gain_ref[level - 1] for level in (3, 4, 5)] + [-gain_ref[5]]
        value = jnp.where(
            at_row == 0, gains[0], jnp.where(at_row == 1, gains[1], jnp.where(at_row == 2, gains[2], gains[3]))
        )
        factor[...] = jnp.where(at_row == at_col, value, 0.0)

    with jax.named_scope("base"):
        await_tables("e0")
        for c in tiles2:
            z2b[c] = y2[:, c * LANES : (c + 1) * LANES]
            grow_rows(z2b.at[c], z1b.at[c], 0, nr // 4 + 8)
        mask_ends()
        base = upward((slice(0, size1),))
        for c in own_range:
            wide[c] = base[:, c * LANES : (c + 1) * LANES]
        for c in own_range:
            for m in range(0, nr // 2, 32):
                rise(c, m, 32)

    with jax.named_scope("w_edges"):
        await_edges(lambda d: d[0] != 0)
        await_tables("ec0", "r012", "er", "second")
    packed_lanes = jnp.logical_and(lane8 % (LANES // 2) >= MIDDLE[0], lane8 % (LANES // 2) <= MIDDLE[-1])
    with jax.named_scope("edges"):
        for rp, at1, at2, firsts in ((1, 0, 0, tops), (2, nr // 2, nr // 4, bottoms)):
            def moved_to(y, by, ok):
                return [jnp.where(ok, pltpu.roll(z, LANES - by, axis=1), 0.0) for z in y]

            got = edge_r.at[rp - 1, 0]
            tail = unpack(got[OWN_TILES - 1])
            adds1 = [unpack(got[0]), unpack(got[1]), [jnp.where(lane8 < 8, y, 0.0) for y in tail]]
            adds2 = [unpack(got[2]), moved_to(tail, 8, lane8 < 8)]
            deep = [unpack(got[3]), moved_to(tail, 16, lane8 < 32)]
            for cp in range(1, 1 + ns):
                y = edge_r[rp - 1, cp, 1]
                for a, more in enumerate(unpack(edge_r[rp - 1, cp, 0])):
                    deep[0][a] = deep[0][a] + more
                for a, more in enumerate(moved_to(unpack(y), 16, lane8 < 32)):
                    deep[1][a] = deep[1][a] + more
            for x, at, adds in ((x1, at1, adds1), (x2, at2, adds2)):
                for c, more in enumerate(adds):
                    for a in range(2):
                        x[a, c, at : at + 8, :] = x[a, c, at : at + 8, :] + more[a]
            for cp in range(1, 1 + ns):
                y = edge_r[rp - 1, cp, 1]
                for x, at, into, z in ((x1, at1, into1[cp], y), (x2, at2, into2[cp], pltpu.roll(y, LANES - 8, axis=1))):
                    for a, more in enumerate(unpack_lanes(jnp.where(packed_lanes, z, 0.0))):
                        x[a, into, at : at + 8, :] = x[a, into, at : at + 8, :] + more
            for c in range(2):
                for a in range(2):
                    for f in firsts:
                        g[a, c, f : f + 8, :] = g[a, c, f : f + 8, :] + deep[c][a]
        for x, y, at, gain in ((x1, y1, nr // 2, gain1), (x2, y2, nr // 4, gain2)):
            q_rows(x, y, slice(0, 8), gain)
            q_rows(x, y, slice(at, at + 8), gain)
    with jax.named_scope("fix"):
        for c in tiles2:
            for at in (0, nr // 4):
                z2b[c, at : at + 8, :] = y2[at : at + 8, c * LANES : (c + 1) * LANES]
                grow_rows(z2b.at[c], z1b.at[c], at, 8)
        mask_ends()
        parts = (slice(0, 16), slice(nr // 2, nr // 2 + 16))
        base = upward(parts)
        for c in own_range:
            for i, p in enumerate(parts):
                wide[c, p, :] = base[16 * i : 16 * i + 16, c * LANES : (c + 1) * LANES]
            rise(c, 0, 8)
            rise(c, nr // 2 - 8, 8)

    with jax.named_scope("deep"):
        n, d = (jnp.concatenate([g[a, 0], g[a, 1]], axis=1) for a in range(2))
        x = jnp.where(d > 0, factor[...] * (n / d), 0.0)
        high, low = split(x)
        er = [table("er", k) for k in (0, 1)]
        x = dot(er[0], high) + dot(er[0], low) + dot(er[1], high)
        high, low = split(x)
        x = dot(high, table("ec0")) + dot(low, table("ec0")) + dot(high, table("ec0", 1))

    with jax.named_scope("w_top"):
        everything = pltpu.make_async_copy(slots, slots, precv)
        everything.wait()
        pltpu.make_async_copy(slots, slots, psend).wait()
    with jax.named_scope("top"):
        total = part[...] + jnp.sum(slots[...], axis=0)
        top_sum = jnp.sum(jnp.where(lane1 < LANES // 2, total, 0.0), axis=1, keepdims=True)
        top_weight = jnp.sum(jnp.where(lane1 < LANES // 2, 0.0, total), axis=1, keepdims=True)
        top_line = (top_sum / top_weight) * table("line", 0, (1, 2))
        ones = table("second")
        x = x + jnp.concatenate(
            [ones * top_line[:, c * LANES : (c + 1) * LANES] for c in own_range], axis=1
        )
        high, low = split(x)
        us_ref[...] = jnp.concatenate([high, high, low], axis=0)


def last(base_ref, us_ref, rows_ref, out_ref, buf, sem):
    nr, nc = buf.shape
    step = nr // sem.shape[0]
    writes = []
    for k in range(sem.shape[0]):
        here = slice(k * step, (k + 1) * step)
        y = dot(rows_ref[here, :], us_ref[...])
        for c in range(base_ref.shape[0]):
            cols = slice(c * LANES, (c + 1) * LANES)
            buf[here, cols] = base_ref[c, here, :] + y[:, cols]
        writes.append(pltpu.make_async_copy(buf.at[here, :], out_ref.at[here, :], sem.at[k]))
        writes[-1].start()
    for write in writes:
        write.wait()


def local(mesh_shape, heights, scene_ids, scene_offset, scene_weight, band_gain):
    nx, ny, nz = mesh_shape
    nr, nc = heights.shape
    ns = 1 if nx == 2 else 2
    made = tables(nr, nc, nx, ny * nz)
    given, places = merge(made)
    sizes = (nr, nc, nx, ny, nz, ns)
    ext = (nr + 2 * HALO, nc)
    tiles = nc // LANES
    own_tiles = tiles
    m3 = nr // 8 + 8
    size1, size2, stack = nr // 2 + 16, nr // 4 + 16, nr // 8 + nr // 16 + nr // 32 + nr // 64 + 40
    tiles1, tiles2 = nc // 2 // LANES + 1, nc // 4 // LANES + 1
    beside = size1 + size2 + 4 * stack
    peers = nx * ny * nz - 1
    messages = 3 * (1 + ns) - 1
    hbm = pl.BlockSpec(memory_space=pltpu.HBM)
    deep_rows = made["r012"].shape[-1]
    vmem = pl.BlockSpec(memory_space=pltpu.VMEM)
    kept = pl.pallas_call(
        functools.partial(kernel, sizes, places),
        out_shape=(
            pltpu.VMEM((own_tiles, nr, LANES), F32),
            pltpu.VMEM((deep_rows, nc), BF16),
            pltpu.VMEM((nr, deep_rows), BF16),
        ),
        in_specs=[hbm] * (5 + len(given)),
        out_specs=(vmem, vmem, vmem),
        scratch_shapes=[pltpu.VMEM(x.shape[1:], x.dtype) for x in given[:-1]]
        + [
            pltpu.SMEM(scene_offset.shape, F32),
            pltpu.SMEM(scene_weight.shape, F32),
            pltpu.SMEM(band_gain.shape, F32),
            pltpu.VMEM(ext, F32),
            pltpu.VMEM(ext, jnp.int32),
            pltpu.VMEM((own_tiles, nr, LANES), F32),
        ]
        + [pltpu.VMEM((tiles, nr + 3 * HALO, LANES), F32)] * 2
        + [pltpu.VMEM((tiles, nr // 2 + 32, LANES), F32)] * 2
        + [pltpu.VMEM((tiles, nr // 4 + 24, LANES), F32)] * 2
        + [pltpu.VMEM((own_tiles, m3, LANES), F32)] * 2
        + [
            pltpu.VMEM((2, tiles1, size1, LANES), F32),
            pltpu.VMEM((2, tiles2, size2, LANES), F32),
            pltpu.VMEM((2, 2, stack, LANES), F32),
            pltpu.VMEM((stack, 256), F32),
            pltpu.VMEM((size1, tiles1 * LANES), F32),
            pltpu.VMEM((size2, tiles2 * LANES), F32),
            pltpu.VMEM((ns, beside, LANES), F32),
            pltpu.VMEM((ns, beside, LANES), F32),
            pltpu.VMEM((2, 1 + ns, OWN_TILES, 8, LANES), F32),
            pltpu.VMEM((2, 1 + ns, OWN_TILES, 8, LANES), F32),
            pltpu.VMEM((tiles2, nr // 4 + 16, LANES), F32),
            pltpu.VMEM((tiles2, nr // 2 + 16, LANES), F32),
            pltpu.VMEM((own_tiles, nr // 2 + 16, LANES), F32),
            pltpu.VMEM((1, LANES), F32),
            pltpu.VMEM((peers, 1, LANES), F32),
            pltpu.SemaphoreType.DMA((CHUNKS + 3,)),
            pltpu.SemaphoreType.DMA((len(given),)),
            pltpu.SemaphoreType.DMA((messages,)),
            pltpu.SemaphoreType.DMA((messages,)),
            pltpu.SemaphoreType.DMA(()),
            pltpu.SemaphoreType.DMA(()),
        ],
        compiler_params=pltpu.CompilerParams(collective_id=0, has_side_effects=True),
    )(scene_offset, scene_weight, band_gain, heights, scene_ids, *given)
    return pl.pallas_call(
        last,
        out_shape=jax.ShapeDtypeStruct((nr, nc), F32),
        in_specs=[vmem] * 3,
        out_specs=pl.BlockSpec(memory_space=pltpu.HBM),
        scratch_shapes=[pltpu.VMEM((nr, nc), F32), pltpu.SemaphoreType.DMA((PIECES,))],
        compiler_params=pltpu.CompilerParams(vmem_limit_bytes=16 * 1024 * 1024),
    )(*kept)


def solution(mesh):
    placed = (P(("gy", "gz"), "gx"), P(("gy", "gz"), "gx"), P(), P(), P())
    shape = tuple(mesh.shape[name] for name in ("gx", "gy", "gz"))
    return jax.shard_map(
        functools.partial(local, shape), mesh=mesh, in_specs=placed,
        out_specs=P(("gy", "gz"), "gx"), check_vma=False,
    )
```
